512 devices in a mesh: tile: 64 (over x, z_lo, core), loop: 8 (over y, z_hi).
Axes of the slice: x: 4, y: 4, z: 16 (z_hi: 2, z_lo: 8; z = z_hi * 8 + z_lo), core: 2. Of those that a mesh axis runs over, the one named last changes fastest.
Arguments:
- star_slot: int32 [64, 128, 128], P('tile', 'loop'), may hold values from 0 to 255
- star_block: int32 [64, 128], P('tile', 'loop'), may hold values from 0 to 1, as said below
- exposure: int32 [64, 128, 128], P('tile', 'loop'), may hold values from 0 to 511
- superpixel: int32 [64, 128, 128], P('tile', 'loop'), may hold values from 0 to 2047
- magnitude: float32 [64, 128, 128], P('tile', 'loop'), may hold values from -7 to 7
- weight: float32 [64, 128, 128], P('tile', 'loop'), may hold values from 0.25 to 4
Outputs:
- star_mags: float32 [262144], P(('tile', 'loop'))
- zero_points: float32 [4096], P('loop')
- flat_field: float32 [512, 256], P('tile')
The draws below stay inside these ranges and needn't reach their ends.
Inputs may be any that keep to these rules, and one draw needn't show every extreme that they name: `star_block`: observation blocks of one device at positions 2 * o to 2 * o + 1 of its 16 blocks observe stars of the star shard held by loop index o of the same tile.
All inputs are finite; a program needn't handle non-finite values.
Results may differ from the reference program's by a relative error of at most 0.00022.
Values sent between devices are 32-bit elements; how exact they have to be, the bound alone decides.
No kernel may reach another device: no remote copies, remote signals or barrier semaphores. Data moves between devices by JAX's collectives and lax.ppermute only.
A program may use at most 64 MiB of HBM per device.

```python
import math
import jax
import jax.numpy as jnp
from jax import lax

FC = 256
ROWS_DEV = 8
BLK_DEV = 16
SBLK_DEV = 2
EXP_DEV = 512
STAR_BLK = 256
OBS_BLK = 128
ITERS = 2
TILES = 64
GROUPS = 8
BLK_OWN = 2
STAR_DEV = 512
STARS = 262144
EXPOSURES = 4096
FLAT_ROWS = 512
OBS_ROWS = 128


def observation_tables(key):
    tile_count = FLAT_ROWS // ROWS_DEV
    group_count = EXPOSURES // EXP_DEV
    row_count = BLK_DEV * group_count
    keys = jax.random.split(jax.random.fold_in(key, 101), 4)
    slots = jax.random.randint(keys[0], (tile_count, row_count, OBS_BLK), 0, STAR_BLK, dtype=jnp.int32)
    blocks = jax.random.randint(keys[1], (tile_count, row_count), 0, SBLK_DEV, dtype=jnp.int32)
    exposures = jax.random.randint(keys[2], (tile_count, row_count, OBS_BLK), 0, EXP_DEV, dtype=jnp.int32)
    pixels = jax.random.randint(keys[3], (tile_count, row_count, OBS_BLK), 0, ROWS_DEV * FC, dtype=jnp.int32)
    return (slots, blocks, exposures, pixels)


def draw_star_slot(key, part):
    return observation_tables(key)[0]


def draw_star_block(key, part):
    return observation_tables(key)[1]


def draw_exposure(key, part):
    return observation_tables(key)[2]


def draw_superpixel(key, part):
    return observation_tables(key)[3]


def draw_magnitude(key, part):
    slots, blocks, exposures, pixels = observation_tables(key)
    group_count = EXPOSURES // EXP_DEV
    tile_ids = lax.broadcasted_iota(jnp.int32, slots.shape, 0)
    row_ids = lax.broadcasted_iota(jnp.int32, slots.shape, 1)
    group_ids = row_ids // BLK_DEV
    owner_ids = row_ids % BLK_DEV // (BLK_DEV // group_count)
    star_ids = (tile_ids * group_count + owner_ids) * STAR_DEV + blocks[:, :, None] * STAR_BLK + slots
    expo_ids = group_ids * EXP_DEV + exposures
    pixel_ids = tile_ids * (ROWS_DEV * FC) + pixels
    keys = jax.random.split(jax.random.fold_in(key, 202), 4)
    star_true = jnp.clip(jax.random.normal(keys[0], (STARS,), jnp.float32), -4.0, 4.0)
    expo_true = jnp.clip(0.4 * jax.random.normal(keys[1], (EXPOSURES,), jnp.float32), -1.6, 1.6)
    flat_true = jnp.clip(0.25 * jax.random.normal(keys[2], (FLAT_ROWS * FC,), jnp.float32), -1.0, 1.0)
    noise = jnp.clip(0.1 * jax.random.normal(keys[3], slots.shape, jnp.float32), -0.4, 0.4)
    values = star_true[star_ids] + expo_true[expo_ids] + flat_true[pixel_ids] + noise
    return values.astype(jnp.float32)


def steps_of(stream_key, dims, pieces, smallest, largest):
    gain = 1.0
    for axis_at, parts in pieces:
        draws = jax.random.uniform(jax.random.fold_in(jax.random.fold_in(stream_key, 6), axis_at), (parts,), jnp.float32, smallest / len(pieces), largest / len(pieces))
        gain = gain * jnp.repeat(jnp.exp(draws), dims[axis_at] // parts).reshape((-1,) + (1,) * (len(dims) - 1 - axis_at))
    return gain


def setup_inputs(seed: int = 0) -> dict:
    seeds = jax.random.split(jax.random.key(seed), 7)
    return {
        "star_slot": draw_star_slot(jax.random.fold_in(seeds[6], 71), 0),
        "star_block": draw_star_block(jax.random.fold_in(seeds[6], 71), 0),
        "exposure": draw_exposure(jax.random.fold_in(seeds[6], 71), 0),
        "superpixel": draw_superpixel(jax.random.fold_in(seeds[6], 71), 0),
        "magnitude": draw_magnitude(jax.random.fold_in(seeds[6], 71), 0),
        "weight": jnp.clip(jnp.exp(math.log(4.0) - 2.7725887 * jax.random.uniform(seeds[5], (TILES, OBS_ROWS, OBS_BLK), jnp.float32) ** steps_of(seeds[5], (TILES, OBS_ROWS, OBS_BLK), ((0, 64), (1, 8)), -0.2, 0.2)), 0.25, 4.0),
    }


SMOOTH = 2.0
RIDGE = 0.5


def observation_indices(star_slot, star_block, exposure, superpixel):
    tile_ids = lax.broadcasted_iota(jnp.int32, star_slot.shape, 0)
    row_ids = lax.broadcasted_iota(jnp.int32, star_slot.shape, 1)
    group_ids = row_ids // BLK_DEV
    owner_ids = (row_ids % BLK_DEV) // BLK_OWN
    star_ids = (tile_ids * GROUPS + owner_ids) * STAR_DEV + star_block[:, :, None] * STAR_BLK + star_slot
    expo_ids = group_ids * EXP_DEV + exposure
    pixel_ids = tile_ids * (ROWS_DEV * FC) + superpixel
    return star_ids.reshape(-1), expo_ids.reshape(-1), pixel_ids.reshape(-1)


def laplace(flat):
    padded = jnp.pad(flat, 1)
    beside = padded[2:, 1:-1] + padded[:-2, 1:-1] + padded[1:-1, 2:] + padded[1:-1, :-2]
    return SMOOTH * (4.0 * flat - beside)


def combine(vector, other, factor):
    return jax.tree.map(lambda values, others: values + factor * others, vector, other)


def reference(star_slot, star_block, exposure, superpixel, magnitude, weight):
    star_ids, expo_ids, pixel_ids = observation_indices(star_slot, star_block, exposure, superpixel)
    weights = weight.reshape(-1)
    magnitudes = magnitude.reshape(-1)
    pixels = FLAT_ROWS * FC

    def adjoint(values):
        return (jax.ops.segment_sum(values, star_ids, num_segments=STARS),
                jax.ops.segment_sum(values, expo_ids, num_segments=EXPOSURES),
                jax.ops.segment_sum(values, pixel_ids, num_segments=pixels).reshape(FLAT_ROWS, FC))

    right_side = adjoint(weights * magnitudes)
    counts = adjoint(weights)
    diagonal = (counts[0] + RIDGE, counts[1] + RIDGE, counts[2] + (4.0 * SMOOTH + RIDGE))

    def operate(vector):
        fitted = vector[0][star_ids] + vector[1][expo_ids] + vector[2].reshape(-1)[pixel_ids]
        sums = adjoint(weights * fitted)
        return (sums[0] + RIDGE * vector[0], sums[1] + RIDGE * vector[1],
                sums[2] + laplace(vector[2]) + RIDGE * vector[2])

    def inner(first_vec, second_vec):
        return (jnp.sum(first_vec[0] * second_vec[0]) + jnp.sum(first_vec[1] * second_vec[1])
                + jnp.sum(first_vec[2] * second_vec[2]))

    def divide(vector):
        return jax.tree.map(lambda values, scales: values / scales, vector, diagonal)

    solution = jax.tree.map(jnp.zeros_like, right_side)
    residual = right_side
    precon = divide(residual)
    norm_now = inner(residual, precon)
    direction = precon
    for iteration in range(ITERS):
        image = operate(direction)
        step_size = norm_now / inner(direction, image)
        solution = combine(solution, direction, step_size)
        residual = combine(residual, image, -step_size)
        if iteration + 1 < ITERS:
            precon = divide(residual)
            norm_next = inner(residual, precon)
            direction = combine(precon, direction, norm_next / norm_now)
            norm_now = norm_next
    return (solution[0], solution[1], solution[2])
```

```python
import jax
import jax.numpy as jnp
from jax import lax
from jax.experimental import pallas as pl
from jax.experimental.pallas import tpu as pltpu
from jax.sharding import Mesh
from jax.sharding import PartitionSpec as P

SMOOTH = 2.0
RIDGE = 0.5
LO = 128
NX, NZ, NC, NY, NH = 4, 8, 2, 4, 2
ALL = ("x", "zl", "c", "y", "zh")
F32 = jnp.float32
I32 = jnp.int32
BF16 = jnp.bfloat16
NT = (((1,), (1,)), ((), ()))
NN = (((1,), (0,)), ((), ()))


def split3(v):
    first = v.astype(BF16).astype(F32)
    rest = v - first
    second = rest.astype(BF16).astype(F32)
    return first, second, rest - second


def pad16(rows):
    count = sum(row.shape[0] for row in rows)
    if count % 16:
        rows = rows + [jnp.zeros((16 - count % 16, rows[0].shape[1]), F32)]
    return jnp.concatenate(rows, axis=0).astype(BF16)


def onehot(lo):
    n = lo.shape[1]
    return jnp.where(lax.broadcasted_iota(I32, (LO, n), 0) == lo, 1.0, 0.0).astype(BF16)


def scatter(values, hi, high, hot):
    mask = lax.broadcasted_iota(I32, (high, hi.shape[1]), 0) == hi
    rows = [jnp.where(mask, part, 0.0) for v in values for part in split3(v)]
    sums = lax.dot_general(pad16(rows), hot, NT, preferred_element_type=F32)
    return [
        sums[3 * high * i : 3 * high * i + high]
        + sums[3 * high * i + high : 3 * high * i + 2 * high]
        + sums[3 * high * i + 2 * high : 3 * high * (i + 1)]
        for i in range(len(values))
    ]


def gather(table, hi, hot):
    high = table.shape[0]
    parts = lax.dot_general(pad16(list(split3(table))), hot, NN, preferred_element_type=F32)
    found = parts[:high] + parts[high : 2 * high] + parts[2 * high : 3 * high]
    mask = lax.broadcasted_iota(I32, found.shape, 0) == hi
    return jnp.sum(jnp.where(mask, found, 0.0), axis=0, keepdims=True)


def row_iota(shape):
    return lax.broadcasted_iota(I32, shape, 0)


def pack_kernel(block_ref, slot_ref, expo_ref, pix_ref, mag_ref, w_ref, out_ref):
    rows = row_iota((8, LO))
    for r in range(16):
        star = slot_ref[r : r + 1, :] + (block_ref[0, r] * 256 + ((r // 2) % 2) * 512)
        pix = pix_ref[r : r + 1, :]
        pix = (((pix >> 7) & 1) * 8 + (pix >> 8)) * LO + (pix & 127)
        w = w_ref[r : r + 1, :]
        fields = (
            star.astype(F32),
            pix.astype(F32),
            expo_ref[r : r + 1, :].astype(F32),
            w,
            w * mag_ref[r : r + 1, :],
        )
        tile = jnp.zeros((8, LO), F32)
        for f, field in enumerate(fields):
            tile = jnp.where(rows == f, field, tile)
        out_ref[r // 4, :, (r % 4) * LO : (r % 4 + 1) * LO] = tile


def expo_kernel(obs_ref, out_ref):
    x = jnp.concatenate([obs_ref[k] for k in range(4)], axis=1)
    e = x[2:3].astype(I32)
    weighted, count = scatter([x[4:5], x[3:4]], e >> 7, 8, onehot(e & 127))
    both = jnp.where(row_iota((8, LO)) < 4, weighted, pltpu.roll(count, 4, 0))
    for peer in range(16):
        out_ref[peer] = both


def fields_of(obs_ref, k):
    x = jnp.concatenate([obs_ref[g, k] for g in range(8)], axis=1)
    ids = x.astype(I32)
    return ids[0:1], ids[1:2], ids[2:3], x[3:4], x[4:5]


def own_fields(obs_ref, y, k):
    x = jnp.concatenate([obs_ref[2 * y + rel, k] for rel in range(2)], axis=1)
    ids = x.astype(I32)
    return ids[0:1], ids[1:2], ids[2:3], x[3:4]


def tile_kernel(
    pos_ref, obs_ref, g0s_ref, ds_ref, cs_ref, g0f_ref, df_ref, cf_ref, ru_ref, top_ref, bot_ref,
    hot_s, hot_p, fit_ref,
):
    g0f_ref[...] = jnp.zeros((16, LO), F32)
    df_ref[...] = jnp.zeros((16, LO), F32)

    def sums(k, carry):
        s, p, e, w, wm = fields_of(obs_ref, k)
        hs = onehot(s & 127)
        hp = onehot(p & 127)
        hot_s[k] = hs
        hot_p[k] = hp
        weighted, count = scatter([wm, w], s >> 7, 8, hs)
        diag = count + RIDGE
        g0s_ref[k] = weighted / diag
        ds_ref[k] = diag
        weighted, count = scatter([wm, w], p >> 7, 16, hp)
        g0f_ref[...] += weighted
        df_ref[...] += count
        return carry

    lax.fori_loop(0, 4, sums, 0)
    diag = df_ref[...] + (4.0 * SMOOTH + RIDGE)
    g0f = g0f_ref[...] / diag
    df_ref[...] = diag
    g0f_ref[...] = g0f
    top_ref[...] = jnp.concatenate([g0f[0:1], g0f[8:9]], axis=0)
    bot_ref[...] = jnp.concatenate([g0f[7:8], g0f[15:16]], axis=0)
    cf_ref[...] = jnp.zeros((16, LO), F32)

    def couple(k, carry):
        s, p, e, w, wm = fields_of(obs_ref, k)
        hs = hot_s[k]
        hp = hot_p[k]
        from_star = gather(g0s_ref[k], s >> 7, hs)
        from_flat = gather(g0f_ref[...], p >> 7, hp)
        (cs_ref[k],) = scatter([w * from_flat], s >> 7, 8, hs)
        (added,) = scatter([w * from_star], p >> 7, 16, hp)
        cf_ref[...] += added
        fit_ref[k] = w * (from_star + from_flat)
        return carry

    lax.fori_loop(0, 4, couple, 0)
    y = pos_ref[0]
    total = jnp.zeros((8, LO), F32)
    for k in range(4):
        s, p, e, w = own_fields(obs_ref, y, k)
        hi = (e >> 7) + (lax.broadcasted_iota(I32, e.shape, 1) >> 9) * 4
        fit = fit_ref[k, :, pl.ds(pl.multiple_of(y * 1024, 1024), 1024)]
        (added,) = scatter([fit], hi, 8, onehot(e & 127))
        total += added
    ru_ref[...] = total


def pair_rows(first, second):
    low = row_iota((8, LO)) < 4
    return jnp.where(low, first, pltpu.roll(second, 4, 0)), jnp.where(
        low, pltpu.roll(first, 4, 0), second
    )


def beside(flat, above, below):
    left, right = flat[:8], flat[8:]
    rows = row_iota((8, LO))
    lanes = lax.broadcasted_iota(I32, (8, LO), 1)
    out = []
    left_up, right_up = pltpu.roll(left, 1, 1), pltpu.roll(right, 1, 1)
    left_down, right_down = pltpu.roll(left, 127, 1), pltpu.roll(right, 127, 1)
    sides = (
        jnp.where(lanes == 0, 0.0, left_up) + jnp.where(lanes == 127, right_down, left_down),
        jnp.where(lanes == 0, left_up, right_up) + jnp.where(lanes == 127, 0.0, right_down),
    )
    for i, half in enumerate((left, right)):
        upper = jnp.where(rows == 0, above[i : i + 1], pltpu.roll(half, 1, 0))
        lower = jnp.where(rows == 7, below[i : i + 1], pltpu.roll(half, 7, 0))
        out.append(sides[i] + upper + lower)
    return jnp.concatenate(out, axis=0)


def expo_apply_kernel(
    obs_ref, expo_ref, g0f_ref, cs_ref, cf_ref, ds_ref, df_ref, above_ref, below_ref,
    cs_out, ys_out, cf_out, yf_out, g0z_out, dz_out, top_out,
):
    for y in range(4):
        part = expo_ref[y]
        for xc in range(1, 8):
            part = part + expo_ref[xc * 4 + y]
        weighted, count = pair_rows(part[:8], part[8:])
        diag = count + RIDGE
        g0z_out[y] = weighted / diag
        dz_out[y] = diag
    table = jnp.concatenate([g0z_out[y] for y in range(4)], axis=0)
    cf_out[...] = cf_ref[...]

    def apply(k, carry):
        s, p, e, w, wm = fields_of(obs_ref, k)
        hi = (e >> 7) + (lax.broadcasted_iota(I32, e.shape, 1) >> 9) * 4
        fit = w * gather(table, hi, onehot(e & 127))
        (added,) = scatter([fit], s >> 7, 8, onehot(s & 127))
        total = cs_ref[k] + added
        cs_out[k] = total
        ys_out[k] = total / ds_ref[k]
        (added,) = scatter([fit], p >> 7, 16, onehot(p & 127))
        cf_out[...] += added
        return carry

    lax.fori_loop(0, 4, apply, 0)
    cf = cf_out[...] - SMOOTH * beside(g0f_ref[...], above_ref[...], below_ref[...])
    cf_out[...] = cf
    yf = cf / df_ref[...]
    yf_out[...] = yf
    top_out[...] = jnp.concatenate([yf[0:1], yf[8:9]], axis=0)


def fold8(a):
    total = a[0:8]
    for i in range(8, a.shape[0], 8):
        total = total + a[i : i + 8]
    return jnp.sum(total, axis=0, keepdims=True)


def fold_lanes(a):
    total = a[:, 0:LO]
    for i in range(LO, a.shape[1], LO):
        total = total + a[:, i : i + LO]
    return total


def last_kernel(
    pos_ref, obs_ref, g0s_ref, ds_ref, cs_ref, ys_ref, g0f_ref, df_ref, cf_ref, yf_ref, ru_ref, out_ref
):
    y = pos_ref[0]
    total = jnp.zeros((8, LO), F32)
    cross = jnp.zeros((1, LO), F32)
    yf = yf_ref[...]
    for k in range(4):
        s, p, e, w = own_fields(obs_ref, y, k)
        hi = (e >> 7) + (lax.broadcasted_iota(I32, e.shape, 1) >> 9) * 4
        from_star = gather(ys_ref[k], s >> 7, onehot(s & 127))
        from_flat = gather(yf, p >> 7, onehot(p & 127))
        (added,) = scatter([w * (from_star + from_flat)], hi, 8, onehot(e & 127))
        total += added
        cross += fold_lanes(w * from_star * from_flat)
    out_ref[0:8] = jnp.where(row_iota((8, LO)) < 4, ru_ref[...], pltpu.roll(total, 4, 0))
    out_ref[8:16] = jnp.where(row_iota((8, LO)) < 4, pltpu.roll(ru_ref[...], 4, 0), total)
    g0s = jnp.concatenate([g0s_ref[k] for k in range(4)], axis=0)
    ds = jnp.concatenate([ds_ref[k] for k in range(4)], axis=0)
    cs = jnp.concatenate([cs_ref[k] for k in range(4)], axis=0)
    ys = jnp.concatenate([ys_ref[k] for k in range(4)], axis=0)
    g0f, df, cf = g0f_ref[...], df_ref[...], cf_ref[...]
    none = jnp.zeros((2, LO), F32)
    rho = 0.25 * (fold8(g0s * g0s * ds) + fold8(g0f * g0f * df))
    beta = 0.25 * (fold8(g0s * cs) + fold8(g0f * cf))
    eta = 0.25 * (fold8(cs * ys) + fold8(cf * yf))
    delta = 2.0 * cross - (0.25 * SMOOTH) * fold8(yf * beside(yf, none, none))
    out_ref[16:24] = jnp.concatenate([rho, beta, eta, delta, jnp.zeros((4, LO), F32)], axis=0)


def whole(a):
    return jnp.sum(jnp.sum(a, axis=0, keepdims=True), axis=1, keepdims=True)


def finish_kernel(
    pos_ref, sums_ref, g0z_ref, dz_ref, g0s_ref, ys_ref, g0f_ref, yf_ref, star_out, zero_out, flat_out
):
    y, zh = pos_ref[0], pos_ref[1]
    scal = sums_ref[0, 16:24]
    for peer in range(1, 32):
        scal = scal + sums_ref[peer, 16:24]
    z_rho = jnp.zeros((8, LO), F32)
    z_beta, z_eta, z_delta = z_rho, z_rho, z_rho
    z_own = z_rho
    for i in range(4):
        part = sums_ref[i, 0:16]
        for xc in range(1, 8):
            part = part + sums_ref[xc * 4 + i, 0:16]
        cz, qz = pair_rows(part[:8], part[8:])
        g0z, dz = g0z_ref[i], dz_ref[i]
        yz = cz / dz
        z_rho += g0z * g0z * dz
        z_beta += g0z * cz
        z_eta += cz * yz
        z_delta += qz * yz
        z_own = jnp.where(i == y, yz, z_own)
    rho0 = whole(z_rho) + whole(scal[0:1])
    beta = whole(z_beta) + whole(scal[1:2])
    eta = whole(z_eta) + whole(scal[2:3])
    delta = 2.0 * whole(z_delta) + whole(scal[3:4])
    curv0 = rho0 + beta
    step0 = rho0 / curv0
    left = beta / curv0
    rho1 = left * left * rho0 - 2.0 * step0 * left * beta + step0 * step0 * eta
    curv_g = (
        left * left * curv0
        - 2.0 * step0 * left * (beta + eta)
        + step0 * step0 * (eta + delta)
    )
    ratio = rho1 / rho0
    mixed = left * curv0 - step0 * (beta + eta)
    curv1 = curv_g + 2.0 * ratio * mixed + ratio * ratio * curv0
    step1 = rho1 / curv1
    along_g = step0 + step1 * (left + ratio)
    along_y = -step1 * step0
    star = along_g * g0s_ref[y] + along_y * ys_ref[y]
    star_out[...] = jnp.where(zh == 0, star, pltpu.roll(star, 4, 0))[0:4]
    zero_out[...] = (along_g * g0z_ref[y] + along_y * z_own)[0:4]
    flat = along_g * g0f_ref[...] + along_y * yf_ref[...]
    flat_out[:, 0:LO] = flat[:8]
    flat_out[:, LO : 2 * LO] = flat[8:]


VMEM = pl.BlockSpec(memory_space=pltpu.VMEM)
SMEM = pl.BlockSpec(memory_space=pltpu.SMEM)


def call(kernel, name, shapes, args, smem=0, scratch=(), flops=0):
    out = [jax.ShapeDtypeStruct(shape, F32) for shape in shapes]
    many = len(out) > 1
    return pl.pallas_call(
        kernel,
        name=name,
        out_shape=tuple(out) if many else out[0],
        in_specs=[SMEM] * smem + [VMEM] * (len(args) - smem),
        out_specs=tuple([VMEM] * len(out)) if many else VMEM,
        scratch_shapes=list(scratch),
        cost_estimate=pl.CostEstimate(flops=flops, bytes_accessed=1 << 20, transcendentals=0),
    )(*args)


def exchange(blocks, axes):
    return lax.all_to_all(blocks, axes, 0, 0, tiled=True)


def flat_pairs():
    def place(tile, y, zh):
        x, rest = divmod(tile, NZ * NC)
        zl, c = divmod(rest, NC)
        return (((x * NZ + zl) * NC + c) * NY + y) * NH + zh

    up = []
    for tile in range(NX * NZ * NC - 1):
        far = (tile + 1) % (NZ * NC) == 0
        for y in range(NY):
            for zh in range(NH):
                up.append((place(tile, y, zh), place(tile + 1, y, 1 - zh if far else zh)))
    return up, [(j, i) for i, j in up]


def on_device(star_slot, star_block, exposure, superpixel, magnitude, weight):
    y = lax.axis_index("y")
    zh = lax.axis_index("zh")
    pos = jnp.stack([y, zh]).astype(I32)
    up, down = flat_pairs()
    obs = call(
        pack_kernel, "pack", [(4, 8, 512)],
        (star_block, star_slot[0], exposure[0], superpixel[0], magnitude[0], weight[0]), smem=1,
    )
    partner = lax.ppermute(obs, "zh", [(0, 1), (1, 0)])
    expo = exchange(call(expo_kernel, "expo", [(16, 8, LO)], (obs,)), ("zl", "zh"))
    expo = expo.reshape(NZ, NH, 8, LO).sum(axis=0)
    expo = jnp.where(zh == 0, expo, expo[::-1]).reshape(16, LO)
    both = jnp.stack([obs, partner])
    tile_obs = exchange(jnp.broadcast_to(both[None], (NY, *both.shape)), "y")
    tile_obs = tile_obs.reshape(8, 4, 8, 512)
    expo, tile_obs = lax.optimization_barrier((expo, tile_obs))
    expo = exchange(jnp.broadcast_to(expo[None], (32, 16, LO)), ("x", "c", "y"))
    g0s, ds, cs, g0f, df, cf, ru, top, bot = call(
        tile_kernel, "tile",
        [(4, 8, LO)] * 3 + [(16, LO)] * 3 + [(8, LO)] + [(2, LO)] * 2,
        (pos, tile_obs), smem=1,
        scratch=[pltpu.VMEM((4, LO, 4096), BF16)] * 2 + [pltpu.VMEM((4, 1, 4096), F32)],
        flops=1 << 30,
    )
    above = lax.ppermute(bot, ALL, up)
    below = lax.ppermute(top, ALL, down)
    cs, ys, cf, yf, g0z, dz, first = call(
        expo_apply_kernel, "apply",
        [(4, 8, LO)] * 2 + [(16, LO)] * 2 + [(4, 8, LO)] * 2 + [(2, LO)],
        (tile_obs, expo, g0f, cs, cf, ds, df, above, below),
        flops=1 << 30,
    )
    next_first = lax.ppermute(first, ALL, down)
    payload = call(
        last_kernel, "last", [(24, LO)],
        (pos, tile_obs, g0s, ds, cs, ys, g0f, df, cf, yf, ru), smem=1,
        flops=1 << 28,
    )
    edge = -(0.5 * SMOOTH) * (yf[7] * next_first[0] + yf[15] * next_first[1])
    payload = payload + jnp.where(
        lax.broadcasted_iota(I32, (24, LO), 0) == 19, edge[None], 0.0
    )
    sums = exchange(jnp.broadcast_to(payload[None], (NZ, 24, LO)), "zl").sum(axis=0)
    sums = exchange(jnp.broadcast_to(sums[None], (32, 24, LO)), ("x", "c", "y"))
    star, zero, flat = call(
        finish_kernel, "finish", [(4, LO), (4, LO), (8, 2 * LO)],
        (pos, sums, g0z, dz, g0s, ys, g0f, yf), smem=1,
    )
    return star.reshape(-1), zero.reshape(-1), flat


def solution(mesh):
    split = Mesh(mesh.devices.reshape(NX, NZ, NC, NY, NH), ALL)
    tile, loop = ("x", "zl", "c"), ("y", "zh")
    placed = (
        P(tile, loop, None),
        P(tile, loop),
        P(tile, loop, None),
        P(tile, loop, None),
        P(tile, loop, None),
        P(tile, loop, None),
    )
    return jax.shard_map(
        on_device,
        mesh=split,
        in_specs=placed,
        out_specs=(P(ALL), P(loop), P(tile, None)),
        check_vma=False,
    )
```

```python
import jax
import jax.numpy as jnp
from jax import lax
from jax.experimental import pallas as pl
from jax.experimental.pallas import tpu as pltpu
from jax.sharding import Mesh
from jax.sharding import PartitionSpec as P

SMOOTH = 2.0
RIDGE = 0.5
LO = 128
NX, NZ, NC, NY, NH = 4, 8, 2, 4, 2
ALL = ("x", "zl", "c", "y", "zh")
F32 = jnp.float32
I32 = jnp.int32
BF16 = jnp.bfloat16
NT = (((1,), (1,)), ((), ()))
NN = (((1,), (0,)), ((), ()))


def split3(v):
    first = v.astype(BF16)
    rest = v - first.astype(F32)
    second = rest.astype(BF16)
    return first, second, (rest - second.astype(F32)).astype(BF16)


def bf_iota(shape, wrap=None):
    rows = lax.broadcasted_iota(I32, shape, 0)
    if wrap:
        rows = rows & (wrap - 1)
    return rows.astype(F32).astype(BF16)


def onehot(lo):
    rows = bf_iota((LO, LO))
    one, zero = jnp.ones((), BF16), jnp.zeros((), BF16)
    tiles = [
        jnp.where(rows == jnp.broadcast_to(lo[:, i : i + LO], (LO, LO)), one, zero)
        for i in range(0, lo.shape[1], LO)
    ]
    return jnp.concatenate(tiles, axis=1)


def spread(parts, hi, high):
    n = hi.shape[1]
    shape = (16, n)
    zero = jnp.zeros((), BF16)
    mask = bf_iota((16, LO), high)
    mask = jnp.concatenate(
        [mask == jnp.broadcast_to(hi[:, i : i + LO], (16, LO)) for i in range(0, n, LO)], axis=1
    )
    if high == 16:
        return [jnp.where(mask, jnp.broadcast_to(part, shape), zero) for part in parts]
    if len(parts) % 2:
        parts = list(parts) + [jnp.zeros_like(parts[0])]
    low = lax.broadcasted_iota(I32, (16, n), 0) < 8
    return [
        jnp.where(
            mask,
            jnp.where(low, jnp.broadcast_to(a.astype(F32), shape), jnp.broadcast_to(b.astype(F32), shape)).astype(BF16),
            zero,
        )
        for a, b in zip(parts[::2], parts[1::2])
    ]


def scatter(values, hi, high, hot):
    parts = [part for value in values for part in value]
    rows = jnp.concatenate(spread(parts, hi, high), axis=0)
    sums = lax.dot_general(rows, hot, NT, preferred_element_type=F32)
    out = []
    for i in range(len(values)):
        at = 3 * high * i
        out.append(
            sums[at : at + high] + sums[at + high : at + 2 * high] + sums[at + 2 * high : at + 3 * high]
        )
    return out


def gather(table, hi, hot):
    high = table.shape[0]
    parts = [part.astype(F32) for part in split3(table)]
    if 3 * high % 16:
        parts.append(jnp.zeros((high, LO), F32))
    parts = jnp.concatenate(parts, axis=0).astype(BF16)
    parts = lax.dot_general(parts, hot, NN, preferred_element_type=F32)
    found = parts[:high] + parts[high : 2 * high] + parts[2 * high : 3 * high]
    mask = lax.broadcasted_iota(I32, found.shape, 0).astype(F32) == hi
    return jnp.sum(jnp.where(mask, found, 0.0), axis=0, keepdims=True)


def row_iota(shape):
    return lax.broadcasted_iota(I32, shape, 0)


def pack_kernel(block_ref, slot_ref, expo_ref, pix_ref, mag_ref, w_ref, out_ref):
    rows = row_iota((8, LO))
    for r in range(16):
        star = slot_ref[r : r + 1, :] + (block_ref[0, r] * 256 + ((r // 2) % 2) * 512)
        pix = pix_ref[r : r + 1, :]
        expo = expo_ref[r : r + 1, :]
        w = w_ref[r : r + 1, :]
        ids = (star & 127, star >> 7, pix & 127, ((pix >> 7) & 1) * 8 + (pix >> 8), expo & 127, expo >> 7)
        tile = jnp.zeros((8, LO), I32)
        for f, field in enumerate(ids):
            tile = jnp.where(rows == f, field, tile)
        tile = jnp.where(rows == 6, w, tile.astype(F32))
        tile = jnp.where(rows == 7, w * mag_ref[r : r + 1, :], tile)
        out_ref[r // 4, :, (r % 4) * LO : (r % 4 + 1) * LO] = tile


S_LO, S_HI, P_LO, P_HI, E_LO, E_HI, W, WM = range(8)


def row(x, f):
    return x[f : f + 1]


def expo_kernel(obs_ref, out_ref):
    x = jnp.concatenate([obs_ref[k] for k in range(4)], axis=1)
    parts = split3(x)
    weighted, count = scatter(
        [[row(part, WM) for part in parts], [row(part, W) for part in parts]],
        row(parts[0], E_HI), 8, onehot(row(parts[0], E_LO)),
    )
    both = jnp.where(row_iota((8, LO)) < 4, weighted, pltpu.roll(count, 4, 0))
    for peer in range(16):
        out_ref[peer] = both


def fields_of(obs_ref, k):
    return jnp.concatenate([obs_ref[g, k] for g in range(8)], axis=1)


def own_fields(obs_ref, y, k):
    return jnp.concatenate([obs_ref[2 * y + rel, k] for rel in range(2)], axis=1)


def expo_hi(x):
    hi = row(x, E_HI)
    shift = (lax.broadcasted_iota(I32, hi.shape, 1) >> 9) & 1
    return hi + 4.0 * shift.astype(F32)


def two_rows(first, second):
    return jnp.where(row_iota((8, first.shape[1])) == 0, first, second)


def tile_kernel(
    obs_ref, g0s_ref, ds_ref, cs_ref, g0f_ref, df_ref, cf_ref, ru_ref, hop_ref, chip_ref,
    hot_s, hot_p, fit_ref,
):
    g0f_ref[...] = jnp.zeros((16, LO), F32)
    df_ref[...] = jnp.zeros((16, LO), F32)

    def sums(k, carry):
        x = fields_of(obs_ref, k)
        parts = split3(x)
        hs = onehot(row(parts[0], S_LO))
        hp = onehot(row(parts[0], P_LO))
        hot_s[k] = hs
        hot_p[k] = hp
        values = [[row(part, WM) for part in parts], [row(part, W) for part in parts]]
        weighted, count = scatter(values, row(parts[0], S_HI), 8, hs)
        diag = count + RIDGE
        g0s_ref[k] = weighted / diag
        ds_ref[k] = diag
        weighted, count = scatter(values, row(parts[0], P_HI), 16, hp)
        g0f_ref[...] += weighted
        df_ref[...] += count
        return carry

    lax.fori_loop(0, 4, sums, 0)
    diag = df_ref[...] + (4.0 * SMOOTH + RIDGE)
    g0f = g0f_ref[...] / diag
    df_ref[...] = diag
    g0f_ref[...] = g0f
    odd = lax.axis_index("c") == 1
    top = jnp.concatenate([g0f[0:1], g0f[8:9]], axis=0)
    bot = jnp.concatenate([g0f[7:8], g0f[15:16]], axis=0)
    hop_ref[...] = jnp.where(odd, bot, top)
    chip_ref[...] = jnp.where(odd, top, bot)
    cf_ref[...] = jnp.zeros((16, LO), F32)

    def couple(k, carry):
        x = fields_of(obs_ref, k)
        ids = x.astype(BF16)
        hs = hot_s[k]
        hp = hot_p[k]
        from_star = gather(g0s_ref[k], row(x, S_HI), hs)
        from_flat = gather(g0f_ref[...], row(x, P_HI), hp)
        fit = two_rows(from_star, from_flat) * row(x, W)
        parts = split3(fit)
        (cs_ref[k],) = scatter([[row(part, 1) for part in parts]], row(ids, S_HI), 8, hs)
        (added,) = scatter([[row(part, 0) for part in parts]], row(ids, P_HI), 16, hp)
        cf_ref[...] += added
        fit_ref[k] = fit
        return carry

    lax.fori_loop(0, 4, couple, 0)
    y = lax.axis_index("y")
    total = jnp.zeros((8, LO), F32)
    for k in range(4):
        x = own_fields(obs_ref, y, k)
        fit = fit_ref[k, :, pl.ds(pl.multiple_of(y * 1024, 1024), 1024)]
        parts = split3(fit)
        hi = expo_hi(x).astype(BF16)
        star_part, flat_part = scatter(
            [[row(part, 0) for part in parts], [row(part, 1) for part in parts]],
            hi, 8, onehot(row(x, E_LO).astype(BF16)),
        )
        total += star_part + flat_part
    ru_ref[...] = total


def pair_rows(first, second):
    low = row_iota((8, LO)) < 4
    return jnp.where(low, first, pltpu.roll(second, 4, 0)), jnp.where(
        low, pltpu.roll(first, 4, 0), second
    )


def beside(flat, above, below):
    left, right = flat[:8], flat[8:]
    rows = row_iota((8, LO))
    lanes = lax.broadcasted_iota(I32, (8, LO), 1)
    out = []
    left_up, right_up = pltpu.roll(left, 1, 1), pltpu.roll(right, 1, 1)
    left_down, right_down = pltpu.roll(left, 127, 1), pltpu.roll(right, 127, 1)
    sides = (
        jnp.where(lanes == 0, 0.0, left_up) + jnp.where(lanes == 127, right_down, left_down),
        jnp.where(lanes == 0, left_up, right_up) + jnp.where(lanes == 127, 0.0, right_down),
    )
    for i, half in enumerate((left, right)):
        upper = jnp.where(rows == 0, above[i : i + 1], pltpu.roll(half, 1, 0))
        lower = jnp.where(rows == 7, below[i : i + 1], pltpu.roll(half, 7, 0))
        out.append(sides[i] + upper + lower)
    return jnp.concatenate(out, axis=0)


def expo_apply_kernel(
    obs_ref, expo_ref, g0f_ref, cs_ref, cf_ref, ds_ref, df_ref, hop_ref, chip_ref,
    cs_out, ys_out, cf_out, yf_out, g0z_out, dz_out, top_out,
):
    for y in range(4):
        part = expo_ref[y]
        for xc in range(1, 8):
            part = part + expo_ref[xc * 4 + y]
        weighted, count = pair_rows(part[:8], part[8:])
        diag = count + RIDGE
        g0z_out[y] = weighted / diag
        dz_out[y] = diag
    cf_out[...] = cf_ref[...]

    def apply(k, carry):
        x = fields_of(obs_ref, k)
        ids = x.astype(BF16)
        hot = onehot(row(ids, E_LO))
        hi = expo_hi(x)
        found = [
            gather(g0z_out[y], hi[:, 1024 * y : 1024 * (y + 1)], hot[:, 1024 * y : 1024 * (y + 1)])
            for y in range(4)
        ]
        parts = split3(row(x, W) * jnp.concatenate(found, axis=1))
        (added,) = scatter([parts], row(ids, S_HI), 8, onehot(row(ids, S_LO)))
        total = cs_ref[k] + added
        cs_out[k] = total
        ys_out[k] = total / ds_ref[k]
        (added,) = scatter([parts], row(ids, P_HI), 16, onehot(row(ids, P_LO)))
        cf_out[...] += added
        return carry

    lax.fori_loop(0, 4, apply, 0)
    odd = lax.axis_index("c") == 1
    above = jnp.where(odd, chip_ref[...], hop_ref[...])
    below = jnp.where(odd, hop_ref[...], chip_ref[...])
    cf = cf_out[...] - SMOOTH * beside(g0f_ref[...], above, below)
    cf_out[...] = cf
    yf = cf / df_ref[...]
    yf_out[...] = yf
    top_out[...] = jnp.concatenate([yf[0:1], yf[8:9]], axis=0)


def fold8(a):
    total = a[0:8]
    for i in range(8, a.shape[0], 8):
        total = total + a[i : i + 8]
    return jnp.sum(total, axis=0, keepdims=True)


def fold_lanes(a):
    total = a[:, 0:LO]
    for i in range(LO, a.shape[1], LO):
        total = total + a[:, i : i + LO]
    return total


def last_kernel(
    obs_ref, g0s_ref, ds_ref, cs_ref, ys_ref, g0f_ref, df_ref, cf_ref, yf_ref, ru_ref, out_ref
):
    y = lax.axis_index("y")
    total = jnp.zeros((8, LO), F32)
    cross = jnp.zeros((1, LO), F32)
    yf = yf_ref[...]
    for k in range(4):
        x = own_fields(obs_ref, y, k)
        ids = x.astype(BF16)
        w = row(x, W)
        from_star = gather(ys_ref[k], row(x, S_HI), onehot(row(ids, S_LO)))
        from_flat = gather(yf, row(x, P_HI), onehot(row(ids, P_LO)))
        parts = split3(w * (from_star + from_flat))
        (added,) = scatter([parts], expo_hi(x).astype(BF16), 8, onehot(row(ids, E_LO)))
        total += added
        cross += fold_lanes(w * from_star * from_flat)
    out_ref[0:8] = jnp.where(row_iota((8, LO)) < 4, ru_ref[...], pltpu.roll(total, 4, 0))
    out_ref[8:16] = jnp.where(row_iota((8, LO)) < 4, pltpu.roll(ru_ref[...], 4, 0), total)
    g0s = jnp.concatenate([g0s_ref[k] for k in range(4)], axis=0)
    ds = jnp.concatenate([ds_ref[k] for k in range(4)], axis=0)
    cs = jnp.concatenate([cs_ref[k] for k in range(4)], axis=0)
    ys = jnp.concatenate([ys_ref[k] for k in range(4)], axis=0)
    g0f, df, cf = g0f_ref[...], df_ref[...], cf_ref[...]
    none = jnp.zeros((2, LO), F32)
    rho = 0.25 * (fold8(g0s * g0s * ds) + fold8(g0f * g0f * df))
    beta = 0.25 * (fold8(g0s * cs) + fold8(g0f * cf))
    eta = 0.25 * (fold8(cs * ys) + fold8(cf * yf))
    delta = 2.0 * cross - (0.25 * SMOOTH) * fold8(yf * beside(yf, none, none))
    out_ref[16:24] = jnp.concatenate([rho, beta, eta, delta, jnp.zeros((4, LO), F32)], axis=0)


def edge_kernel(payload_ref, yf_ref, next_ref, out_ref):
    edge = yf_ref[7:8] * next_ref[0:1] + yf_ref[15:16] * next_ref[1:2]
    edge = jnp.where(row_iota((8, LO)) == 3, -(0.5 * SMOOTH) * edge, 0.0)
    scal = payload_ref[16:24] + edge
    for peer in range(8):
        out_ref[peer, 0:16] = payload_ref[0:16]
        out_ref[peer, 16:24] = scal


def whole(a):
    return jnp.sum(jnp.sum(a, axis=0, keepdims=True), axis=1, keepdims=True)


def finish_kernel(
    sums_ref, g0z_ref, dz_ref, g0s_ref, ys_ref, g0f_ref, yf_ref, star_out, zero_out, flat_out
):
    y, zh = lax.axis_index("y"), lax.axis_index("zh")
    scal = sums_ref[0, 16:24]
    for peer in range(1, 32):
        scal = scal + sums_ref[peer, 16:24]
    z_rho = jnp.zeros((8, LO), F32)
    z_beta, z_eta, z_delta = z_rho, z_rho, z_rho
    z_own = z_rho
    for i in range(4):
        part = sums_ref[i, 0:16]
        for xc in range(1, 8):
            part = part + sums_ref[xc * 4 + i, 0:16]
        cz, qz = pair_rows(part[:8], part[8:])
        g0z, dz = g0z_ref[i], dz_ref[i]
        yz = cz / dz
        z_rho += g0z * g0z * dz
        z_beta += g0z * cz
        z_eta += cz * yz
        z_delta += qz * yz
        z_own = jnp.where(i == y, yz, z_own)
    rho0 = whole(z_rho) + whole(scal[0:1])
    beta = whole(z_beta) + whole(scal[1:2])
    eta = whole(z_eta) + whole(scal[2:3])
    delta = 2.0 * whole(z_delta) + whole(scal[3:4])
    curv0 = rho0 + beta
    step0 = rho0 / curv0
    left = beta / curv0
    rho1 = left * left * rho0 - 2.0 * step0 * left * beta + step0 * step0 * eta
    curv_g = (
        left * left * curv0
        - 2.0 * step0 * left * (beta + eta)
        + step0 * step0 * (eta + delta)
    )
    ratio = rho1 / rho0
    mixed = left * curv0 - step0 * (beta + eta)
    curv1 = curv_g + 2.0 * ratio * mixed + ratio * ratio * curv0
    step1 = rho1 / curv1
    along_g = step0 + step1 * (left + ratio)
    along_y = -step1 * step0
    star = along_g * g0s_ref[y] + along_y * ys_ref[y]
    star_out[...] = jnp.where(zh == 0, star, pltpu.roll(star, 4, 0))[0:4]
    zero_out[...] = (along_g * g0z_ref[y] + along_y * z_own)[0:4]
    flat = along_g * g0f_ref[...] + along_y * yf_ref[...]
    flat_out[:, 0:LO] = flat[:8]
    flat_out[:, LO : 2 * LO] = flat[8:]


VMEM = pl.BlockSpec(memory_space=pltpu.VMEM)
SMEM = pl.BlockSpec(memory_space=pltpu.SMEM)


def call(kernel, name, shapes, args, smem=0, scratch=(), flops=0):
    out = [jax.ShapeDtypeStruct(shape, F32) for shape in shapes]
    many = len(out) > 1
    return pl.pallas_call(
        kernel,
        name=name,
        out_shape=tuple(out) if many else out[0],
        in_specs=[SMEM] * smem + [VMEM] * (len(args) - smem),
        out_specs=tuple([VMEM] * len(out)) if many else VMEM,
        scratch_shapes=list(scratch),
        cost_estimate=pl.CostEstimate(flops=flops, bytes_accessed=1 << 20, transcendentals=0),
    )(*args)


def exchange(blocks, axes):
    return lax.all_to_all(blocks, axes, 0, 0, tiled=True)


def flat_pairs():
    def place(tile, y, zh):
        x, rest = divmod(tile, NZ * NC)
        zl, c = divmod(rest, NC)
        return (((x * NZ + zl) * NC + c) * NY + y) * NH + zh

    chip, hop, down = [], [], []
    for tile in range(NX * NZ * NC - 1):
        far = (tile + 1) % (NZ * NC) == 0
        for y in range(NY):
            for zh in range(NH):
                here, there = place(tile, y, zh), place(tile + 1, y, 1 - zh if far else zh)
                (hop if tile % 2 else chip).extend([(here, there), (there, here)])
                down.append((there, here))
    return chip, hop, down


def on_device(star_slot, star_block, exposure, superpixel, magnitude, weight):
    zh = lax.axis_index("zh")
    chip, hop, down = flat_pairs()
    obs = call(
        pack_kernel, "pack", [(4, 8, 512)],
        (star_block, star_slot[0], exposure[0], superpixel[0], magnitude[0], weight[0]), smem=1,
    )
    partner = lax.ppermute(obs, "zh", [(0, 1), (1, 0)])
    expo = exchange(call(expo_kernel, "expo", [(16, 8, LO)], (obs,)), ("zl", "zh"))
    expo = expo.reshape(NZ, NH, 8, LO).sum(axis=0)
    expo = jnp.where(zh == 0, expo, expo[::-1]).reshape(16, LO)
    both = jnp.stack([obs, partner])
    expo, both = lax.optimization_barrier((expo, both))
    tile_obs = exchange(jnp.broadcast_to(both[None], (NY, *both.shape)), "y")
    tile_obs = tile_obs.reshape(8, 4, 8, 512)
    expo, tile_obs = lax.optimization_barrier((expo, tile_obs))
    expo = exchange(jnp.broadcast_to(expo[None], (32, 16, LO)), ("x", "c", "y"))
    g0s, ds, cs, g0f, df, cf, ru, hop_row, chip_row = call(
        tile_kernel, "tile",
        [(4, 8, LO)] * 3 + [(16, LO)] * 3 + [(8, LO)] + [(2, LO)] * 2,
        (tile_obs,),
        scratch=[pltpu.VMEM((4, LO, 4096), BF16)] * 2 + [pltpu.VMEM((4, 8, 4096), F32)],
        flops=1 << 30,
    )
    by_hop = lax.ppermute(hop_row, ALL, hop)
    by_chip = lax.ppermute(chip_row, ALL, chip)
    cs, ys, cf, yf, g0z, dz, first = call(
        expo_apply_kernel, "apply",
        [(4, 8, LO)] * 2 + [(16, LO)] * 2 + [(4, 8, LO)] * 2 + [(2, LO)],
        (tile_obs, expo, g0f, cs, cf, ds, df, by_hop, by_chip),
        flops=1 << 30,
    )
    next_first = lax.ppermute(first, ALL, down)
    payload = call(
        last_kernel, "last", [(24, LO)],
        (tile_obs, g0s, ds, cs, ys, g0f, df, cf, yf, ru),
        flops=1 << 28,
    )
    payload = call(edge_kernel, "edge", [(NZ, 24, LO)], (payload, yf, next_first))
    sums = exchange(payload, "zl").sum(axis=0)
    sums = exchange(jnp.broadcast_to(sums[None], (32, 24, LO)), ("x", "c", "y"))
    star, zero, flat = call(
        finish_kernel, "finish", [(4, LO), (4, LO), (8, 2 * LO)],
        (sums, g0z, dz, g0s, ys, g0f, yf),
    )
    return star.reshape(-1), zero.reshape(-1), flat


def solution(mesh):
    split = Mesh(mesh.devices.reshape(NX, NZ, NC, NY, NH), ALL)
    tile, loop = ("x", "zl", "c"), ("y", "zh")
    placed = (
        P(tile, loop, None),
        P(tile, loop),
        P(tile, loop, None),
        P(tile, loop, None),
        P(tile, loop, None),
        P(tile, loop, None),
    )
    return jax.shard_map(
        on_device,
        mesh=split,
        in_specs=placed,
        out_specs=(P(ALL), P(loop), P(tile, None)),
        check_vma=False,
    )
```

```python
import jax
import jax.numpy as jnp
from jax import lax
from jax.experimental import pallas as pl
from jax.experimental.pallas import tpu as pltpu
from jax.sharding import Mesh
from jax.sharding import PartitionSpec as P

SMOOTH = 2.0
RIDGE = 0.5
LO, HALF, HI = 128, 64, 16
NX, NZ, NC, NY, NH = 4, 8, 2, 4, 2
ALL = ("x", "zl", "c", "y", "zh")
PLANE = ("x", "c", "y")
F32 = jnp.float32
I32 = jnp.int32
BF16 = jnp.bfloat16
NT = (((1,), (1,)), ((), ()))
NN = (((1,), (0,)), ((), ()))
S_LO, S_HI, P_LO, P_HI, E_LO, E_HI, W, WM = range(8)
STAR, FLAT = 3, 7


def split3(v):
    first = v.astype(BF16)
    rest = v - first.astype(F32)
    second = rest.astype(BF16)
    return first, second, (rest - second.astype(F32)).astype(BF16)


def row(x, f):
    return x[f : f + 1]


def row_iota(shape):
    return lax.broadcasted_iota(I32, shape, 0)


def lane_tiles(n):
    return [slice(i, i + LO) for i in range(0, n, LO)]


def is_row(ids, count):
    rows = row_iota((count, LO)).astype(F32).astype(ids.dtype)
    return [rows == jnp.broadcast_to(ids[:, at], (count, LO)) for at in lane_tiles(ids.shape[1])]


def onehot(lo, size):
    one, zero = jnp.ones((), BF16), jnp.zeros((), BF16)
    return jnp.concatenate([jnp.where(same, one, zero) for same in is_row(lo, size)], axis=1)


def scatter(values, hi, hot):
    masks = is_row(hi, HI)
    zero = jnp.zeros((), BF16)
    rows = jnp.concatenate(
        [
            jnp.concatenate(
                [
                    jnp.where(mask, jnp.broadcast_to(part[:, at], (HI, LO)), zero)
                    for mask, at in zip(masks, lane_tiles(hi.shape[1]))
                ],
                axis=1,
            )
            for value in values
            for part in value
        ],
        axis=0,
    )
    sums = lax.dot_general(rows, hot, NT, preferred_element_type=F32)
    sums = [sums[at : at + HI] for at in range(0, sums.shape[0], HI)]
    return [sums[i] + sums[i + 1] + sums[i + 2] for i in range(0, len(sums), 3)]


def picked(table, hi, hot):
    parts = jnp.concatenate([part.astype(F32) for part in split3(table)], axis=0).astype(BF16)
    parts = lax.dot_general(parts, hot, NN, preferred_element_type=F32)
    found = parts[:HI] + parts[HI : 2 * HI] + parts[2 * HI :]
    found = jnp.where(row_iota(found.shape).astype(F32) == hi, found, 0.0)
    return found[:8] + found[8:]


def folded(a, *shifts):
    for shift in shifts:
        a = a + pltpu.roll(a, shift, 0)
    return a


def gather(table, hi, hot):
    return folded(picked(table, hi, hot), 4, 2, 1)


def gather_both(first, second):
    a, b = folded(picked(*first), 4), folded(picked(*second), 4)
    return folded(jnp.where(row_iota(a.shape) & 7 < 4, a, b), 2, 1)


def pack_kernel(block_ref, slot_ref, expo_ref, pix_ref, mag_ref, w_ref, out_ref):
    rows = row_iota((8, LO))
    for r in range(16):
        star = slot_ref[r : r + 1, :] + (block_ref[0, r] * 256 + ((r // 2) % 2) * 512)
        pix = pix_ref[r : r + 1, :]
        expo = expo_ref[r : r + 1, :]
        w = w_ref[r : r + 1, :]
        ids = (
            star & 63,
            ((star >> 6) & 1) * 8 + (star >> 7),
            pix & 127,
            ((pix >> 7) & 1) * 8 + (pix >> 8),
            expo & 63,
            ((expo >> 6) & 1) * 4 + (expo >> 7),
        )
        tile = jnp.zeros((8, LO), I32)
        for f, field in enumerate(ids):
            tile = jnp.where(rows == f, field, tile)
        tile = jnp.where(rows == W, w, tile.astype(F32))
        tile = jnp.where(rows == WM, w * mag_ref[r : r + 1, :], tile)
        out_ref[r // 4, :, (r % 4) * LO : (r % 4 + 1) * LO] = tile


def expo_kernel(obs_ref, out_ref):
    x = jnp.concatenate([obs_ref[k] for k in range(4)], axis=1)
    parts = split3(x)
    weighted, count = scatter(
        [[row(part, WM) for part in parts], [row(part, W) for part in parts]],
        row(parts[0], E_HI),
        onehot(row(parts[0], E_LO), HALF),
    )
    both = jnp.concatenate([weighted[:8], count[:8]], axis=1)
    for peer in range(NZ * NH):
        out_ref[peer] = both


def fields_of(obs_ref, k):
    return jnp.concatenate([obs_ref[g, k] for g in range(8)], axis=1)


def own_fields(obs_ref, y, k):
    return jnp.concatenate([obs_ref[2 * y + rel, k] for rel in range(2)], axis=1)


def expo_hi(x):
    hi = row(x, E_HI)
    rel = (lax.broadcasted_iota(I32, hi.shape, 1) >> 9) & 1
    return hi + 8.0 * rel.astype(F32)


def by_rel(pair):
    return jnp.concatenate([pair[:8], pair[8:]], axis=1)


def sums_kernel(obs_ref, g0s_ref, ds_ref, g0f_ref, df_ref, hop_ref, chip_ref):
    g0f_ref[...] = jnp.zeros((HI, LO), F32)
    df_ref[...] = jnp.zeros((HI, LO), F32)

    def sums(k, carry):
        parts = split3(fields_of(obs_ref, k))
        values = [[row(part, WM) for part in parts], [row(part, W) for part in parts]]
        weighted, count = scatter(values, row(parts[0], S_HI), onehot(row(parts[0], S_LO), HALF))
        diag = count + RIDGE
        g0s_ref[k] = weighted / diag
        ds_ref[k] = diag
        weighted, count = scatter(values, row(parts[0], P_HI), onehot(row(parts[0], P_LO), LO))
        g0f_ref[...] += weighted
        df_ref[...] += count
        return carry

    lax.fori_loop(0, 4, sums, 0)
    diag = df_ref[...] + (4.0 * SMOOTH + RIDGE)
    g0f = g0f_ref[...] / diag
    df_ref[...] = diag
    g0f_ref[...] = g0f
    odd = lax.axis_index("c") == 1
    top = jnp.concatenate([g0f[0:1], g0f[8:9]], axis=0)
    bot = jnp.concatenate([g0f[7:8], g0f[15:16]], axis=0)
    hop_ref[...] = jnp.where(odd, bot, top)
    chip_ref[...] = jnp.where(odd, top, bot)


def couple_kernel(obs_ref, g0s_ref, g0f_ref, cs_ref, cf_ref, ru_ref, fit_ref):
    cf_ref[...] = jnp.zeros((HI, LO), F32)

    def couple(k, carry):
        x = fields_of(obs_ref, k)
        ids = x.astype(BF16)
        hs = onehot(row(ids, S_LO), HALF)
        hp = onehot(row(ids, P_LO), LO)
        fit = row(x, W) * gather_both(
            (g0s_ref[k], row(x, S_HI), hs), (g0f_ref[...], row(x, P_HI), hp)
        )
        parts = split3(fit)
        (cs_ref[k],) = scatter([[row(part, FLAT) for part in parts]], row(ids, S_HI), hs)
        (added,) = scatter([[row(part, STAR) for part in parts]], row(ids, P_HI), hp)
        cf_ref[...] += added
        fit_ref[k] = fit
        return carry

    lax.fori_loop(0, 4, couple, 0)
    y = lax.axis_index("y")
    total = jnp.zeros((HI, HALF), F32)
    for k in range(4):
        x = own_fields(obs_ref, y, k)
        fit = fit_ref[k, :, pl.ds(pl.multiple_of(y * 1024, 1024), 1024)]
        (added,) = scatter(
            [split3(row(fit, STAR) + row(fit, FLAT))],
            expo_hi(x).astype(BF16),
            onehot(row(x, E_LO).astype(BF16), HALF),
        )
        total += added
    ru_ref[...] = total


def beside(flat, above, below):
    left, right = flat[:8], flat[8:]
    rows = row_iota((8, LO))
    lanes = lax.broadcasted_iota(I32, (8, LO), 1)
    out = []
    left_up, right_up = pltpu.roll(left, 1, 1), pltpu.roll(right, 1, 1)
    left_down, right_down = pltpu.roll(left, 127, 1), pltpu.roll(right, 127, 1)
    sides = (
        jnp.where(lanes == 0, 0.0, left_up) + jnp.where(lanes == 127, right_down, left_down),
        jnp.where(lanes == 0, left_up, right_up) + jnp.where(lanes == 127, 0.0, right_down),
    )
    for i, half in enumerate((left, right)):
        upper = jnp.where(rows == 0, above[i : i + 1], pltpu.roll(half, 1, 0))
        lower = jnp.where(rows == 7, below[i : i + 1], pltpu.roll(half, 7, 0))
        out.append(sides[i] + upper + lower)
    return jnp.concatenate(out, axis=0)


def expo_apply_kernel(
    obs_ref, expo_ref, g0f_ref, cf_ref, df_ref, hop_ref, chip_ref,
    fit_ref, cf_out, yf_out, g0z_out, dz_out, top_out,
):
    for y in range(4):
        part = expo_ref[y]
        for xc in range(1, 8):
            part = part + expo_ref[xc * 4 + y]
        diag = part[:, HALF:] + RIDGE
        g0z_out[y] = part[:, :HALF] / diag
        dz_out[y] = diag
    cf_out[...] = cf_ref[...]

    def apply(k, carry):
        x = fields_of(obs_ref, k)
        ids = x.astype(BF16)
        hot = onehot(row(ids, E_LO), HALF)
        hi = expo_hi(x)
        found = [
            gather(g0z_out[y], hi[:, 1024 * y : 1024 * (y + 1)], hot[:, 1024 * y : 1024 * (y + 1)])
            for y in range(4)
        ]
        fit = row(x, W) * jnp.concatenate(found, axis=1)
        fit_ref[k] = fit
        parts = [row(part, 0) for part in split3(fit)]
        (added,) = scatter([parts], row(ids, P_HI), onehot(row(ids, P_LO), LO))
        cf_out[...] += added
        return carry

    lax.fori_loop(0, 4, apply, 0)
    odd = lax.axis_index("c") == 1
    above = jnp.where(odd, chip_ref[...], hop_ref[...])
    below = jnp.where(odd, hop_ref[...], chip_ref[...])
    cf = cf_out[...] - SMOOTH * beside(g0f_ref[...], above, below)
    cf_out[...] = cf
    yf = cf / df_ref[...]
    yf_out[...] = yf
    top_out[...] = jnp.concatenate([yf[0:1], yf[8:9]], axis=0)


def fold8(a):
    total = a[0:8]
    for i in range(8, a.shape[0], 8):
        total = total + a[i : i + 8]
    total = jnp.sum(total, axis=0, keepdims=True)
    if total.shape[1] < LO:
        total = jnp.concatenate([total, jnp.zeros((1, LO - total.shape[1]), F32)], axis=1)
    return total


def fold_lanes(a):
    total = a[:, 0:LO]
    for i in range(LO, a.shape[1], LO):
        total = total + a[:, i : i + LO]
    return total


def last_kernel(
    obs_ref, fit_ref, g0s_ref, ds_ref, cs_ref, g0f_ref, df_ref, cf_ref, yf_ref, ru_ref, ys_ref, out_ref
):
    star = jnp.zeros((3, LO), F32)
    rho, beta, eta = row(star, 0), row(star, 1), row(star, 2)

    def finish_star(k, sums):
        ids = fields_of(obs_ref, k).astype(BF16)
        parts = [row(part, 0) for part in split3(fit_ref[k])]
        (added,) = scatter([parts], row(ids, S_HI), onehot(row(ids, S_LO), HALF))
        g0s, ds = g0s_ref[k], ds_ref[k]
        cs = cs_ref[k] + added
        ys = cs / ds
        ys_ref[k] = ys
        return (
            sums[0] + fold8(g0s * g0s * ds),
            sums[1] + fold8(g0s * cs),
            sums[2] + fold8(cs * ys),
        )

    rho, beta, eta = lax.fori_loop(0, 4, finish_star, (rho, beta, eta))
    y = lax.axis_index("y")
    total = jnp.zeros((HI, HALF), F32)
    cross = jnp.zeros((1, LO), F32)
    yf = yf_ref[...]
    for k in range(4):
        x = own_fields(obs_ref, y, k)
        ids = x.astype(BF16)
        w = row(x, W)
        both = gather_both(
            (ys_ref[k], row(x, S_HI), onehot(row(ids, S_LO), HALF)),
            (yf, row(x, P_HI), onehot(row(ids, P_LO), LO)),
        )
        from_star, from_flat = row(both, STAR), row(both, FLAT)
        (added,) = scatter(
            [split3(w * (from_star + from_flat))],
            expo_hi(x).astype(BF16),
            onehot(row(ids, E_LO), HALF),
        )
        total += added
        cross += fold_lanes(w * from_star * from_flat)
    ru = ru_ref[...]
    out_ref[0:16] = jnp.concatenate([ru, total], axis=1)
    g0f, df, cf = g0f_ref[...], df_ref[...], cf_ref[...]
    none = jnp.zeros((2, LO), F32)
    rho = 0.25 * (rho + fold8(g0f * g0f * df))
    beta = 0.25 * (beta + fold8(g0f * cf))
    eta = 0.25 * (eta + fold8(cf * yf))
    delta = 2.0 * cross - (0.25 * SMOOTH) * fold8(yf * beside(yf, none, none))
    out_ref[16:24] = jnp.concatenate([rho, beta, eta, delta, jnp.zeros((4, LO), F32)], axis=0)


def edge_kernel(payload_ref, yf_ref, next_ref, out_ref):
    edge = yf_ref[7:8] * next_ref[0:1] + yf_ref[15:16] * next_ref[1:2]
    edge = jnp.where(row_iota((8, LO)) == 3, -(0.5 * SMOOTH) * edge, 0.0)
    scal = payload_ref[16:24] + edge
    for peer in range(NZ):
        out_ref[peer, 0:16] = payload_ref[0:16]
        out_ref[peer, 16:24] = scal


def whole(a):
    return jnp.sum(jnp.sum(a, axis=0, keepdims=True), axis=1, keepdims=True)


def finish_kernel(
    sums_ref, g0z_ref, dz_ref, g0s_ref, ys_ref, g0f_ref, yf_ref, star_out, zero_out, flat_out
):
    y, zh = lax.axis_index("y"), lax.axis_index("zh")
    scal = sums_ref[0, 16:24]
    for peer in range(1, 32):
        scal = scal + sums_ref[peer, 16:24]
    z_rho = jnp.zeros((HI, HALF), F32)
    z_beta, z_eta, z_delta = z_rho, z_rho, z_rho
    z_own = z_rho
    for i in range(4):
        part = sums_ref[i, 0:16]
        for xc in range(1, 8):
            part = part + sums_ref[xc * 4 + i, 0:16]
        cz, qz = part[:, :HALF], part[:, HALF:]
        g0z, dz = g0z_ref[i], dz_ref[i]
        yz = cz / dz
        z_rho += g0z * g0z * dz
        z_beta += g0z * cz
        z_eta += cz * yz
        z_delta += qz * yz
        z_own = jnp.where(i == y, yz, z_own)
    rho0 = whole(z_rho) + whole(scal[0:1])
    beta = whole(z_beta) + whole(scal[1:2])
    eta = whole(z_eta) + whole(scal[2:3])
    delta = 2.0 * whole(z_delta) + whole(scal[3:4])
    curv0 = rho0 + beta
    step0 = rho0 / curv0
    left = beta / curv0
    rho1 = left * left * rho0 - 2.0 * step0 * left * beta + step0 * step0 * eta
    curv_g = (
        left * left * curv0
        - 2.0 * step0 * left * (beta + eta)
        + step0 * step0 * (eta + delta)
    )
    ratio = rho1 / rho0
    mixed = left * curv0 - step0 * (beta + eta)
    curv1 = curv_g + 2.0 * ratio * mixed + ratio * ratio * curv0
    step1 = rho1 / curv1
    along_g = step0 + step1 * (left + ratio)
    along_y = -step1 * step0
    star = by_rel(along_g * g0s_ref[y] + along_y * ys_ref[y])
    star_out[...] = jnp.where(zh == 0, star, pltpu.roll(star, 4, 0))[0:4]
    zero = along_g * g0z_ref[y] + along_y * z_own
    zero_out[...] = jnp.concatenate([zero[0:4], pltpu.roll(zero[0:8], 4, 0)[0:4]], axis=1)
    flat_out[...] = by_rel(along_g * g0f_ref[...] + along_y * yf_ref[...])


VMEM = pl.BlockSpec(memory_space=pltpu.VMEM)
SMEM = pl.BlockSpec(memory_space=pltpu.SMEM)


def call(kernel, shapes, args, smem=0, scratch=(), mib=8, work=20):
    out = [jax.ShapeDtypeStruct(shape, F32) for shape in shapes]
    many = len(out) > 1
    return pl.pallas_call(
        kernel,
        name=kernel.__name__,
        out_shape=tuple(out) if many else out[0],
        in_specs=[SMEM] * smem + [VMEM] * (len(args) - smem),
        out_specs=tuple([VMEM] * len(out)) if many else VMEM,
        scratch_shapes=list(scratch),
        compiler_params=pltpu.CompilerParams(vmem_limit_bytes=mib << 20),
        cost_estimate=pl.CostEstimate(flops=1 << work, bytes_accessed=1 << 20, transcendentals=0),
    )(*args)


def exchange(blocks, axes):
    return lax.all_to_all(blocks, axes, 0, 0, tiled=True)


def to_all(block, peers, axes):
    return exchange(jnp.broadcast_to(block[None], (peers, *block.shape)), axes)


def flat_pairs():
    def place(tile, y, zh):
        x, rest = divmod(tile, NZ * NC)
        zl, c = divmod(rest, NC)
        return (((x * NZ + zl) * NC + c) * NY + y) * NH + zh

    chip, hop, down = [], [], []
    for tile in range(NX * NZ * NC - 1):
        far = (tile + 1) % (NZ * NC) == 0
        for y in range(NY):
            for zh in range(NH):
                here, there = place(tile, y, zh), place(tile + 1, y, 1 - zh if far else zh)
                (hop if tile % 2 else chip).extend([(here, there), (there, here)])
                down.append((there, here))
    return chip, hop, down


def on_device(star_slot, star_block, exposure, superpixel, magnitude, weight):
    zh = lax.axis_index("zh")
    chip, hop, down = flat_pairs()
    stars, flats = (4, HI, HALF), (HI, LO)
    obs = call(
        pack_kernel, [(4, 8, 512)],
        (star_block, star_slot[0], exposure[0], superpixel[0], magnitude[0], weight[0]), smem=1,
    )
    partner = lax.ppermute(obs, "zh", [(0, 1), (1, 0)])
    expo = exchange(call(expo_kernel, [(16, 8, LO)], (obs,)), ("zl", "zh"))
    expo = expo.reshape(NZ, NH, 8, LO).sum(axis=0)
    expo = jnp.where(zh == 0, expo, expo[::-1]).reshape(HI, LO)
    both = jnp.stack([obs, partner])
    expo, both = lax.optimization_barrier((expo, both))
    tile_obs = to_all(both, NY, "y").reshape(8, 4, 8, 512)
    expo, tile_obs = lax.optimization_barrier((expo, tile_obs))
    expo = to_all(expo, 32, PLANE)
    g0s, ds, g0f, df, hop_row, chip_row = call(
        sums_kernel, [stars] * 2 + [flats] * 2 + [(2, LO)] * 2, (tile_obs,), mib=16, work=29
    )
    by_hop = lax.ppermute(hop_row, ALL, hop)
    by_chip = lax.ppermute(chip_row, ALL, chip)
    cs, cf, ru = call(
        couple_kernel, [stars, flats, (HI, HALF)], (tile_obs, g0s, g0f),
        scratch=[pltpu.VMEM((4, 8, 4096), F32)], mib=16, work=30,
    )
    fit, cf, yf, g0z, dz, first = call(
        expo_apply_kernel, [(4, 8, 4096)] + [flats] * 2 + [stars] * 2 + [(2, LO)],
        (tile_obs, expo.reshape(32, HI, LO), g0f, cf, df, by_hop, by_chip), mib=16, work=30,
    )
    next_first = lax.ppermute(first, ALL, down)
    ys, payload = call(
        last_kernel, [stars, (24, LO)],
        (tile_obs, fit, g0s, ds, cs, g0f, df, cf, yf, ru), mib=16, work=30,
    )
    payload = call(edge_kernel, [(NZ, 24, LO)], (payload, yf, next_first))
    sums = exchange(payload, "zl").sum(axis=0)
    sums = to_all(sums, 32, PLANE)
    star, zero, flat = call(
        finish_kernel, [(4, LO), (4, LO), (8, 2 * LO)], (sums, g0z, dz, g0s, ys, g0f, yf)
    )
    return star.reshape(-1), zero.reshape(-1), flat


def solution(mesh):
    split = Mesh(mesh.devices.reshape(NX, NZ, NC, NY, NH), ALL)
    tile, loop = ("x", "zl", "c"), ("y", "zh")
    placed = (
        P(tile, loop, None),
        P(tile, loop),
        P(tile, loop, None),
        P(tile, loop, None),
        P(tile, loop, None),
        P(tile, loop, None),
    )
    return jax.shard_map(
        on_device,
        mesh=split,
        in_specs=placed,
        out_specs=(P(ALL), P(loop), P(tile, None)),
        check_vma=False,
    )
```

```python
import jax
import jax.numpy as jnp
from jax import lax
from jax.experimental import pallas as pl
from jax.experimental.pallas import tpu as pltpu
from jax.sharding import Mesh
from jax.sharding import PartitionSpec as P

SMOOTH = 2.0
RIDGE = 0.5
LO, HALF, HI = 128, 64, 16
NX, NZ, NC, NY, NH = 4, 8, 2, 4, 2
ALL = ("x", "zl", "c", "y", "zh")
PLANE = ("x", "c", "y")
COLS = ("x", "c")
F32 = jnp.float32
I32 = jnp.int32
BF16 = jnp.bfloat16
NT = (((1,), (1,)), ((), ()))
NN = (((1,), (0,)), ((), ()))
S, PX, E, W, WM = range(5)
STAR, FLAT = 3, 7


def split3(v):
    first = v.astype(BF16)
    rest = v - first.astype(F32)
    second = rest.astype(BF16)
    return first, second, (rest - second.astype(F32)).astype(BF16)


def row_iota(shape):
    return lax.broadcasted_iota(I32, shape, 0)


def row(x, f):
    return x[f : f + 1]


def rows_of(tiles):
    return [row(tile, i) for tile in tiles for i in range(tile.shape[0])]


def small(ids):
    return ids.astype(F32).astype(BF16)


def joined(tiles):
    return jnp.concatenate(tiles, axis=1)


def is_row(ids, count):
    rows = row_iota((count, LO)).astype(F32).astype(ids[0].dtype)
    return [rows == jnp.broadcast_to(one, (count, LO)) for one in ids]


def onehot(lo, size):
    one, zero = jnp.ones((), BF16), jnp.zeros((), BF16)
    return joined([jnp.where(same, one, zero) for same in is_row(lo, size)])


def scatter(values, hi, hot):
    masks = is_row(hi, HI)
    zero = jnp.zeros((), BF16)
    rows = [
        joined([jnp.where(m, jnp.broadcast_to(p, (HI, LO)), zero) for m, p in zip(masks, part)])
        for value in values
        for part in value
    ]
    sums = lax.dot_general(jnp.concatenate(rows, axis=0), hot, NT, preferred_element_type=F32)
    sums = [sums[at : at + HI] for at in range(0, sums.shape[0], HI)]
    return [sums[i] + sums[i + 1] + sums[i + 2] for i in range(0, len(sums), 3)]


def picked(table, hi, hot):
    parts = jnp.concatenate([part.astype(F32) for part in split3(table)], axis=0).astype(BF16)
    parts = lax.dot_general(parts, hot, NN, preferred_element_type=F32)
    found = parts[:HI] + parts[HI : 2 * HI] + parts[2 * HI :]
    found = jnp.where(joined(is_row(hi, HI)), found, 0.0)
    return found[:8] + found[8:]


def folded(a, *shifts):
    for shift in shifts:
        a = a + pltpu.roll(a, shift, 0)
    return a


def gather(table, hi, hot):
    return folded(picked(table, hi, hot), 4, 2, 1)


def gather_both(first, second):
    a, b = folded(picked(*first), 4), folded(picked(*second), 4)
    return folded(jnp.where((row_iota(a.shape) & 7) < 4, a, b), 2, 1)


def across(x, f):
    return [x[f : f + 1, i : i + LO] for i in range(0, x.shape[1], LO)]


def split_rows(tiles):
    return [rows_of(part) for part in zip(*(split3(tile) for tile in tiles))]


class Ids:
    def __init__(self, tiles, size, offsets=None):
        ids = [tile.astype(I32) for tile in tiles]
        if offsets is None:
            high = [i >> 7 for i in ids]
        else:
            high = [((i >> 6) & 1) * 4 + (i >> 7) + at for i, at in zip(ids, offsets)]
        self.size = size
        self.low_rows = rows_of([small(i & (size - 1)) for i in ids])
        self.bf = rows_of([small(h) for h in high])
        self.full = rows_of([h.astype(F32) for h in high])

    def hot(self):
        return onehot(self.low_rows, self.size)


def copies(refs, held, sems):
    return [pltpu.make_async_copy(ref, to, sems.at[i]) for i, (ref, to) in enumerate(zip(refs, held))]


def pack_kernel(block_ref, slot_in, expo_in, pix_in, mag_in, w_in, out_ref, slot, expo, pix, mag, w, sems):
    moves = copies((slot_in, expo_in, pix_in, mag_in, w_in), (slot, expo, pix, mag, w), sems)
    for move in moves:
        move.start()
    for move in moves:
        move.wait()
    rows = row_iota((8, LO))
    for kk in range(2):
        at = pl.ds(8 * kk, 8)
        base = jnp.zeros((8, LO), I32)
        for i in range(8):
            base = jnp.where(rows == i, block_ref[0, 8 * kk + i] * 256 + (i // 2) * 512, base)
        p = pix[at, :]
        out_ref[kk, 0] = (slot[at, :] + base).astype(F32)
        out_ref[kk, 1] = ((((p >> 7) & 1) * 8 + (p >> 8)) * LO + (p & 127)).astype(F32)
        out_ref[kk, 2] = expo[at, :].astype(F32)
        out_ref[kk, 3] = w[at, :]
        out_ref[kk, 4] = w[at, :] * mag[at, :]


def expo_kernel(obs_ref, out_ref):
    ids = Ids([obs_ref[kk, E] for kk in range(2)], HALF, (0, 0))
    weighted, count = scatter(
        [split_rows([obs_ref[kk, f] for kk in range(2)]) for f in (WM, W)], ids.bf, ids.hot()
    )
    both = joined([weighted[:8], count[:8]])
    for peer in range(NZ * NH):
        out_ref[peer] = both


def field(obs_ref, y, rel, kk, f):
    return obs_ref[y, pl.ds(pl.multiple_of(rel * 80 + kk * 40 + f * 8, 8), 8), :]


def chunk(obs_ref, step, f):
    kk, half = step // 2, step % 2
    return [field(obs_ref, 2 * half + yy, rel, kk, f) for yy in range(2) for rel in range(2)]


def own(obs_ref, y, kk, f):
    return [field(obs_ref, y, rel, kk, f) for rel in range(2)]


def sums_kernel(obs_ref, g0s_ref, ds_ref, g0f_ref, df_ref, hop_ref, chip_ref):
    for ref in (g0s_ref, ds_ref, g0f_ref, df_ref):
        ref[...] = jnp.zeros(ref.shape, F32)

    def sums(step, carry):
        values = [split_rows(chunk(obs_ref, step, f)) for f in (WM, W)]
        ids = Ids(chunk(obs_ref, step, S), LO)
        weighted, count = scatter(values, ids.bf, ids.hot())
        g0s_ref[step // 2] += weighted
        ds_ref[step // 2] += count
        ids = Ids(chunk(obs_ref, step, PX), LO)
        weighted, count = scatter(values, ids.bf, ids.hot())
        g0f_ref[...] += weighted
        df_ref[...] += count
        return carry

    lax.fori_loop(0, 4, sums, 0)
    diag = df_ref[...] + (4.0 * SMOOTH + RIDGE)
    g0f = g0f_ref[...] / diag
    df_ref[...] = diag
    g0f_ref[...] = g0f
    diag = ds_ref[...] + RIDGE
    g0s_ref[...] = g0s_ref[...] / diag
    ds_ref[...] = diag
    odd = lax.axis_index("c") == 1
    top = jnp.concatenate([g0f[0:1], g0f[8:9]], axis=0)
    bot = jnp.concatenate([g0f[7:8], g0f[15:16]], axis=0)
    hop_ref[...] = jnp.where(odd, bot, top)
    chip_ref[...] = jnp.where(odd, top, bot)


def couple_kernel(obs_ref, g0s_ref, g0f_ref, cs_ref, cf_ref, ru_ref, fit_ref):
    cs_ref[...] = jnp.zeros(cs_ref.shape, F32)
    cf_ref[...] = jnp.zeros((HI, LO), F32)

    def couple(step, carry):
        star, flat = Ids(chunk(obs_ref, step, S), LO), Ids(chunk(obs_ref, step, PX), LO)
        hs, hp = star.hot(), flat.hot()
        fit = joined(rows_of(chunk(obs_ref, step, W))) * gather_both(
            (g0s_ref[step // 2], star.full, hs), (g0f_ref[...], flat.full, hp)
        )
        parts = split3(fit)
        (added,) = scatter([[across(part, FLAT) for part in parts]], star.bf, hs)
        cs_ref[step // 2] += added
        (added,) = scatter([[across(part, STAR) for part in parts]], flat.bf, hp)
        cf_ref[...] += added
        fit_ref[step] = fit
        return carry

    lax.fori_loop(0, 4, couple, 0)
    y = lax.axis_index("y")
    total = jnp.zeros((HI, HALF), F32)
    for kk in range(2):
        ids = Ids(own(obs_ref, y, kk, E), HALF, (0, 8))
        at = pl.ds(pl.multiple_of((y % 2) * 2048, 2048), 2048)
        fit = fit_ref[2 * kk + y // 2, :, at]
        parts = split3(row(fit, STAR) + row(fit, FLAT))
        (added,) = scatter([[across(part, 0) for part in parts]], ids.bf, ids.hot())
        total += added
    ru_ref[...] = total


def beside(flat, above, below):
    left, right = flat[:8], flat[8:]
    rows = row_iota((8, LO))
    lanes = lax.broadcasted_iota(I32, (8, LO), 1)
    out = []
    left_up, right_up = pltpu.roll(left, 1, 1), pltpu.roll(right, 1, 1)
    left_down, right_down = pltpu.roll(left, 127, 1), pltpu.roll(right, 127, 1)
    sides = (
        jnp.where(lanes == 0, 0.0, left_up) + jnp.where(lanes == 127, right_down, left_down),
        jnp.where(lanes == 0, left_up, right_up) + jnp.where(lanes == 127, 0.0, right_down),
    )
    for i, half in enumerate((left, right)):
        upper = jnp.where(rows == 0, above[i : i + 1], pltpu.roll(half, 1, 0))
        lower = jnp.where(rows == 7, below[i : i + 1], pltpu.roll(half, 7, 0))
        out.append(sides[i] + upper + lower)
    return jnp.concatenate(out, axis=0)


def expo_apply_kernel(
    obs_ref, expo_ref, g0f_ref, cf_ref, df_ref, hop_ref, chip_ref,
    fit_ref, cf_out, yf_out, g0z_out, dz_out, top_out,
):
    part = expo_ref[0]
    for xc in range(1, 8):
        part = part + expo_ref[xc]
    for y in range(4):
        diag = part[16 * y : 16 * y + 16, HALF:] + RIDGE
        g0z_out[y] = part[16 * y : 16 * y + 16, :HALF] / diag
        dz_out[y] = diag
    cf_out[...] = cf_ref[...]

    def apply(step, carry):
        expo = Ids(chunk(obs_ref, step, E), HALF, (0, 8, 0, 8))
        hot = expo.hot()
        found = [
            gather(
                g0z_out[2 * (step % 2) + yy],
                expo.full[16 * yy : 16 * yy + 16],
                hot[:, 2048 * yy : 2048 * (yy + 1)],
            )
            for yy in range(2)
        ]
        fit = joined(rows_of(chunk(obs_ref, step, W))) * joined(found)
        fit_ref[step] = fit
        flat = Ids(chunk(obs_ref, step, PX), LO)
        (added,) = scatter([[across(part, 0) for part in split3(fit)]], flat.bf, flat.hot())
        cf_out[...] += added
        return carry

    lax.fori_loop(0, 4, apply, 0)
    odd = lax.axis_index("c") == 1
    above = jnp.where(odd, chip_ref[...], hop_ref[...])
    below = jnp.where(odd, hop_ref[...], chip_ref[...])
    cf = cf_out[...] - SMOOTH * beside(g0f_ref[...], above, below)
    cf_out[...] = cf
    yf = cf / df_ref[...]
    yf_out[...] = yf
    top_out[...] = jnp.concatenate([yf[0:1], yf[8:9]], axis=0)


def fold8(a):
    total = a[0:8]
    for i in range(8, a.shape[0], 8):
        total = total + a[i : i + 8]
    return jnp.sum(total, axis=0, keepdims=True)


def fold_lanes(a):
    total = a[:, 0:LO]
    for i in range(LO, a.shape[1], LO):
        total = total + a[:, i : i + LO]
    return total


def last_kernel(
    obs_ref, fit_ref, g0s_ref, ds_ref, cs_in, g0f_ref, df_ref, cf_ref, yf_ref, ru_ref, ys_ref, out_ref, cs_ref
):
    cs_ref[...] = cs_in[...]

    def finish_star(step, carry):
        star = Ids(chunk(obs_ref, step, S), LO)
        parts = split3(fit_ref[step])
        (added,) = scatter([[across(part, 0) for part in parts]], star.bf, star.hot())
        cs_ref[step // 2] += added
        return carry

    lax.fori_loop(0, 4, finish_star, 0)
    rho = jnp.zeros((1, LO), F32)
    beta, eta = rho, rho
    for kk in range(2):
        g0s, ds, cs = g0s_ref[kk], ds_ref[kk], cs_ref[kk]
        ys = cs / ds
        ys_ref[kk] = ys
        rho += fold8(g0s * g0s * ds)
        beta += fold8(g0s * cs)
        eta += fold8(cs * ys)
    y = lax.axis_index("y")
    total = jnp.zeros((HI, HALF), F32)
    cross = jnp.zeros((1, LO), F32)
    yf = yf_ref[...]
    for kk in range(2):
        star, flat = Ids(own(obs_ref, y, kk, S), LO), Ids(own(obs_ref, y, kk, PX), LO)
        expo = Ids(own(obs_ref, y, kk, E), HALF, (0, 8))
        w = joined(rows_of(own(obs_ref, y, kk, W)))
        both = gather_both((ys_ref[kk], star.full, star.hot()), (yf, flat.full, flat.hot()))
        from_star, from_flat = row(both, STAR), row(both, FLAT)
        parts = split3(w * (from_star + from_flat))
        (added,) = scatter([[across(part, 0) for part in parts]], expo.bf, expo.hot())
        total += added
        cross += fold_lanes(w * from_star * from_flat)
    ru = ru_ref[...]
    out_ref[0:16] = jnp.concatenate([ru, total], axis=1)
    g0f, df, cf = g0f_ref[...], df_ref[...], cf_ref[...]
    none = jnp.zeros((2, LO), F32)
    rho = 0.25 * (rho + fold8(g0f * g0f * df))
    beta = 0.25 * (beta + fold8(g0f * cf))
    eta = 0.25 * (eta + fold8(cf * yf))
    delta = 2.0 * cross - (0.25 * SMOOTH) * fold8(yf * beside(yf, none, none))
    out_ref[16:24] = jnp.concatenate([rho, beta, eta, delta, jnp.zeros((4, LO), F32)], axis=0)


def edge_kernel(payload_ref, yf_ref, next_ref, out_ref):
    edge = yf_ref[7:8] * next_ref[0:1] + yf_ref[15:16] * next_ref[1:2]
    edge = jnp.where(row_iota((8, LO)) == 3, -(0.5 * SMOOTH) * edge, 0.0)
    scal = payload_ref[16:24] + edge
    for peer in range(NZ):
        out_ref[peer, 0:16] = payload_ref[0:16]
        out_ref[peer, 16:24] = scal


def whole(a):
    return jnp.sum(jnp.sum(a, axis=0, keepdims=True), axis=1, keepdims=True)


def finish_kernel(
    sums_ref, g0z_ref, dz_ref, g0s_ref, ys_ref, g0f_ref, yf_ref, star_out, zero_out, flat_out
):
    y, zh = lax.axis_index("y"), lax.axis_index("zh")
    scal = sums_ref[0, 16:24]
    for peer in range(1, 32):
        scal = scal + sums_ref[peer, 16:24]
    z_rho = jnp.zeros((HI, HALF), F32)
    z_beta, z_eta, z_delta = z_rho, z_rho, z_rho
    z_own = z_rho
    for i in range(4):
        part = sums_ref[i, 0:16]
        for xc in range(1, 8):
            part = part + sums_ref[xc * 4 + i, 0:16]
        cz, qz = part[:, :HALF], part[:, HALF:]
        g0z, dz = g0z_ref[i], dz_ref[i]
        yz = cz / dz
        z_rho += g0z * g0z * dz
        z_beta += g0z * cz
        z_eta += cz * yz
        z_delta += qz * yz
        z_own = jnp.where(i == y, yz, z_own)
    rho0 = whole(z_rho) + whole(scal[0:1])
    beta = whole(z_beta) + whole(scal[1:2])
    eta = whole(z_eta) + whole(scal[2:3])
    delta = 2.0 * whole(z_delta) + whole(scal[3:4])
    curv0 = rho0 + beta
    step0 = rho0 / curv0
    left = beta / curv0
    rho1 = left * left * rho0 - 2.0 * step0 * left * beta + step0 * step0 * eta
    curv_g = (
        left * left * curv0
        - 2.0 * step0 * left * (beta + eta)
        + step0 * step0 * (eta + delta)
    )
    ratio = rho1 / rho0
    mixed = left * curv0 - step0 * (beta + eta)
    curv1 = curv_g + 2.0 * ratio * mixed + ratio * ratio * curv0
    step1 = rho1 / curv1
    along_g = step0 + step1 * (left + ratio)
    along_y = -step1 * step0
    star = along_g * g0s_ref[y // 2] + along_y * ys_ref[y // 2]
    shard = (y % 2) * 2 + zh
    mine = jnp.zeros((4, LO), F32)
    for i in range(4):
        mine = jnp.where(shard == i, star[4 * i : 4 * i + 4], mine)
    star_out[...] = mine
    zero = along_g * g0z_ref[y] + along_y * z_own
    zero_out[...] = jnp.concatenate([zero[0:4], pltpu.roll(zero[0:8], 4, 0)[0:4]], axis=1)
    flat = along_g * g0f_ref[...] + along_y * yf_ref[...]
    flat_out[...] = joined([flat[:8], flat[8:]])


VMEM = pl.BlockSpec(memory_space=pltpu.VMEM)
SMEM = pl.BlockSpec(memory_space=pltpu.SMEM)


HBM = pl.BlockSpec(memory_space=pltpu.HBM)


def call(kernel, shapes, args, specs=None, scratch=(), mib=8, work=20):
    out = [jax.ShapeDtypeStruct(shape, F32) for shape in shapes]
    many = len(out) > 1
    return pl.pallas_call(
        kernel,
        name=kernel.__name__,
        out_shape=tuple(out) if many else out[0],
        in_specs=specs or [VMEM] * len(args),
        out_specs=tuple([VMEM] * len(out)) if many else VMEM,
        scratch_shapes=list(scratch),
        compiler_params=pltpu.CompilerParams(vmem_limit_bytes=mib << 20),
        cost_estimate=pl.CostEstimate(flops=1 << work, bytes_accessed=1 << 20, transcendentals=0),
    )(*args)


def exchange(blocks, axes):
    return lax.all_to_all(blocks, axes, 0, 0, tiled=True)


def to_all(block, peers, axes):
    return exchange(jnp.broadcast_to(block[None], (peers, *block.shape)), axes)


def flat_pairs():
    def place(tile, y, zh):
        x, rest = divmod(tile, NZ * NC)
        zl, c = divmod(rest, NC)
        return (((x * NZ + zl) * NC + c) * NY + y) * NH + zh

    chip, hop, down = [], [], []
    for tile in range(NX * NZ * NC - 1):
        far = (tile + 1) % (NZ * NC) == 0
        for y in range(NY):
            for zh in range(NH):
                here, there = place(tile, y, zh), place(tile + 1, y, 1 - zh if far else zh)
                (hop if tile % 2 else chip).extend([(here, there), (there, here)])
                down.append((there, here))
    return chip, hop, down


def on_device(star_slot, star_block, exposure, superpixel, magnitude, weight):
    zh = lax.axis_index("zh")
    chip, hop, down = flat_pairs()
    stars, flats, expos = (2, HI, LO), (HI, LO), (4, HI, HALF)
    obs = call(
        pack_kernel, [(2, 5, 8, LO)],
        (star_block, star_slot[0], exposure[0], superpixel[0], magnitude[0], weight[0]),
        specs=[SMEM] + [HBM] * 5,
        scratch=[pltpu.VMEM((16, LO), t) for t in (I32, I32, I32, F32, F32)]
        + [pltpu.SemaphoreType.DMA((5,))],
    )
    obs = obs.reshape(80, LO)
    partner = lax.ppermute(obs, "zh", [(0, 1), (1, 0)])
    expo = exchange(call(expo_kernel, [(16, 8, LO)], (obs.reshape(2, 5, 8, LO),)), ("zl", "zh"))
    expo = expo.reshape(NZ, NH, 8, LO).sum(axis=0)
    expo = jnp.where(zh == 0, expo, expo[::-1]).reshape(HI, LO)
    tile_obs = jnp.concatenate([obs, partner, expo], axis=0)
    tile_obs = to_all(lax.optimization_barrier(tile_obs), NY, "y")
    tile_obs = lax.optimization_barrier(tile_obs)
    expo = to_all(tile_obs[:, 160:].reshape(64, LO), 8, COLS)
    g0s, ds, g0f, df, hop_row, chip_row = call(
        sums_kernel, [stars] * 2 + [flats] * 2 + [(2, LO)] * 2, (tile_obs,), mib=16, work=29
    )
    by_hop = lax.ppermute(hop_row, ALL, hop)
    by_chip = lax.ppermute(chip_row, ALL, chip)
    cs, cf, ru = call(
        couple_kernel, [stars, flats, (HI, HALF)], (tile_obs, g0s, g0f),
        scratch=[pltpu.VMEM((4, 8, 4096), F32)], mib=16, work=30,
    )
    fit, cf, yf, g0z, dz, first = call(
        expo_apply_kernel, [(4, 8, 4096)] + [flats] * 2 + [expos] * 2 + [(2, LO)],
        (tile_obs, expo, g0f, cf, df, by_hop, by_chip), mib=16, work=30,
    )
    next_first = lax.ppermute(first, ALL, down)
    ys, payload = call(
        last_kernel, [stars, (24, LO)],
        (tile_obs, fit, g0s, ds, cs, g0f, df, cf, yf, ru),
        scratch=[pltpu.VMEM(stars, F32)], mib=16, work=30,
    )
    payload = call(edge_kernel, [(NZ, 24, LO)], (payload, yf, next_first))
    sums = exchange(payload, "zl").sum(axis=0)
    sums = to_all(sums, 32, PLANE)
    star, zero, flat = call(
        finish_kernel, [(4, LO), (4, LO), (8, 2 * LO)], (sums, g0z, dz, g0s, ys, g0f, yf)
    )
    return star.reshape(-1), zero.reshape(-1), flat


def solution(mesh):
    split = Mesh(mesh.devices.reshape(NX, NZ, NC, NY, NH), ALL)
    tile, loop = ("x", "zl", "c"), ("y", "zh")
    placed = (
        P(tile, loop, None),
        P(tile, loop),
        P(tile, loop, None),
        P(tile, loop, None),
        P(tile, loop, None),
        P(tile, loop, None),
    )
    return jax.shard_map(
        on_device,
        mesh=split,
        in_specs=placed,
        out_specs=(P(ALL), P(loop), P(tile, None)),
        check_vma=False,
    )
```

```python
import jax
import jax.numpy as jnp
from jax import lax
from jax.experimental import pallas as pl
from jax.experimental.pallas import tpu as pltpu
from jax.sharding import Mesh
from jax.sharding import PartitionSpec as P

SMOOTH = 2.0
RIDGE = 0.5
LO, HALF, HI = 128, 64, 16
NX, NZ, NC, NY, NH = 4, 8, 2, 4, 2
ALL = ("x", "zl", "c", "y", "zh")
PLANE = ("x", "c", "y")
COLS = ("x", "c")
F32 = jnp.float32
I32 = jnp.int32
BF16 = jnp.bfloat16
NT = (((1,), (1,)), ((), ()))
NN = (((1,), (0,)), ((), ()))
S, PX, E, W, WM = range(5)
STAR, FLAT = 3, 7


def split3(v):
    first = v.astype(BF16)
    rest = v - first.astype(F32)
    second = rest.astype(BF16)
    return first, second, (rest - second.astype(F32)).astype(BF16)


def row_iota(shape):
    return lax.broadcasted_iota(I32, shape, 0)


def row(x, f):
    return x[f : f + 1]


def rows_of(tiles):
    return [row(tile, i) for tile in tiles for i in range(tile.shape[0])]


def small(ids):
    return ids.astype(F32).astype(BF16)


def joined(tiles):
    return jnp.concatenate(tiles, axis=1)


def is_row(ids, count):
    rows = row_iota((count, LO)).astype(F32).astype(ids[0].dtype)
    return [rows == jnp.broadcast_to(one, (count, LO)) for one in ids]


def onehot(lo, size):
    one, zero = jnp.ones((), BF16), jnp.zeros((), BF16)
    return joined([jnp.where(same, one, zero) for same in is_row(lo, size)])


def scatter(values, hi, hot):
    masks = is_row(hi, HI)
    zero = jnp.zeros((), BF16)
    rows = [
        joined([jnp.where(m, jnp.broadcast_to(p, (HI, LO)), zero) for m, p in zip(masks, part)])
        for value in values
        for part in value
    ]
    sums = lax.dot_general(jnp.concatenate(rows, axis=0), hot, NT, preferred_element_type=F32)
    sums = [sums[at : at + HI] for at in range(0, sums.shape[0], HI)]
    return [sums[i] + sums[i + 1] + sums[i + 2] for i in range(0, len(sums), 3)]


def picked(table, hi, hot):
    parts = jnp.concatenate([part.astype(F32) for part in split3(table)], axis=0).astype(BF16)
    parts = lax.dot_general(parts, hot, NN, preferred_element_type=F32)
    found = parts[:HI] + parts[HI : 2 * HI] + parts[2 * HI :]
    found = jnp.where(joined(is_row(hi, HI)), found, 0.0)
    return found[:8] + found[8:]


def folded(a, *shifts):
    for shift in shifts:
        a = a + pltpu.roll(a, shift, 0)
    return a


def gather(table, hi, hot):
    return folded(picked(table, hi, hot), 4, 2, 1)


def gather_both(first, second):
    a, b = folded(picked(*first), 4), folded(picked(*second), 4)
    return folded(jnp.where((row_iota(a.shape) & 7) < 4, a, b), 2, 1)


def across(x, f):
    return [x[f : f + 1, i : i + LO] for i in range(0, x.shape[1], LO)]


def split_rows(tiles):
    return [rows_of(part) for part in zip(*(split3(tile) for tile in tiles))]


class Ids:
    def __init__(self, tiles, size, offsets=None):
        ids = [tile.astype(I32) for tile in tiles]
        if offsets is None:
            high = [i >> 7 for i in ids]
        else:
            high = [((i >> 6) & 1) * 4 + (i >> 7) + at for i, at in zip(ids, offsets)]
        self.size = size
        self.low_rows = rows_of([small(i & (size - 1)) for i in ids])
        self.bf = rows_of([small(h) for h in high])
        self.full = rows_of([h.astype(F32) for h in high])

    def hot(self):
        return onehot(self.low_rows, self.size)


def copies(refs, held, sems):
    return [pltpu.make_async_copy(ref, to, sems.at[i]) for i, (ref, to) in enumerate(zip(refs, held))]


def pack_kernel(
    block_ref, slot_in, expo_in, pix_in, mag_in, w_in, out_ref, expo_ref, slot, expo, pix, mag, w, sems
):
    moves = copies((slot_in, expo_in, pix_in, mag_in, w_in), (slot, expo, pix, mag, w), sems)
    for move in moves:
        move.start()
    for move in moves:
        move.wait()
    rows = row_iota((8, LO))
    weights, weighted = [], []
    for kk in range(2):
        at = pl.ds(8 * kk, 8)
        base = jnp.zeros((8, LO), I32)
        for i in range(8):
            base = jnp.where(rows == i, block_ref[0, 8 * kk + i] * 256 + (i // 2) * 512, base)
        p = pix[at, :]
        weights.append(w[at, :])
        weighted.append(w[at, :] * mag[at, :])
        fields = (
            (slot[at, :] + base).astype(F32),
            ((((p >> 7) & 1) * 8 + (p >> 8)) * LO + (p & 127)).astype(F32),
            expo[at, :].astype(F32),
            weights[kk],
            weighted[kk],
        )
        for f, tile in enumerate(fields):
            out_ref[40 * kk + 8 * f : 40 * kk + 8 * f + 8] = tile
    ids = Ids([expo[0:8], expo[8:16]], HALF, (0, 0))
    total, count = scatter([split_rows(weighted), split_rows(weights)], ids.bf, ids.hot())
    both = joined([total[:8], count[:8]])
    for peer in range(NZ * NH):
        expo_ref[peer] = both


def field(obs_ref, y, rel, kk, f):
    return obs_ref[y, pl.ds(pl.multiple_of(rel * 80 + kk * 40 + f * 8, 8), 8), :]


def chunk(obs_ref, step, f):
    kk, half = step // 2, step % 2
    return [field(obs_ref, 2 * half + yy, rel, kk, f) for yy in range(2) for rel in range(2)]


def own(obs_ref, y, kk, f):
    return [field(obs_ref, y, rel, kk, f) for rel in range(2)]


def sums_kernel(obs_ref, g0s_ref, ds_ref, g0f_ref, df_ref, hop_ref, chip_ref):
    for ref in (g0s_ref, ds_ref, g0f_ref, df_ref):
        ref[...] = jnp.zeros(ref.shape, F32)

    def sums(step, carry):
        values = [split_rows(chunk(obs_ref, step, f)) for f in (WM, W)]
        ids = Ids(chunk(obs_ref, step, S), LO)
        weighted, count = scatter(values, ids.bf, ids.hot())
        g0s_ref[step // 2] += weighted
        ds_ref[step // 2] += count
        ids = Ids(chunk(obs_ref, step, PX), LO)
        weighted, count = scatter(values, ids.bf, ids.hot())
        g0f_ref[...] += weighted
        df_ref[...] += count
        return carry

    lax.fori_loop(0, 4, sums, 0)
    diag = df_ref[...] + (4.0 * SMOOTH + RIDGE)
    g0f = g0f_ref[...] / diag
    df_ref[...] = diag
    g0f_ref[...] = g0f
    diag = ds_ref[...] + RIDGE
    g0s_ref[...] = g0s_ref[...] / diag
    ds_ref[...] = diag
    odd = lax.axis_index("c") == 1
    top = jnp.concatenate([g0f[0:1], g0f[8:9]], axis=0)
    bot = jnp.concatenate([g0f[7:8], g0f[15:16]], axis=0)
    hop_ref[...] = jnp.where(odd, bot, top)
    chip_ref[...] = jnp.where(odd, top, bot)


def couple_kernel(obs_ref, g0s_ref, g0f_ref, cs_ref, cf_ref, ru_ref, fit_ref):
    cs_ref[...] = jnp.zeros(cs_ref.shape, F32)
    cf_ref[...] = jnp.zeros((HI, LO), F32)

    def couple(step, carry):
        star, flat = Ids(chunk(obs_ref, step, S), LO), Ids(chunk(obs_ref, step, PX), LO)
        hs, hp = star.hot(), flat.hot()
        fit = joined(rows_of(chunk(obs_ref, step, W))) * gather_both(
            (g0s_ref[step // 2], star.full, hs), (g0f_ref[...], flat.full, hp)
        )
        parts = split3(fit)
        (added,) = scatter([[across(part, FLAT) for part in parts]], star.bf, hs)
        cs_ref[step // 2] += added
        (added,) = scatter([[across(part, STAR) for part in parts]], flat.bf, hp)
        cf_ref[...] += added
        fit_ref[step] = fit
        return carry

    lax.fori_loop(0, 4, couple, 0)
    y = lax.axis_index("y")
    total = jnp.zeros((HI, HALF), F32)
    for kk in range(2):
        ids = Ids(own(obs_ref, y, kk, E), HALF, (0, 8))
        at = pl.ds(pl.multiple_of((y % 2) * 2048, 2048), 2048)
        fit = fit_ref[2 * kk + y // 2, :, at]
        parts = split3(row(fit, STAR) + row(fit, FLAT))
        (added,) = scatter([[across(part, 0) for part in parts]], ids.bf, ids.hot())
        total += added
    ru_ref[...] = total


def beside(flat, above, below):
    left, right = flat[:8], flat[8:]
    rows = row_iota((8, LO))
    lanes = lax.broadcasted_iota(I32, (8, LO), 1)
    out = []
    left_up, right_up = pltpu.roll(left, 1, 1), pltpu.roll(right, 1, 1)
    left_down, right_down = pltpu.roll(left, 127, 1), pltpu.roll(right, 127, 1)
    sides = (
        jnp.where(lanes == 0, 0.0, left_up) + jnp.where(lanes == 127, right_down, left_down),
        jnp.where(lanes == 0, left_up, right_up) + jnp.where(lanes == 127, 0.0, right_down),
    )
    for i, half in enumerate((left, right)):
        upper = jnp.where(rows == 0, above[i : i + 1], pltpu.roll(half, 1, 0))
        lower = jnp.where(rows == 7, below[i : i + 1], pltpu.roll(half, 7, 0))
        out.append(sides[i] + upper + lower)
    return jnp.concatenate(out, axis=0)


def expo_apply_kernel(
    obs_ref, expo_ref, g0f_ref, cf_ref, df_ref, hop_ref, chip_ref,
    fit_ref, cf_out, yf_out, g0z_out, dz_out, edge_out,
):
    part = expo_ref[0]
    for xc in range(1, 8):
        part = part + expo_ref[xc]
    for y in range(4):
        diag = part[16 * y : 16 * y + 16, HALF:] + RIDGE
        g0z_out[y] = part[16 * y : 16 * y + 16, :HALF] / diag
        dz_out[y] = diag
    cf_out[...] = cf_ref[...]

    def apply(step, carry):
        expo = Ids(chunk(obs_ref, step, E), HALF, (0, 8, 0, 8))
        hot = expo.hot()
        found = [
            gather(
                g0z_out[2 * (step % 2) + yy],
                expo.full[16 * yy : 16 * yy + 16],
                hot[:, 2048 * yy : 2048 * (yy + 1)],
            )
            for yy in range(2)
        ]
        fit = joined(rows_of(chunk(obs_ref, step, W))) * joined(found)
        fit_ref[step] = fit
        flat = Ids(chunk(obs_ref, step, PX), LO)
        (added,) = scatter([[across(part, 0) for part in split3(fit)]], flat.bf, flat.hot())
        cf_out[...] += added
        return carry

    lax.fori_loop(0, 4, apply, 0)
    odd = lax.axis_index("c") == 1
    above = jnp.where(odd, chip_ref[...], hop_ref[...])
    below = jnp.where(odd, hop_ref[...], chip_ref[...])
    cf = cf_out[...] - SMOOTH * beside(g0f_ref[...], above, below)
    cf_out[...] = cf
    yf = cf / df_ref[...]
    yf_out[...] = yf
    edge_out[...] = jnp.concatenate([yf[0:1], yf[8:9], yf[7:8], yf[15:16]], axis=0)


def fold8(a):
    total = a[0:8]
    for i in range(8, a.shape[0], 8):
        total = total + a[i : i + 8]
    return jnp.sum(total, axis=0, keepdims=True)


def fold_lanes(a):
    total = a[:, 0:LO]
    for i in range(LO, a.shape[1], LO):
        total = total + a[:, i : i + LO]
    return total


def last_kernel(
    obs_ref, fit_ref, g0s_ref, ds_ref, cs_in, g0f_ref, df_ref, cf_ref, yf_ref, ru_ref, ys_ref, out_ref, cs_ref
):
    cs_ref[...] = cs_in[...]

    def finish_star(step, carry):
        star = Ids(chunk(obs_ref, step, S), LO)
        parts = split3(fit_ref[step])
        (added,) = scatter([[across(part, 0) for part in parts]], star.bf, star.hot())
        cs_ref[step // 2] += added
        return carry

    lax.fori_loop(0, 4, finish_star, 0)
    rho = jnp.zeros((1, LO), F32)
    beta, eta = rho, rho
    for kk in range(2):
        g0s, ds, cs = g0s_ref[kk], ds_ref[kk], cs_ref[kk]
        ys = cs / ds
        ys_ref[kk] = ys
        rho += fold8(g0s * g0s * ds)
        beta += fold8(g0s * cs)
        eta += fold8(cs * ys)
    y = lax.axis_index("y")
    total = jnp.zeros((HI, HALF), F32)
    cross = jnp.zeros((1, LO), F32)
    yf = yf_ref[...]
    for kk in range(2):
        star, flat = Ids(own(obs_ref, y, kk, S), LO), Ids(own(obs_ref, y, kk, PX), LO)
        expo = Ids(own(obs_ref, y, kk, E), HALF, (0, 8))
        w = joined(rows_of(own(obs_ref, y, kk, W)))
        both = gather_both((ys_ref[kk], star.full, star.hot()), (yf, flat.full, flat.hot()))
        from_star, from_flat = row(both, STAR), row(both, FLAT)
        parts = split3(w * (from_star + from_flat))
        (added,) = scatter([[across(part, 0) for part in parts]], expo.bf, expo.hot())
        total += added
        cross += fold_lanes(w * from_star * from_flat)
    ru = ru_ref[...]
    out_ref[0:16] = jnp.concatenate([ru, total], axis=1)
    g0f, df, cf = g0f_ref[...], df_ref[...], cf_ref[...]
    none = jnp.zeros((2, LO), F32)
    rho = 0.25 * (rho + fold8(g0f * g0f * df))
    beta = 0.25 * (beta + fold8(g0f * cf))
    eta = 0.25 * (eta + fold8(cf * yf))
    delta = 2.0 * cross - (0.25 * SMOOTH) * fold8(yf * beside(yf, none, none))
    out_ref[16:24] = jnp.concatenate([rho, beta, eta, delta, jnp.zeros((4, LO), F32)], axis=0)


def edge_dot(last, first):
    both = last * first
    return -(0.25 * SMOOTH) * (both[0:1] + both[1:2])


def edge_kernel(payload_ref, mine_ref, other_ref, out_ref):
    odd = lax.axis_index("c") == 1
    mine, other = mine_ref[...], other_ref[...]
    upper, lower = jnp.where(odd, other, mine), jnp.where(odd, mine, other)
    chip = edge_dot(upper[2:4], lower[0:2])
    scal = payload_ref[16:24]
    scal = scal + jnp.where(row_iota((8, LO)) == 3, chip, 0.0)
    scal = jnp.concatenate([scal[0:4], upper[0:2], lower[2:4]], axis=0)
    for peer in range(NZ):
        out_ref[peer, 0:16] = payload_ref[0:16]
        out_ref[peer, 16:24] = scal


def column_kernel(parts_ref, out_ref):
    total = parts_ref[0]
    for peer in range(1, NZ):
        total = total + parts_ref[peer]
    between = edge_dot(parts_ref[0, 22:24], parts_ref[1, 20:22])
    for peer in range(1, NZ - 1):
        between += edge_dot(parts_ref[peer, 22:24], parts_ref[peer + 1, 20:22])
    scal = total[16:20] + jnp.where(row_iota((4, LO)) == 3, between, 0.0)
    ends = jnp.concatenate([scal, parts_ref[0, 20:22], parts_ref[NZ - 1, 22:24]], axis=0)
    for peer in range(NX * NC * NY):
        out_ref[peer, 0:16] = total[0:16]
        out_ref[peer, 16:24] = ends


def whole(a):
    return jnp.sum(jnp.sum(a, axis=0, keepdims=True), axis=1, keepdims=True)


def finish_kernel(
    sums_ref, g0z_ref, dz_ref, g0s_ref, ys_ref, g0f_ref, yf_ref, star_out, zero_out, flat_out
):
    y, zh = lax.axis_index("y"), lax.axis_index("zh")
    scal = sums_ref[0, 16:24]
    for peer in range(1, 32):
        scal = scal + sums_ref[peer, 16:24]
    z_rho = jnp.zeros((HI, HALF), F32)
    z_beta, z_eta, z_delta = z_rho, z_rho, z_rho
    z_own = z_rho
    for i in range(4):
        part = sums_ref[i, 0:16]
        for xc in range(1, 8):
            part = part + sums_ref[xc * 4 + i, 0:16]
        cz, qz = part[:, :HALF], part[:, HALF:]
        g0z, dz = g0z_ref[i], dz_ref[i]
        yz = cz / dz
        z_rho += g0z * g0z * dz
        z_beta += g0z * cz
        z_eta += cz * yz
        z_delta += qz * yz
        z_own = jnp.where(i == y, yz, z_own)
    rho0 = whole(z_rho) + whole(scal[0:1])
    beta = whole(z_beta) + whole(scal[1:2])
    eta = whole(z_eta) + whole(scal[2:3])
    between = jnp.zeros((1, LO), F32)
    for x in range(NX - 1):
        between += 8.0 * edge_dot(sums_ref[8 * x, 22:24], sums_ref[8 * x + 8, 20:22])
    delta = 2.0 * whole(z_delta) + whole(scal[3:4] + between)
    curv0 = rho0 + beta
    step0 = rho0 / curv0
    left = beta / curv0
    rho1 = left * left * rho0 - 2.0 * step0 * left * beta + step0 * step0 * eta
    curv_g = (
        left * left * curv0
        - 2.0 * step0 * left * (beta + eta)
        + step0 * step0 * (eta + delta)
    )
    ratio = rho1 / rho0
    mixed = left * curv0 - step0 * (beta + eta)
    curv1 = curv_g + 2.0 * ratio * mixed + ratio * ratio * curv0
    step1 = rho1 / curv1
    along_g = step0 + step1 * (left + ratio)
    along_y = -step1 * step0
    star = along_g * g0s_ref[y // 2] + along_y * ys_ref[y // 2]
    shard = (y % 2) * 2 + zh
    mine = jnp.zeros((4, LO), F32)
    for i in range(4):
        mine = jnp.where(shard == i, star[4 * i : 4 * i + 4], mine)
    star_out[...] = mine
    zero = along_g * g0z_ref[y] + along_y * z_own
    zero_out[...] = jnp.concatenate([zero[0:4], pltpu.roll(zero[0:8], 4, 0)[0:4]], axis=1)
    flat = along_g * g0f_ref[...] + along_y * yf_ref[...]
    flat_out[...] = joined([flat[:8], flat[8:]])


VMEM = pl.BlockSpec(memory_space=pltpu.VMEM)
SMEM = pl.BlockSpec(memory_space=pltpu.SMEM)


HBM = pl.BlockSpec(memory_space=pltpu.HBM)


def call(kernel, shapes, args, specs=None, scratch=(), mib=8, work=20):
    out = [jax.ShapeDtypeStruct(shape, F32) for shape in shapes]
    many = len(out) > 1
    return pl.pallas_call(
        kernel,
        out_shape=tuple(out) if many else out[0],
        in_specs=specs or [VMEM] * len(args),
        out_specs=tuple([VMEM] * len(out)) if many else VMEM,
        scratch_shapes=list(scratch),
        compiler_params=pltpu.CompilerParams(vmem_limit_bytes=mib << 20 if mib else None),
        cost_estimate=pl.CostEstimate(flops=1 << work, bytes_accessed=1 << 20, transcendentals=0),
    )(*args)


def exchange(blocks, axes):
    return lax.all_to_all(blocks, axes, 0, 0, tiled=True)


def to_all(block, peers, axes):
    return exchange(jnp.broadcast_to(block[None], (peers, *block.shape)), axes)


def flat_pairs():
    def place(tile, y, zh):
        x, rest = divmod(tile, NZ * NC)
        zl, c = divmod(rest, NC)
        return (((x * NZ + zl) * NC + c) * NY + y) * NH + zh

    chip, hop = [], []
    for tile in range(NX * NZ * NC - 1):
        far = (tile + 1) % (NZ * NC) == 0
        for y in range(NY):
            for zh in range(NH):
                here, there = place(tile, y, zh), place(tile + 1, y, 1 - zh if far else zh)
                (hop if tile % 2 else chip).extend([(here, there), (there, here)])
    return chip, hop


def on_device(star_slot, star_block, exposure, superpixel, magnitude, weight):
    zh = lax.axis_index("zh")
    chip, hop = flat_pairs()
    stars, flats, expos = (2, HI, LO), (HI, LO), (4, HI, HALF)
    obs, expo = call(
        pack_kernel, [(80, LO), (16, 8, LO)],
        (star_block, star_slot[0], exposure[0], superpixel[0], magnitude[0], weight[0]),
        specs=[SMEM] + [HBM] * 5,
        scratch=[pltpu.VMEM((16, LO), t) for t in (I32, I32, I32, F32, F32)]
        + [pltpu.SemaphoreType.DMA((5,))],
        mib=None,
    )
    partner = lax.ppermute(obs, "zh", [(0, 1), (1, 0)])
    expo = exchange(expo, ("zl", "zh"))
    expo = expo.reshape(NZ, NH, 8, LO).sum(axis=0)
    expo = jnp.where(zh == 0, expo, expo[::-1]).reshape(HI, LO)
    tile_obs = jnp.concatenate([obs, partner, expo], axis=0)
    tile_obs = to_all(lax.optimization_barrier(tile_obs), NY, "y")
    tile_obs = lax.optimization_barrier(tile_obs)
    expo = to_all(tile_obs[:, 160:].reshape(64, LO), 8, COLS)
    g0s, ds, g0f, df, hop_row, chip_row = call(
        sums_kernel, [stars] * 2 + [flats] * 2 + [(2, LO)] * 2, (tile_obs,), mib=16, work=29
    )
    by_hop = lax.ppermute(hop_row, ALL, hop)
    by_chip = lax.ppermute(chip_row, ALL, chip)
    cs, cf, ru = call(
        couple_kernel, [stars, flats, (HI, HALF)], (tile_obs, g0s, g0f),
        scratch=[pltpu.VMEM((4, 8, 4096), F32)], mib=16, work=30,
    )
    fit, cf, yf, g0z, dz, edges = call(
        expo_apply_kernel, [(4, 8, 4096)] + [flats] * 2 + [expos] * 2 + [(4, LO)],
        (tile_obs, expo, g0f, cf, df, by_hop, by_chip), mib=16, work=30,
    )
    others = lax.ppermute(edges, "c", [(0, 1), (1, 0)])
    ys, payload = call(
        last_kernel, [stars, (24, LO)],
        (tile_obs, fit, g0s, ds, cs, g0f, df, cf, yf, ru),
        scratch=[pltpu.VMEM(stars, F32)], mib=16, work=30,
    )
    payload = exchange(call(edge_kernel, [(NZ, 24, LO)], (payload, edges, others)), "zl")
    sums = exchange(call(column_kernel, [(32, 24, LO)], (payload,)), PLANE)
    star, zero, flat = call(
        finish_kernel, [(4, LO), (4, LO), (8, 2 * LO)], (sums, g0z, dz, g0s, ys, g0f, yf)
    )
    return star.reshape(-1), zero.reshape(-1), flat


def solution(mesh):
    split = Mesh(mesh.devices.reshape(NX, NZ, NC, NY, NH), ALL)
    tile, loop = ("x", "zl", "c"), ("y", "zh")
    placed = (
        P(tile, loop, None),
        P(tile, loop),
        P(tile, loop, None),
        P(tile, loop, None),
        P(tile, loop, None),
        P(tile, loop, None),
    )
    return jax.shard_map(
        on_device,
        mesh=split,
        in_specs=placed,
        out_specs=(P(ALL), P(loop), P(tile, None)),
        check_vma=False,
    )
```

```python
import jax
import jax.numpy as jnp
from jax import lax
from jax.experimental import pallas as pl
from jax.experimental.pallas import tpu as pltpu
from jax.sharding import Mesh
from jax.sharding import PartitionSpec as P

SMOOTH = 2.0
RIDGE = 0.5
LO, HALF, HI = 128, 64, 16
NX, NZ, NC, NY, NH = 4, 8, 2, 4, 2
ALL = ("x", "zl", "c", "y", "zh")
PLANE = ("x", "c", "y")
COLS = ("x", "c")
F32 = jnp.float32
I32 = jnp.int32
BF16 = jnp.bfloat16
NT = (((1,), (1,)), ((), ()))
NN = (((1,), (0,)), ((), ()))
S, PX, E, W, WM = range(5)
EXACT, FEW = 3, 2
STAR, FLAT = 3, 7


def split(v, count):
    parts = []
    for _ in range(count):
        parts.append(v.astype(BF16))
        v = v - parts[-1].astype(F32)
    return parts


def row_iota(shape):
    return lax.broadcasted_iota(I32, shape, 0)


def row(x, f):
    return x[f : f + 1]


def rows_of(tiles):
    return [row(tile, i) for tile in tiles for i in range(tile.shape[0])]


def small(ids):
    return ids.astype(F32).astype(BF16)


def joined(tiles):
    return jnp.concatenate(tiles, axis=1)


def is_row(ids, count):
    rows = row_iota((count, LO)).astype(F32).astype(ids[0].dtype)
    return [rows == jnp.broadcast_to(one, (count, LO)) for one in ids]


def onehot(lo, size):
    one, zero = jnp.ones((), BF16), jnp.zeros((), BF16)
    return joined([jnp.where(same, one, zero) for same in is_row(lo, size)])


def scatter(values, hi, hot):
    masks = is_row(hi, HI)
    zero = jnp.zeros((), BF16)
    rows = [
        joined([jnp.where(m, jnp.broadcast_to(p, (HI, LO)), zero) for m, p in zip(masks, part)])
        for value in values
        for part in value
    ]
    sums = lax.dot_general(jnp.concatenate(rows, axis=0), hot, NT, preferred_element_type=F32)
    sums = [sums[at : at + HI] for at in range(0, sums.shape[0], HI)]
    count = len(values[0])
    return [sum(sums[i + 1 : i + count], sums[i]) for i in range(0, len(sums), count)]


def picked(table, hi, hot):
    parts = lax.dot_general(
        jnp.concatenate(split(table, FEW), axis=0), hot, NN, preferred_element_type=F32
    )
    found = sum((parts[at : at + HI] for at in range(HI, parts.shape[0], HI)), parts[:HI])
    found = jnp.where(joined(is_row(hi, HI)), found, 0.0)
    return found[:8] + found[8:]


def folded(a, *shifts):
    for shift in shifts:
        a = a + pltpu.roll(a, shift, 0)
    return a


def gather(table, hi, hot):
    return folded(picked(table, hi, hot), 4, 2, 1)


def gather_both(first, second):
    a, b = folded(picked(*first), 4), folded(picked(*second), 4)
    return folded(jnp.where((row_iota(a.shape) & 7) < 4, a, b), 2, 1)


def across(x, f):
    return [x[f : f + 1, i : i + LO] for i in range(0, x.shape[1], LO)]


def split_rows(tiles):
    return [rows_of(part) for part in zip(*(split(tile, EXACT) for tile in tiles))]


class Ids:
    def __init__(self, tiles, size, offsets=None):
        ids = [tile.astype(I32) for tile in tiles]
        if offsets is None:
            high = [i >> 7 for i in ids]
        else:
            high = [((i >> 6) & 1) * 4 + (i >> 7) + at for i, at in zip(ids, offsets)]
        self.size = size
        self.low_rows = rows_of([small(i & (size - 1)) for i in ids])
        self.bf = rows_of([small(h) for h in high])
        self.full = rows_of([h.astype(F32) for h in high])

    def hot(self):
        return onehot(self.low_rows, self.size)


def copies(refs, held, sems):
    return [pltpu.make_async_copy(ref, to, sems.at[i]) for i, (ref, to) in enumerate(zip(refs, held))]


def pack_kernel(
    block_ref, slot_in, expo_in, pix_in, mag_in, w_in, out_ref, expo_ref, slot, expo, pix, mag, w, sems
):
    moves = copies((slot_in, expo_in, pix_in, mag_in, w_in), (slot, expo, pix, mag, w), sems)
    for move in moves:
        move.start()
    for move in moves:
        move.wait()
    rows = row_iota((8, LO))
    weights, weighted = [], []
    for kk in range(2):
        at = pl.ds(8 * kk, 8)
        base = jnp.zeros((8, LO), I32)
        for i in range(8):
            base = jnp.where(rows == i, block_ref[0, 8 * kk + i] * 256 + (i // 2) * 512, base)
        p = pix[at, :]
        weights.append(w[at, :])
        weighted.append(w[at, :] * mag[at, :])
        fields = (
            (slot[at, :] + base).astype(F32),
            ((((p >> 7) & 1) * 8 + (p >> 8)) * LO + (p & 127)).astype(F32),
            expo[at, :].astype(F32),
            weights[kk],
            weighted[kk],
        )
        for f, tile in enumerate(fields):
            out_ref[40 * kk + 8 * f : 40 * kk + 8 * f + 8] = tile
    ids = Ids([expo[0:8], expo[8:16]], HALF, (0, 0))
    total, count = scatter([split_rows(weighted), split_rows(weights)], ids.bf, ids.hot())
    both = joined([total[:8], count[:8]])
    for peer in range(NZ * NH):
        expo_ref[peer] = both


def field(obs_ref, y, rel, kk, f):
    return obs_ref[y, pl.ds(pl.multiple_of(rel * 80 + kk * 40 + f * 8, 8), 8), :]


def chunk(obs_ref, step, f):
    kk, half = step // 2, step % 2
    return [field(obs_ref, 2 * half + yy, rel, kk, f) for yy in range(2) for rel in range(2)]


def own(obs_ref, y, kk, f):
    return [field(obs_ref, y, rel, kk, f) for rel in range(2)]


def edge_rows(flat):
    return jnp.concatenate([flat[0:1], flat[8:9], flat[7:8], flat[15:16]], axis=0)


def sums_kernel(obs_ref, g0s_ref, ds_ref, g0f_ref, df_ref, hop_ref, plane_ref):
    for ref in (g0s_ref, ds_ref, g0f_ref, df_ref):
        ref[...] = jnp.zeros(ref.shape, F32)

    def sums(step, carry):
        values = [split_rows(chunk(obs_ref, step, f)) for f in (WM, W)]
        ids = Ids(chunk(obs_ref, step, S), LO)
        weighted, count = scatter(values, ids.bf, ids.hot())
        g0s_ref[step // 2] += weighted
        ds_ref[step // 2] += count
        ids = Ids(chunk(obs_ref, step, PX), LO)
        weighted, count = scatter(values, ids.bf, ids.hot())
        g0f_ref[...] += weighted
        df_ref[...] += count
        return carry

    lax.fori_loop(0, 4, sums, 0)
    diag = df_ref[...] + (4.0 * SMOOTH + RIDGE)
    g0f = g0f_ref[...] / diag
    df_ref[...] = diag
    g0f_ref[...] = g0f
    diag = ds_ref[...] + RIDGE
    g0s_ref[...] = g0s_ref[...] / diag
    ds_ref[...] = diag
    edges = edge_rows(g0f)
    hop_ref[...] = jnp.where(lax.axis_index("c") == 1, edges[2:4], edges[0:2])
    for peer in range(NX * NC):
        for y in range(NY):
            plane_ref[peer, 16 * y : 16 * y + 16] = obs_ref[y, 160:176]
        plane_ref[peer, 64:68] = edges
        plane_ref[peer, 68:72] = jnp.zeros((4, LO), F32)


def couple_kernel(obs_ref, g0s_ref, g0f_ref, cs_ref, cf_ref, ru_ref, fit_ref):
    cs_ref[...] = jnp.zeros(cs_ref.shape, F32)
    cf_ref[...] = jnp.zeros((HI, LO), F32)

    def couple(step, carry):
        star, flat = Ids(chunk(obs_ref, step, S), LO), Ids(chunk(obs_ref, step, PX), LO)
        hs, hp = star.hot(), flat.hot()
        fit = joined(rows_of(chunk(obs_ref, step, W))) * gather_both(
            (g0s_ref[step // 2], star.full, hs), (g0f_ref[...], flat.full, hp)
        )
        parts = split(fit, FEW)
        (added,) = scatter([[across(part, FLAT) for part in parts]], star.bf, hs)
        cs_ref[step // 2] += added
        (added,) = scatter([[across(part, STAR) for part in parts]], flat.bf, hp)
        cf_ref[...] += added
        fit_ref[step] = fit
        return carry

    lax.fori_loop(0, 4, couple, 0)
    y = lax.axis_index("y")
    total = jnp.zeros((HI, HALF), F32)
    for kk in range(2):
        ids = Ids(own(obs_ref, y, kk, E), HALF, (0, 8))
        at = pl.ds(pl.multiple_of((y % 2) * 2048, 2048), 2048)
        fit = fit_ref[2 * kk + y // 2, :, at]
        parts = split(row(fit, STAR) + row(fit, FLAT), FEW)
        (added,) = scatter([[across(part, 0) for part in parts]], ids.bf, ids.hot())
        total += added
    ru_ref[...] = total


def beside(flat, above, below):
    left, right = flat[:8], flat[8:]
    rows = row_iota((8, LO))
    lanes = lax.broadcasted_iota(I32, (8, LO), 1)
    out = []
    left_up, right_up = pltpu.roll(left, 1, 1), pltpu.roll(right, 1, 1)
    left_down, right_down = pltpu.roll(left, 127, 1), pltpu.roll(right, 127, 1)
    sides = (
        jnp.where(lanes == 0, 0.0, left_up) + jnp.where(lanes == 127, right_down, left_down),
        jnp.where(lanes == 0, left_up, right_up) + jnp.where(lanes == 127, 0.0, right_down),
    )
    for i, half in enumerate((left, right)):
        upper = jnp.where(rows == 0, above[i : i + 1], pltpu.roll(half, 1, 0))
        lower = jnp.where(rows == 7, below[i : i + 1], pltpu.roll(half, 7, 0))
        out.append(sides[i] + upper + lower)
    return jnp.concatenate(out, axis=0)


def expo_apply_kernel(
    obs_ref, expo_ref, g0f_ref, cf_ref, df_ref, hop_ref,
    fit_ref, cf_out, yf_out, g0z_out, dz_out,
):
    part = expo_ref[0, 0:64]
    for xc in range(1, 8):
        part = part + expo_ref[xc, 0:64]
    for y in range(4):
        diag = part[16 * y : 16 * y + 16, HALF:] + RIDGE
        g0z_out[y] = part[16 * y : 16 * y + 16, :HALF] / diag
        dz_out[y] = diag
    cf_out[...] = cf_ref[...]

    def apply(step, carry):
        expo = Ids(chunk(obs_ref, step, E), HALF, (0, 8, 0, 8))
        hot = expo.hot()
        found = [
            gather(
                g0z_out[2 * (step % 2) + yy],
                expo.full[16 * yy : 16 * yy + 16],
                hot[:, 2048 * yy : 2048 * (yy + 1)],
            )
            for yy in range(2)
        ]
        fit = joined(rows_of(chunk(obs_ref, step, W))) * joined(found)
        fit_ref[step] = fit
        flat = Ids(chunk(obs_ref, step, PX), LO)
        (added,) = scatter([[across(part, 0) for part in split(fit, FEW)]], flat.bf, flat.hot())
        cf_out[...] += added
        return carry

    lax.fori_loop(0, 4, apply, 0)
    x, c = lax.axis_index("x"), lax.axis_index("c")
    chip = expo_ref[2 * x + 1 - c, 64:68]
    above = jnp.where(c == 1, chip[2:4], hop_ref[...])
    below = jnp.where(c == 1, hop_ref[...], chip[0:2])
    cf = cf_out[...] - SMOOTH * beside(g0f_ref[...], above, below)
    cf_out[...] = cf
    yf = cf / df_ref[...]
    yf_out[...] = yf


def fold8(a):
    total = a[0:8]
    for i in range(8, a.shape[0], 8):
        total = total + a[i : i + 8]
    return jnp.sum(total, axis=0, keepdims=True)


def fold_lanes(a):
    total = a[:, 0:LO]
    for i in range(LO, a.shape[1], LO):
        total = total + a[:, i : i + LO]
    return total


def last_kernel(
    obs_ref, fit_ref, g0s_ref, ds_ref, cs_in, g0f_ref, df_ref, cf_ref, yf_ref, ru_ref, ys_ref, out_ref, cs_ref
):
    cs_ref[...] = cs_in[...]

    def finish_star(step, carry):
        star = Ids(chunk(obs_ref, step, S), LO)
        parts = split(fit_ref[step], FEW)
        (added,) = scatter([[across(part, 0) for part in parts]], star.bf, star.hot())
        cs_ref[step // 2] += added
        return carry

    lax.fori_loop(0, 4, finish_star, 0)
    rho = jnp.zeros((1, LO), F32)
    beta, eta = rho, rho
    for kk in range(2):
        g0s, ds, cs = g0s_ref[kk], ds_ref[kk], cs_ref[kk]
        ys = cs / ds
        ys_ref[kk] = ys
        rho += fold8(g0s * g0s * ds)
        beta += fold8(g0s * cs)
        eta += fold8(cs * ys)
    y = lax.axis_index("y")
    total = jnp.zeros((HI, HALF), F32)
    cross = jnp.zeros((1, LO), F32)
    yf = yf_ref[...]
    for kk in range(2):
        star, flat = Ids(own(obs_ref, y, kk, S), LO), Ids(own(obs_ref, y, kk, PX), LO)
        expo = Ids(own(obs_ref, y, kk, E), HALF, (0, 8))
        w = joined(rows_of(own(obs_ref, y, kk, W)))
        both = gather_both((ys_ref[kk], star.full, star.hot()), (yf, flat.full, flat.hot()))
        from_star, from_flat = row(both, STAR), row(both, FLAT)
        parts = split(w * (from_star + from_flat), FEW)
        (added,) = scatter([[across(part, 0) for part in parts]], expo.bf, expo.hot())
        total += added
        cross += fold_lanes(w * from_star * from_flat)
    expos = joined([ru_ref[...], total])
    g0f, df, cf = g0f_ref[...], df_ref[...], cf_ref[...]
    none = jnp.zeros((2, LO), F32)
    rho = 0.25 * (rho + fold8(g0f * g0f * df))
    beta = 0.25 * (beta + fold8(g0f * cf))
    eta = 0.25 * (eta + fold8(cf * yf))
    delta = 2.0 * cross - (0.25 * SMOOTH) * fold8(yf * beside(yf, none, none))
    scal = jnp.concatenate([rho, beta, eta, delta, edge_rows(yf)], axis=0)
    for zl in range(NZ):
        for c in range(NC):
            out_ref[NC * zl + c, 0:8] = expos[8 * c : 8 * c + 8]
            out_ref[NC * zl + c, 8:16] = scal


def edge_dot(last, first):
    both = last * first
    return -(0.5 * SMOOTH) * (both[0:1] + both[1:2])


def column_kernel(parts_ref, out_ref):
    total = parts_ref[0]
    for peer in range(1, NZ * NC):
        total = total + parts_ref[peer]
    between = edge_dot(parts_ref[0, 14:16], parts_ref[1, 12:14])
    for peer in range(1, NZ * NC - 1):
        between += edge_dot(parts_ref[peer, 14:16], parts_ref[peer + 1, 12:14])
    scal = total[8:12] + jnp.where(row_iota((4, LO)) == 3, between, 0.0)
    ends = jnp.concatenate([scal, parts_ref[0, 12:14], parts_ref[NZ * NC - 1, 14:16]], axis=0)
    for peer in range(NX * NC * NY):
        out_ref[peer, 0:8] = total[0:8]
        out_ref[peer, 8:16] = ends


def whole(a):
    return jnp.sum(jnp.sum(a, axis=0, keepdims=True), axis=1, keepdims=True)


def finish_kernel(
    sums_ref, g0z_ref, dz_ref, g0s_ref, ys_ref, g0f_ref, yf_ref, star_out, zero_out, flat_out
):
    y, zh = lax.axis_index("y"), lax.axis_index("zh")
    scal = jnp.zeros((4, LO), F32)
    for x in range(NX):
        for i in range(NY):
            scal = scal + sums_ref[8 * x + i, 8:12]
    z_rho = jnp.zeros((HI, HALF), F32)
    z_beta, z_eta, z_delta = z_rho, z_rho, z_rho
    z_own = z_rho
    for i in range(4):
        halves = []
        for c in range(NC):
            half = sums_ref[4 * c + i, 0:8]
            for x in range(1, NX):
                half = half + sums_ref[8 * x + 4 * c + i, 0:8]
            halves.append(half)
        part = jnp.concatenate(halves, axis=0)
        cz, qz = part[:, :HALF], part[:, HALF:]
        g0z, dz = g0z_ref[i], dz_ref[i]
        yz = cz / dz
        z_rho += g0z * g0z * dz
        z_beta += g0z * cz
        z_eta += cz * yz
        z_delta += qz * yz
        z_own = jnp.where(i == y, yz, z_own)
    rho0 = whole(z_rho) + whole(scal[0:1])
    beta = whole(z_beta) + whole(scal[1:2])
    eta = whole(z_eta) + whole(scal[2:3])
    between = jnp.zeros((1, LO), F32)
    for x in range(NX - 1):
        between += 4.0 * edge_dot(sums_ref[8 * x, 14:16], sums_ref[8 * x + 8, 12:14])
    delta = 2.0 * whole(z_delta) + whole(scal[3:4] + between)
    curv0 = rho0 + beta
    step0 = rho0 / curv0
    left = beta / curv0
    rho1 = left * left * rho0 - 2.0 * step0 * left * beta + step0 * step0 * eta
    curv_g = (
        left * left * curv0
        - 2.0 * step0 * left * (beta + eta)
        + step0 * step0 * (eta + delta)
    )
    ratio = rho1 / rho0
    mixed = left * curv0 - step0 * (beta + eta)
    curv1 = curv_g + 2.0 * ratio * mixed + ratio * ratio * curv0
    step1 = rho1 / curv1
    along_g = step0 + step1 * (left + ratio)
    along_y = -step1 * step0
    star = along_g * g0s_ref[y // 2] + along_y * ys_ref[y // 2]
    shard = (y % 2) * 2 + zh
    mine = jnp.zeros((4, LO), F32)
    for i in range(4):
        mine = jnp.where(shard == i, star[4 * i : 4 * i + 4], mine)
    star_out[...] = mine
    zero = along_g * g0z_ref[y] + along_y * z_own
    zero_out[...] = jnp.concatenate([zero[0:4], pltpu.roll(zero[0:8], 4, 0)[0:4]], axis=1)
    flat = along_g * g0f_ref[...] + along_y * yf_ref[...]
    flat_out[...] = joined([flat[:8], flat[8:]])


VMEM = pl.BlockSpec(memory_space=pltpu.VMEM)
SMEM = pl.BlockSpec(memory_space=pltpu.SMEM)


HBM = pl.BlockSpec(memory_space=pltpu.HBM)


def call(kernel, shapes, args, specs=None, scratch=(), mib=8, work=20):
    out = [jax.ShapeDtypeStruct(shape, F32) for shape in shapes]
    many = len(out) > 1
    return pl.pallas_call(
        kernel,
        out_shape=tuple(out) if many else out[0],
        in_specs=specs or [VMEM] * len(args),
        out_specs=tuple([VMEM] * len(out)) if many else VMEM,
        scratch_shapes=list(scratch),
        compiler_params=pltpu.CompilerParams(vmem_limit_bytes=mib << 20 if mib else None),
        cost_estimate=pl.CostEstimate(flops=1 << work, bytes_accessed=1 << 20, transcendentals=0),
    )(*args)


def exchange(blocks, axes):
    return lax.all_to_all(blocks, axes, 0, 0, tiled=True)


def to_all(block, peers, axes):
    return exchange(jnp.broadcast_to(block[None], (peers, *block.shape)), axes)


def hop_pairs():
    def place(tile, y, zh):
        x, rest = divmod(tile, NZ * NC)
        zl, c = divmod(rest, NC)
        return (((x * NZ + zl) * NC + c) * NY + y) * NH + zh

    hop = []
    for tile in range(1, NX * NZ * NC - 1, 2):
        far = (tile + 1) % (NZ * NC) == 0
        for y in range(NY):
            for zh in range(NH):
                here, there = place(tile, y, zh), place(tile + 1, y, 1 - zh if far else zh)
                hop.extend([(here, there), (there, here)])
    return hop


def on_device(star_slot, star_block, exposure, superpixel, magnitude, weight):
    zh = lax.axis_index("zh")
    hop = hop_pairs()
    stars, flats, expos = (2, HI, LO), (HI, LO), (4, HI, HALF)
    obs, expo = call(
        pack_kernel, [(80, LO), (16, 8, LO)],
        (star_block, star_slot[0], exposure[0], superpixel[0], magnitude[0], weight[0]),
        specs=[SMEM] + [HBM] * 5,
        scratch=[pltpu.VMEM((16, LO), t) for t in (I32, I32, I32, F32, F32)]
        + [pltpu.SemaphoreType.DMA((5,))],
        mib=None,
    )
    partner = lax.ppermute(obs, "zh", [(0, 1), (1, 0)])
    expo = exchange(expo, ("zl", "zh"))
    expo = expo.reshape(NZ, NH, 8, LO).sum(axis=0)
    expo = jnp.where(zh == 0, expo, expo[::-1]).reshape(HI, LO)
    tile_obs = jnp.concatenate([obs, partner, expo], axis=0)
    tile_obs = to_all(lax.optimization_barrier(tile_obs), NY, "y")
    g0s, ds, g0f, df, hop_row, plane = call(
        sums_kernel, [stars] * 2 + [flats] * 2 + [(2, LO), (8, 72, LO)], (tile_obs,), mib=16, work=29
    )
    expo = exchange(plane, COLS)
    by_hop = lax.ppermute(hop_row, ALL, hop)
    cs, cf, ru = call(
        couple_kernel, [stars, flats, (HI, HALF)], (tile_obs, g0s, g0f),
        scratch=[pltpu.VMEM((4, 8, 4096), F32)], mib=16, work=30,
    )
    fit, cf, yf, g0z, dz = call(
        expo_apply_kernel, [(4, 8, 4096)] + [flats] * 2 + [expos] * 2,
        (tile_obs, expo, g0f, cf, df, by_hop), mib=16, work=30,
    )
    ys, payload = call(
        last_kernel, [stars, (16, 16, LO)],
        (tile_obs, fit, g0s, ds, cs, g0f, df, cf, yf, ru),
        scratch=[pltpu.VMEM(stars, F32)], mib=16, work=30,
    )
    payload = exchange(payload, ("zl", "c"))
    sums = exchange(call(column_kernel, [(32, 16, LO)], (payload,)), PLANE)
    star, zero, flat = call(
        finish_kernel, [(4, LO), (4, LO), (8, 2 * LO)], (sums, g0z, dz, g0s, ys, g0f, yf)
    )
    return star.reshape(-1), zero.reshape(-1), flat


def solution(mesh):
    split = Mesh(mesh.devices.reshape(NX, NZ, NC, NY, NH), ALL)
    tile, loop = ("x", "zl", "c"), ("y", "zh")
    placed = (
        P(tile, loop, None),
        P(tile, loop),
        P(tile, loop, None),
        P(tile, loop, None),
        P(tile, loop, None),
        P(tile, loop, None),
    )
    return jax.shard_map(
        on_device,
        mesh=split,
        in_specs=placed,
        out_specs=(P(ALL), P(loop), P(tile, None)),
        check_vma=False,
    )
```

```python
import jax
import jax.numpy as jnp
from jax import lax
from jax.experimental import pallas as pl
from jax.experimental.pallas import tpu as pltpu
from jax.sharding import Mesh
from jax.sharding import PartitionSpec as P

SMOOTH = 2.0
RIDGE = 0.5
LO, HALF, HI = 128, 64, 16
NX, NZ, NC, NY, NH = 4, 8, 2, 4, 2
ALL = ("x", "zl", "c", "y", "zh")
PLANE = ("x", "c", "y")
F32 = jnp.float32
I32 = jnp.int32
BF16 = jnp.bfloat16
NT = (((1,), (1,)), ((), ()))
NN = (((1,), (0,)), ((), ()))
S, PX, E, W, WM = range(5)
EXACT, FEW = 3, 2
STAR, FLAT = 3, 7


def split(v, count):
    parts = []
    for _ in range(count):
        parts.append(v.astype(BF16))
        v = v - parts[-1].astype(F32)
    return parts


def row_iota(shape):
    return lax.broadcasted_iota(I32, shape, 0)


def row(x, f):
    return x[f : f + 1]


def rows_of(tiles):
    return [row(tile, i) for tile in tiles for i in range(tile.shape[0])]


def small(ids):
    return ids.astype(F32).astype(BF16)


def joined(tiles):
    return jnp.concatenate(tiles, axis=1)


def is_row(ids, count):
    rows = row_iota((count, LO)).astype(F32).astype(ids[0].dtype)
    return [rows == jnp.broadcast_to(one, (count, LO)) for one in ids]


def onehot(lo, size):
    one, zero = jnp.ones((), BF16), jnp.zeros((), BF16)
    return joined([jnp.where(same, one, zero) for same in is_row(lo, size)])


def scatter(values, hi, hot):
    masks = is_row(hi, HI)
    zero = jnp.zeros((), BF16)
    rows = [
        joined([jnp.where(m, jnp.broadcast_to(p, (HI, LO)), zero) for m, p in zip(masks, part)])
        for value in values
        for part in value
    ]
    sums = lax.dot_general(jnp.concatenate(rows, axis=0), hot, NT, preferred_element_type=F32)
    sums = [sums[at : at + HI] for at in range(0, sums.shape[0], HI)]
    count = len(values[0])
    return [sum(sums[i + 1 : i + count], sums[i]) for i in range(0, len(sums), count)]


def picked(table, hi, hot):
    parts = lax.dot_general(
        jnp.concatenate(split(table, FEW), axis=0), hot, NN, preferred_element_type=F32
    )
    found = sum((parts[at : at + HI] for at in range(HI, parts.shape[0], HI)), parts[:HI])
    found = jnp.where(joined(is_row(hi, HI)), found, 0.0)
    return found[:8] + found[8:]


def folded(a, *shifts):
    for shift in shifts:
        a = a + pltpu.roll(a, shift, 0)
    return a


def gather(table, hi, hot):
    return folded(picked(table, hi, hot), 4, 2, 1)


def gather_both(first, second):
    a, b = folded(picked(*first), 4), folded(picked(*second), 4)
    return folded(jnp.where((row_iota(a.shape) & 7) < 4, a, b), 2, 1)


def across(x, f):
    return [x[f : f + 1, i : i + LO] for i in range(0, x.shape[1], LO)]


def split_rows(tiles):
    return [rows_of(part) for part in zip(*(split(tile, EXACT) for tile in tiles))]


class Ids:
    def __init__(self, tiles, size, offsets=None):
        ids = [tile.astype(I32) for tile in tiles]
        if offsets is None:
            high = [i >> 7 for i in ids]
        else:
            high = [((i >> 6) & 1) * 4 + (i >> 7) + at for i, at in zip(ids, offsets)]
        self.size = size
        self.low_rows = rows_of([small(i & (size - 1)) for i in ids])
        self.bf = rows_of([small(h) for h in high])
        self.full = rows_of([h.astype(F32) for h in high])

    def hot(self):
        return onehot(self.low_rows, self.size)


def copies(refs, held, sems):
    return [pltpu.make_async_copy(ref, to, sems.at[i]) for i, (ref, to) in enumerate(zip(refs, held))]


def pack_kernel(
    block_ref, slot_in, expo_in, pix_in, mag_in, w_in, out_ref, expo_ref, slot, expo, pix, mag, w, sems
):
    moves = copies((slot_in, expo_in, pix_in, mag_in, w_in), (slot, expo, pix, mag, w), sems)
    for move in moves:
        move.start()
    for move in moves:
        move.wait()
    rows = row_iota((8, LO))
    weights, weighted = [], []
    for kk in range(2):
        at = pl.ds(8 * kk, 8)
        base = jnp.zeros((8, LO), I32)
        for i in range(8):
            base = jnp.where(rows == i, block_ref[0, 8 * kk + i] * 256 + (i // 2) * 512, base)
        p = pix[at, :]
        weights.append(w[at, :])
        weighted.append(w[at, :] * mag[at, :])
        fields = (
            (slot[at, :] + base).astype(F32),
            ((((p >> 7) & 1) * 8 + (p >> 8)) * LO + (p & 127)).astype(F32),
            expo[at, :].astype(F32),
            weights[kk],
            weighted[kk],
        )
        for f, tile in enumerate(fields):
            out_ref[40 * kk + 8 * f : 40 * kk + 8 * f + 8] = tile
    ids = Ids([expo[0:8], expo[8:16]], HALF, (0, 0))
    total, count = scatter([split_rows(weighted), split_rows(weights)], ids.bf, ids.hot())
    both = joined([total[:8], count[:8]])
    for peer in range(NZ * NH):
        expo_ref[peer] = both


def field(obs_ref, y, rel, kk, f):
    return obs_ref[y, pl.ds(pl.multiple_of(rel * 80 + kk * 40 + f * 8, 8), 8), :]


def chunk(obs_ref, step, f):
    kk, half = step // 2, step % 2
    return [field(obs_ref, 2 * half + yy, rel, kk, f) for yy in range(2) for rel in range(2)]


def own(obs_ref, kk, f):
    return [field(obs_ref, 0, rel, kk, f) for rel in range(2)]


def loop_row(slot):
    return (lax.axis_index("y") + NY - slot) % NY


def edge_rows(flat):
    return jnp.concatenate([flat[0:1], flat[8:9], flat[7:8], flat[15:16]], axis=0)


def sums_kernel(obs_ref, expo_ref, g0s_ref, ds_ref, g0f_ref, df_ref, hop_ref, plane_ref):
    for ref in (g0s_ref, ds_ref, g0f_ref, df_ref):
        ref[...] = jnp.zeros(ref.shape, F32)

    def sums(step, carry):
        values = [split_rows(chunk(obs_ref, step, f)) for f in (WM, W)]
        ids = Ids(chunk(obs_ref, step, S), LO)
        weighted, count = scatter(values, ids.bf, ids.hot())
        g0s_ref[step // 2] += weighted
        ds_ref[step // 2] += count
        ids = Ids(chunk(obs_ref, step, PX), LO)
        weighted, count = scatter(values, ids.bf, ids.hot())
        g0f_ref[...] += weighted
        df_ref[...] += count
        return carry

    lax.fori_loop(0, 4, sums, 0)
    diag = df_ref[...] + (4.0 * SMOOTH + RIDGE)
    g0f = g0f_ref[...] / diag
    df_ref[...] = diag
    g0f_ref[...] = g0f
    diag = ds_ref[...] + RIDGE
    g0s_ref[...] = g0s_ref[...] / diag
    ds_ref[...] = diag
    edges = edge_rows(g0f)
    hop_ref[...] = jnp.where(lax.axis_index("c") == 1, edges[2:4], edges[0:2])
    for peer in range(NX * NC * NY):
        plane_ref[peer, 0:16] = expo_ref[...]
        plane_ref[peer, 16:20] = edges
        plane_ref[peer, 20:24] = jnp.zeros((4, LO), F32)


def couple_kernel(obs_ref, g0s_ref, g0f_ref, cs_ref, cf_ref, ru_ref, fit_ref):
    cs_ref[...] = jnp.zeros(cs_ref.shape, F32)
    cf_ref[...] = jnp.zeros((HI, LO), F32)

    def couple(step, carry):
        star, flat = Ids(chunk(obs_ref, step, S), LO), Ids(chunk(obs_ref, step, PX), LO)
        hs, hp = star.hot(), flat.hot()
        fit = joined(rows_of(chunk(obs_ref, step, W))) * gather_both(
            (g0s_ref[step // 2], star.full, hs), (g0f_ref[...], flat.full, hp)
        )
        parts = split(fit, FEW)
        (added,) = scatter([[across(part, FLAT) for part in parts]], star.bf, hs)
        cs_ref[step // 2] += added
        (added,) = scatter([[across(part, STAR) for part in parts]], flat.bf, hp)
        cf_ref[...] += added
        fit_ref[step] = fit
        return carry

    lax.fori_loop(0, 4, couple, 0)
    total = jnp.zeros((HI, HALF), F32)
    for kk in range(2):
        ids = Ids(own(obs_ref, kk, E), HALF, (0, 8))
        fit = fit_ref[2 * kk, :, 0:2048]
        parts = split(row(fit, STAR) + row(fit, FLAT), FEW)
        (added,) = scatter([[across(part, 0) for part in parts]], ids.bf, ids.hot())
        total += added
    ru_ref[...] = total


def beside(flat, above, below):
    left, right = flat[:8], flat[8:]
    rows = row_iota((8, LO))
    lanes = lax.broadcasted_iota(I32, (8, LO), 1)
    out = []
    left_up, right_up = pltpu.roll(left, 1, 1), pltpu.roll(right, 1, 1)
    left_down, right_down = pltpu.roll(left, 127, 1), pltpu.roll(right, 127, 1)
    sides = (
        jnp.where(lanes == 0, 0.0, left_up) + jnp.where(lanes == 127, right_down, left_down),
        jnp.where(lanes == 0, left_up, right_up) + jnp.where(lanes == 127, 0.0, right_down),
    )
    for i, half in enumerate((left, right)):
        upper = jnp.where(rows == 0, above[i : i + 1], pltpu.roll(half, 1, 0))
        lower = jnp.where(rows == 7, below[i : i + 1], pltpu.roll(half, 7, 0))
        out.append(sides[i] + upper + lower)
    return jnp.concatenate(out, axis=0)


def expo_apply_kernel(
    obs_ref, expo_ref, g0f_ref, cf_ref, df_ref, hop_ref,
    fit_ref, cf_out, yf_out, g0z_out, dz_out,
):
    for y in range(NY):
        part = expo_ref[y, 0:16]
        for xc in range(1, NX * NC):
            part = part + expo_ref[NY * xc + y, 0:16]
        diag = part[:, HALF:] + RIDGE
        g0z_out[y] = part[:, :HALF] / diag
        dz_out[y] = diag
    cf_out[...] = cf_ref[...]

    def apply(step, carry):
        expo = Ids(chunk(obs_ref, step, E), HALF, (0, 8, 0, 8))
        hot = expo.hot()
        found = [
            gather(
                g0z_out[loop_row(2 * (step % 2) + yy)],
                expo.full[16 * yy : 16 * yy + 16],
                hot[:, 2048 * yy : 2048 * (yy + 1)],
            )
            for yy in range(2)
        ]
        fit = joined(rows_of(chunk(obs_ref, step, W))) * joined(found)
        fit_ref[step] = fit
        flat = Ids(chunk(obs_ref, step, PX), LO)
        (added,) = scatter([[across(part, 0) for part in split(fit, FEW)]], flat.bf, flat.hot())
        cf_out[...] += added
        return carry

    lax.fori_loop(0, 4, apply, 0)
    x, c = lax.axis_index("x"), lax.axis_index("c")
    chip = expo_ref[8 * x + 4 * (1 - c) + lax.axis_index("y"), 16:20]
    above = jnp.where(c == 1, chip[2:4], hop_ref[...])
    below = jnp.where(c == 1, hop_ref[...], chip[0:2])
    cf = cf_out[...] - SMOOTH * beside(g0f_ref[...], above, below)
    cf_out[...] = cf
    yf = cf / df_ref[...]
    yf_out[...] = yf


def fold8(a):
    total = a[0:8]
    for i in range(8, a.shape[0], 8):
        total = total + a[i : i + 8]
    return jnp.sum(total, axis=0, keepdims=True)


def fold_lanes(a):
    total = a[:, 0:LO]
    for i in range(LO, a.shape[1], LO):
        total = total + a[:, i : i + LO]
    return total


def last_kernel(
    obs_ref, fit_ref, g0s_ref, ds_ref, cs_in, g0f_ref, df_ref, cf_ref, yf_ref, ru_ref, ys_ref, out_ref, cs_ref
):
    cs_ref[...] = cs_in[...]

    def finish_star(step, carry):
        star = Ids(chunk(obs_ref, step, S), LO)
        parts = split(fit_ref[step], FEW)
        (added,) = scatter([[across(part, 0) for part in parts]], star.bf, star.hot())
        cs_ref[step // 2] += added
        return carry

    lax.fori_loop(0, 4, finish_star, 0)
    rho = jnp.zeros((1, LO), F32)
    beta, eta = rho, rho
    for kk in range(2):
        g0s, ds, cs = g0s_ref[kk], ds_ref[kk], cs_ref[kk]
        ys = cs / ds
        ys_ref[kk] = ys
        rho += fold8(g0s * g0s * ds)
        beta += fold8(g0s * cs)
        eta += fold8(cs * ys)
    total = jnp.zeros((HI, HALF), F32)
    cross = jnp.zeros((1, LO), F32)
    yf = yf_ref[...]
    for kk in range(2):
        star, flat = Ids(own(obs_ref, kk, S), LO), Ids(own(obs_ref, kk, PX), LO)
        expo = Ids(own(obs_ref, kk, E), HALF, (0, 8))
        w = joined(rows_of(own(obs_ref, kk, W)))
        both = gather_both((ys_ref[kk], star.full, star.hot()), (yf, flat.full, flat.hot()))
        from_star, from_flat = row(both, STAR), row(both, FLAT)
        parts = split(w * (from_star + from_flat), FEW)
        (added,) = scatter([[across(part, 0) for part in parts]], expo.bf, expo.hot())
        total += added
        cross += fold_lanes(w * from_star * from_flat)
    expos = joined([ru_ref[...], total])
    g0f, df, cf = g0f_ref[...], df_ref[...], cf_ref[...]
    none = jnp.zeros((2, LO), F32)
    rho = 0.25 * (rho + fold8(g0f * g0f * df))
    beta = 0.25 * (beta + fold8(g0f * cf))
    eta = 0.25 * (eta + fold8(cf * yf))
    delta = 2.0 * cross - (0.25 * SMOOTH) * fold8(yf * beside(yf, none, none))
    scal = jnp.concatenate([rho, beta, eta, delta, edge_rows(yf)], axis=0)
    for zl in range(NZ):
        for c in range(NC):
            out_ref[NC * zl + c, 0:8] = expos[8 * c : 8 * c + 8]
            out_ref[NC * zl + c, 8:16] = scal


def edge_dot(last, first):
    both = last * first
    return -(0.5 * SMOOTH) * (both[0:1] + both[1:2])


def column_kernel(parts_ref, out_ref):
    total = parts_ref[0]
    for peer in range(1, NZ * NC):
        total = total + parts_ref[peer]
    between = edge_dot(parts_ref[0, 14:16], parts_ref[1, 12:14])
    for peer in range(1, NZ * NC - 1):
        between += edge_dot(parts_ref[peer, 14:16], parts_ref[peer + 1, 12:14])
    scal = total[8:12] + jnp.where(row_iota((4, LO)) == 3, between, 0.0)
    ends = jnp.concatenate([scal, parts_ref[0, 12:14], parts_ref[NZ * NC - 1, 14:16]], axis=0)
    for peer in range(NX * NC * NY):
        out_ref[peer, 0:8] = total[0:8]
        out_ref[peer, 8:16] = ends


def whole(a):
    return jnp.sum(jnp.sum(a, axis=0, keepdims=True), axis=1, keepdims=True)


def finish_kernel(
    sums_ref, g0z_ref, dz_ref, g0s_ref, ys_ref, g0f_ref, yf_ref, star_out, zero_out, flat_out
):
    y, zh = lax.axis_index("y"), lax.axis_index("zh")
    scal = jnp.zeros((4, LO), F32)
    for x in range(NX):
        for i in range(NY):
            scal = scal + sums_ref[8 * x + i, 8:12]
    z_rho = jnp.zeros((HI, HALF), F32)
    z_beta, z_eta, z_delta = z_rho, z_rho, z_rho
    z_own = z_rho
    for i in range(4):
        halves = []
        for c in range(NC):
            half = sums_ref[4 * c + i, 0:8]
            for x in range(1, NX):
                half = half + sums_ref[8 * x + 4 * c + i, 0:8]
            halves.append(half)
        part = jnp.concatenate(halves, axis=0)
        cz, qz = part[:, :HALF], part[:, HALF:]
        g0z, dz = g0z_ref[i], dz_ref[i]
        yz = cz / dz
        z_rho += g0z * g0z * dz
        z_beta += g0z * cz
        z_eta += cz * yz
        z_delta += qz * yz
        z_own = jnp.where(i == y, yz, z_own)
    rho0 = whole(z_rho) + whole(scal[0:1])
    beta = whole(z_beta) + whole(scal[1:2])
    eta = whole(z_eta) + whole(scal[2:3])
    between = jnp.zeros((1, LO), F32)
    for x in range(NX - 1):
        between += 4.0 * edge_dot(sums_ref[8 * x, 14:16], sums_ref[8 * x + 8, 12:14])
    delta = 2.0 * whole(z_delta) + whole(scal[3:4] + between)
    curv0 = rho0 + beta
    step0 = rho0 / curv0
    left = beta / curv0
    rho1 = left * left * rho0 - 2.0 * step0 * left * beta + step0 * step0 * eta
    curv_g = (
        left * left * curv0
        - 2.0 * step0 * left * (beta + eta)
        + step0 * step0 * (eta + delta)
    )
    ratio = rho1 / rho0
    mixed = left * curv0 - step0 * (beta + eta)
    curv1 = curv_g + 2.0 * ratio * mixed + ratio * ratio * curv0
    step1 = rho1 / curv1
    along_g = step0 + step1 * (left + ratio)
    along_y = -step1 * step0
    star = along_g * g0s_ref[y // 2] + along_y * ys_ref[y // 2]
    shard = (y % 2) * 2 + zh
    mine = jnp.zeros((4, LO), F32)
    for i in range(4):
        mine = jnp.where(shard == i, star[4 * i : 4 * i + 4], mine)
    star_out[...] = mine
    zero = along_g * g0z_ref[y] + along_y * z_own
    zero_out[...] = jnp.concatenate([zero[0:4], pltpu.roll(zero[0:8], 4, 0)[0:4]], axis=1)
    flat = along_g * g0f_ref[...] + along_y * yf_ref[...]
    flat_out[...] = joined([flat[:8], flat[8:]])


VMEM = pl.BlockSpec(memory_space=pltpu.VMEM)
SMEM = pl.BlockSpec(memory_space=pltpu.SMEM)


HBM = pl.BlockSpec(memory_space=pltpu.HBM)


def call(kernel, shapes, args, specs=None, scratch=(), mib=8, work=20):
    out = [jax.ShapeDtypeStruct(shape, F32) for shape in shapes]
    many = len(out) > 1
    return pl.pallas_call(
        kernel,
        out_shape=tuple(out) if many else out[0],
        in_specs=specs or [VMEM] * len(args),
        out_specs=tuple([VMEM] * len(out)) if many else VMEM,
        scratch_shapes=list(scratch),
        compiler_params=pltpu.CompilerParams(vmem_limit_bytes=mib << 20 if mib else None),
        cost_estimate=pl.CostEstimate(flops=1 << work, bytes_accessed=1 << 20, transcendentals=0),
    )(*args)


def exchange(blocks, axes):
    return lax.all_to_all(blocks, axes, 0, 0, tiled=True)


def hop_pairs():
    def place(tile, y, zh):
        x, rest = divmod(tile, NZ * NC)
        zl, c = divmod(rest, NC)
        return (((x * NZ + zl) * NC + c) * NY + y) * NH + zh

    hop = []
    for tile in range(1, NX * NZ * NC - 1, 2):
        far = (tile + 1) % (NZ * NC) == 0
        for y in range(NY):
            for zh in range(NH):
                here, there = place(tile, y, zh), place(tile + 1, y, 1 - zh if far else zh)
                hop.extend([(here, there), (there, here)])
    return hop


def on_device(star_slot, star_block, exposure, superpixel, magnitude, weight):
    zh = lax.axis_index("zh")
    hop = hop_pairs()
    stars, flats, expos = (2, HI, LO), (HI, LO), (4, HI, HALF)
    obs, expo = call(
        pack_kernel, [(80, LO), (16, 8, LO)],
        (star_block, star_slot[0], exposure[0], superpixel[0], magnitude[0], weight[0]),
        specs=[SMEM] + [HBM] * 5,
        scratch=[pltpu.VMEM((16, LO), t) for t in (I32, I32, I32, F32, F32)]
        + [pltpu.SemaphoreType.DMA((5,))],
        mib=None,
    )
    partner = lax.ppermute(obs, "zh", [(0, 1), (1, 0)])
    expo = exchange(expo, ("zl", "zh"))
    both = jnp.concatenate([obs, partner], axis=0)
    turned = [lax.ppermute(both, "y", [(i, (i + k) % NY) for i in range(NY)]) for k in range(1, NY)]
    tile_obs = jnp.stack([both, *turned])
    expo = expo.reshape(NZ, NH, 8, LO).sum(axis=0)
    expo = jnp.where(zh == 0, expo, expo[::-1]).reshape(HI, LO)
    g0s, ds, g0f, df, hop_row, plane = call(
        sums_kernel, [stars] * 2 + [flats] * 2 + [(2, LO), (32, 24, LO)], (tile_obs, expo), mib=16, work=29
    )
    expo = exchange(plane, PLANE)
    by_hop = lax.ppermute(hop_row, ALL, hop)
    cs, cf, ru = call(
        couple_kernel, [stars, flats, (HI, HALF)], (tile_obs, g0s, g0f),
        scratch=[pltpu.VMEM((4, 8, 4096), F32)], mib=16, work=30,
    )
    fit, cf, yf, g0z, dz = call(
        expo_apply_kernel, [(4, 8, 4096)] + [flats] * 2 + [expos] * 2,
        (tile_obs, expo, g0f, cf, df, by_hop), mib=16, work=30,
    )
    ys, payload = call(
        last_kernel, [stars, (16, 16, LO)],
        (tile_obs, fit, g0s, ds, cs, g0f, df, cf, yf, ru),
        scratch=[pltpu.VMEM(stars, F32)], mib=16, work=30,
    )
    payload = exchange(payload, ("zl", "c"))
    sums = exchange(call(column_kernel, [(32, 16, LO)], (payload,)), PLANE)
    star, zero, flat = call(
        finish_kernel, [(4, LO), (4, LO), (8, 2 * LO)], (sums, g0z, dz, g0s, ys, g0f, yf)
    )
    return star.reshape(-1), zero.reshape(-1), flat


def solution(mesh):
    split = Mesh(mesh.devices.reshape(NX, NZ, NC, NY, NH), ALL)
    tile, loop = ("x", "zl", "c"), ("y", "zh")
    placed = (
        P(tile, loop, None),
        P(tile, loop),
        P(tile, loop, None),
        P(tile, loop, None),
        P(tile, loop, None),
        P(tile, loop, None),
    )
    return jax.shard_map(
        on_device,
        mesh=split,
        in_specs=placed,
        out_specs=(P(ALL), P(loop), P(tile, None)),
        check_vma=False,
    )
```

```python
import jax
import jax.numpy as jnp
from jax import lax
from jax.experimental import pallas as pl
from jax.experimental.pallas import tpu as pltpu
from jax.sharding import Mesh
from jax.sharding import PartitionSpec as P

SMOOTH = 2.0
RIDGE = 0.5
LO, HALF, HI = 128, 64, 16
NX, NZ, NC, NY, NH = 4, 8, 2, 4, 2
ALL = ("x", "zl", "c", "y", "zh")
PLANE = ("x", "c", "y")
F32 = jnp.float32
I32 = jnp.int32
BF16 = jnp.bfloat16
NT = (((1,), (1,)), ((), ()))
NN = (((1,), (0,)), ((), ()))
S, PX, E, W, WM = range(5)
EXACT, FEW = 3, 2
STAR, FLAT = 3, 7


def split(v, count):
    parts = []
    for _ in range(count):
        parts.append(v.astype(BF16))
        v = v - parts[-1].astype(F32)
    return parts


def row_iota(shape):
    return lax.broadcasted_iota(I32, shape, 0)


def row(x, f):
    return x[f : f + 1]


def rows_of(tiles):
    return [row(tile, i) for tile in tiles for i in range(tile.shape[0])]


def small(ids):
    return ids.astype(F32).astype(BF16)


def joined(tiles):
    return jnp.concatenate(tiles, axis=1)


def is_row(ids, count):
    rows = row_iota((count, LO)).astype(F32).astype(ids[0].dtype)
    return [rows == jnp.broadcast_to(one, (count, LO)) for one in ids]


def onehot(lo, size):
    one, zero = jnp.ones((), BF16), jnp.zeros((), BF16)
    return joined([jnp.where(same, one, zero) for same in is_row(lo, size)])


def scatter(values, hi, hot):
    masks = is_row(hi, HI)
    zero = jnp.zeros((), BF16)
    rows = [
        joined([jnp.where(m, jnp.broadcast_to(p, (HI, LO)), zero) for m, p in zip(masks, part)])
        for value in values
        for part in value
    ]
    sums = lax.dot_general(jnp.concatenate(rows, axis=0), hot, NT, preferred_element_type=F32)
    sums = [sums[at : at + HI] for at in range(0, sums.shape[0], HI)]
    count = len(values[0])
    return [sum(sums[i + 1 : i + count], sums[i]) for i in range(0, len(sums), count)]


def picked(table, hi, hot):
    parts = lax.dot_general(
        jnp.concatenate(split(table, FEW), axis=0), hot, NN, preferred_element_type=F32
    )
    found = sum((parts[at : at + HI] for at in range(HI, parts.shape[0], HI)), parts[:HI])
    found = jnp.where(joined(is_row(hi, HI)), found, 0.0)
    return found[:8] + found[8:]


def folded(a, *shifts):
    for shift in shifts:
        a = a + pltpu.roll(a, shift, 0)
    return a


def gather(table, hi, hot):
    return folded(picked(table, hi, hot), 4, 2, 1)


def gather_both(first, second):
    a, b = folded(picked(*first), 4), folded(picked(*second), 4)
    return folded(jnp.where((row_iota(a.shape) & 7) < 4, a, b), 2, 1)


def across(x, f):
    return [x[f : f + 1, i : i + LO] for i in range(0, x.shape[1], LO)]


def split_rows(tiles):
    return [rows_of(part) for part in zip(*(split(tile, EXACT) for tile in tiles))]


class Ids:
    def __init__(self, tiles, size, offsets=None):
        ids = [tile.astype(I32) for tile in tiles]
        if offsets is None:
            high = [i >> 7 for i in ids]
        else:
            high = [((i >> 6) & 1) * 4 + (i >> 7) + at for i, at in zip(ids, offsets)]
        self.size = size
        self.low_rows = rows_of([small(i & (size - 1)) for i in ids])
        self.bf = rows_of([small(h) for h in high])
        self.full = rows_of([h.astype(F32) for h in high])

    def hot(self):
        return onehot(self.low_rows, self.size)


def copies(refs, held, sems):
    return [pltpu.make_async_copy(ref, to, sems.at[i]) for i, (ref, to) in enumerate(zip(refs, held))]


def pack_kernel(
    block_ref, slot_in, expo_in, pix_in, mag_in, w_in, out_ref, expo_ref, slot, expo, pix, mag, w, sems
):
    moves = copies((slot_in, expo_in, pix_in, mag_in, w_in), (slot, expo, pix, mag, w), sems)
    for move in moves:
        move.start()
    for move in moves:
        move.wait()
    rows = row_iota((8, LO))
    weights, weighted = [], []
    for kk in range(2):
        at = pl.ds(8 * kk, 8)
        base = jnp.zeros((8, LO), I32)
        for i in range(8):
            base = jnp.where(rows == i, block_ref[0, 8 * kk + i] * 256 + (i // 2) * 512, base)
        p = pix[at, :]
        weights.append(w[at, :])
        weighted.append(w[at, :] * mag[at, :])
        fields = (
            (slot[at, :] + base).astype(F32),
            ((((p >> 7) & 1) * 8 + (p >> 8)) * LO + (p & 127)).astype(F32),
            expo[at, :].astype(F32),
            weights[kk],
            weighted[kk],
        )
        for f, tile in enumerate(fields):
            out_ref[40 * kk + 8 * f : 40 * kk + 8 * f + 8] = tile
    ids = Ids([expo[0:8], expo[8:16]], HALF, (0, 0))
    total, count = scatter([split_rows(weighted), split_rows(weights)], ids.bf, ids.hot())
    both = joined([total[:8], count[:8]])
    for peer in range(NZ * NH):
        expo_ref[peer] = both


def field(obs_ref, y, rel, kk, f):
    return obs_ref[y, pl.ds(pl.multiple_of(rel * 80 + kk * 40 + f * 8, 8), 8), :]


def chunk(obs_ref, step, f):
    kk, half = step // 2, step % 2
    return [field(obs_ref, 2 * half + yy, rel, kk, f) for yy in range(2) for rel in range(2)]


def own(obs_ref, kk, f):
    return [field(obs_ref, 0, rel, kk, f) for rel in range(2)]


def loop_row(slot):
    return (lax.axis_index("y") + NY - slot) % NY


def edge_rows(flat):
    return jnp.concatenate([flat[0:1], flat[8:9], flat[7:8], flat[15:16]], axis=0)


def sums_kernel(obs_ref, expo_ref, g0s_ref, ds_ref, g0f_ref, df_ref, hop_ref, plane_ref):
    for ref in (g0s_ref, ds_ref, g0f_ref, df_ref):
        ref[...] = jnp.zeros(ref.shape, F32)

    def sums(step, carry):
        values = [split_rows(chunk(obs_ref, step, f)) for f in (WM, W)]
        ids = Ids(chunk(obs_ref, step, S), LO)
        weighted, count = scatter(values, ids.bf, ids.hot())
        g0s_ref[step // 2] += weighted
        ds_ref[step // 2] += count
        ids = Ids(chunk(obs_ref, step, PX), LO)
        weighted, count = scatter(values, ids.bf, ids.hot())
        g0f_ref[...] += weighted
        df_ref[...] += count
        return carry

    lax.fori_loop(0, 4, sums, 0)
    diag = df_ref[...] + (4.0 * SMOOTH + RIDGE)
    g0f = g0f_ref[...] / diag
    df_ref[...] = diag
    g0f_ref[...] = g0f
    diag = ds_ref[...] + RIDGE
    g0s_ref[...] = g0s_ref[...] / diag
    ds_ref[...] = diag
    edges = edge_rows(g0f)
    hop_ref[...] = jnp.where(lax.axis_index("c") == 1, edges[2:4], edges[0:2])
    for peer in range(NX * NC * NY):
        plane_ref[peer, 0:16] = expo_ref[...]
        plane_ref[peer, 16:20] = edges
        plane_ref[peer, 20:24] = jnp.zeros((4, LO), F32)


def couple_kernel(obs_ref, g0s_ref, g0f_ref, cs_ref, cf_ref, ru_ref, fit_ref):
    cs_ref[...] = jnp.zeros(cs_ref.shape, F32)
    cf_ref[...] = jnp.zeros((HI, LO), F32)

    def couple(step, carry):
        star, flat = Ids(chunk(obs_ref, step, S), LO), Ids(chunk(obs_ref, step, PX), LO)
        hs, hp = star.hot(), flat.hot()
        fit = joined(rows_of(chunk(obs_ref, step, W))) * gather_both(
            (g0s_ref[step // 2], star.full, hs), (g0f_ref[...], flat.full, hp)
        )
        parts = split(fit, FEW)
        (added,) = scatter([[across(part, FLAT) for part in parts]], star.bf, hs)
        cs_ref[step // 2] += added
        (added,) = scatter([[across(part, STAR) for part in parts]], flat.bf, hp)
        cf_ref[...] += added
        fit_ref[step] = fit
        return carry

    lax.fori_loop(0, 4, couple, 0)
    total = jnp.zeros((HI, HALF), F32)
    for kk in range(2):
        ids = Ids(own(obs_ref, kk, E), HALF, (0, 8))
        fit = fit_ref[2 * kk, :, 0:2048]
        parts = split(row(fit, STAR) + row(fit, FLAT), FEW)
        (added,) = scatter([[across(part, 0) for part in parts]], ids.bf, ids.hot())
        total += added
    ru_ref[...] = total


def beside(flat, above, below):
    left, right = flat[:8], flat[8:]
    rows = row_iota((8, LO))
    lanes = lax.broadcasted_iota(I32, (8, LO), 1)
    out = []
    left_up, right_up = pltpu.roll(left, 1, 1), pltpu.roll(right, 1, 1)
    left_down, right_down = pltpu.roll(left, 127, 1), pltpu.roll(right, 127, 1)
    sides = (
        jnp.where(lanes == 0, 0.0, left_up) + jnp.where(lanes == 127, right_down, left_down),
        jnp.where(lanes == 0, left_up, right_up) + jnp.where(lanes == 127, 0.0, right_down),
    )
    for i, half in enumerate((left, right)):
        upper = jnp.where(rows == 0, above[i : i + 1], pltpu.roll(half, 1, 0))
        lower = jnp.where(rows == 7, below[i : i + 1], pltpu.roll(half, 7, 0))
        out.append(sides[i] + upper + lower)
    return jnp.concatenate(out, axis=0)


def expo_apply_kernel(
    obs_ref, expo_ref, g0f_ref, cf_ref, df_ref, hop_ref,
    fit_ref, cf_out, yf_out, g0z_out, dz_out,
):
    for y in range(NY):
        part = expo_ref[y, 0:16]
        for xc in range(1, NX * NC):
            part = part + expo_ref[NY * xc + y, 0:16]
        diag = part[:, HALF:] + RIDGE
        g0z_out[y] = part[:, :HALF] / diag
        dz_out[y] = diag
    cf_out[...] = cf_ref[...]

    def apply(step, carry):
        expo = Ids(chunk(obs_ref, step, E), HALF, (0, 8, 0, 8))
        hot = expo.hot()
        found = [
            gather(
                g0z_out[loop_row(2 * (step % 2) + yy)],
                expo.full[16 * yy : 16 * yy + 16],
                hot[:, 2048 * yy : 2048 * (yy + 1)],
            )
            for yy in range(2)
        ]
        fit = joined(rows_of(chunk(obs_ref, step, W))) * joined(found)
        fit_ref[step] = fit
        flat = Ids(chunk(obs_ref, step, PX), LO)
        (added,) = scatter([[across(part, 0) for part in split(fit, FEW)]], flat.bf, flat.hot())
        cf_out[...] += added
        return carry

    lax.fori_loop(0, 4, apply, 0)
    x, c = lax.axis_index("x"), lax.axis_index("c")
    chip = expo_ref[8 * x + 4 * (1 - c) + lax.axis_index("y"), 16:20]
    above = jnp.where(c == 1, chip[2:4], hop_ref[...])
    below = jnp.where(c == 1, hop_ref[...], chip[0:2])
    cf = cf_out[...] - SMOOTH * beside(g0f_ref[...], above, below)
    cf_out[...] = cf
    yf = cf / df_ref[...]
    yf_out[...] = yf


def fold8(a):
    total = a[0:8]
    for i in range(8, a.shape[0], 8):
        total = total + a[i : i + 8]
    return jnp.sum(total, axis=0, keepdims=True)


def fold_lanes(a):
    total = a[:, 0:LO]
    for i in range(LO, a.shape[1], LO):
        total = total + a[:, i : i + LO]
    return total


def last_kernel(
    obs_ref, fit_ref, g0s_ref, ds_ref, cs_in, g0f_ref, df_ref, cf_ref, yf_ref, ru_ref, ys_ref, keep_ref, send_ref, cs_ref
):
    cs_ref[...] = cs_in[...]

    def finish_star(step, carry):
        star = Ids(chunk(obs_ref, step, S), LO)
        parts = split(fit_ref[step], FEW)
        (added,) = scatter([[across(part, 0) for part in parts]], star.bf, star.hot())
        cs_ref[step // 2] += added
        return carry

    lax.fori_loop(0, 4, finish_star, 0)
    rho = jnp.zeros((1, LO), F32)
    beta, eta = rho, rho
    for kk in range(2):
        g0s, ds, cs = g0s_ref[kk], ds_ref[kk], cs_ref[kk]
        ys = cs / ds
        ys_ref[kk] = ys
        rho += fold8(g0s * g0s * ds)
        beta += fold8(g0s * cs)
        eta += fold8(cs * ys)
    total = jnp.zeros((HI, HALF), F32)
    cross = jnp.zeros((1, LO), F32)
    yf = yf_ref[...]
    for kk in range(2):
        star, flat = Ids(own(obs_ref, kk, S), LO), Ids(own(obs_ref, kk, PX), LO)
        expo = Ids(own(obs_ref, kk, E), HALF, (0, 8))
        w = joined(rows_of(own(obs_ref, kk, W)))
        both = gather_both((ys_ref[kk], star.full, star.hot()), (yf, flat.full, flat.hot()))
        from_star, from_flat = row(both, STAR), row(both, FLAT)
        parts = split(w * (from_star + from_flat), FEW)
        (added,) = scatter([[across(part, 0) for part in parts]], expo.bf, expo.hot())
        total += added
        cross += fold_lanes(w * from_star * from_flat)
    expos = joined([ru_ref[...], total])
    g0f, df, cf = g0f_ref[...], df_ref[...], cf_ref[...]
    none = jnp.zeros((2, LO), F32)
    rho = 0.25 * (rho + fold8(g0f * g0f * df))
    beta = 0.25 * (beta + fold8(g0f * cf))
    eta = 0.25 * (eta + fold8(cf * yf))
    delta = 2.0 * cross - (0.25 * SMOOTH) * fold8(yf * beside(yf, none, none))
    scal = jnp.concatenate([rho, beta, eta, delta, edge_rows(yf)], axis=0)
    odd = lax.axis_index("c") == 1
    keep_ref[0:8] = jnp.where(odd, expos[8:16], expos[0:8])
    send_ref[0:8] = jnp.where(odd, expos[0:8], expos[8:16])
    keep_ref[8:16] = scal
    send_ref[8:16] = scal


def edge_dot(last, first):
    both = last * first
    return -(0.5 * SMOOTH) * (both[0:1] + both[1:2])


def chip_kernel(keep_ref, got_ref, out_ref):
    odd = lax.axis_index("c") == 1
    keep, got = keep_ref[...], got_ref[...]
    upper, lower = jnp.where(odd, got, keep), jnp.where(odd, keep, got)
    scal = keep[8:12] + got[8:12]
    scal = scal + jnp.where(row_iota((4, LO)) == 3, edge_dot(upper[14:16], lower[12:14]), 0.0)
    scal = jnp.concatenate([scal, upper[12:14], lower[14:16]], axis=0)
    for peer in range(NZ):
        out_ref[peer, 0:8] = keep[0:8] + got[0:8]
        out_ref[peer, 8:16] = scal


def column_kernel(parts_ref, out_ref):
    total = parts_ref[0]
    for peer in range(1, NZ):
        total = total + parts_ref[peer]
    between = edge_dot(parts_ref[0, 14:16], parts_ref[1, 12:14])
    for peer in range(1, NZ - 1):
        between += edge_dot(parts_ref[peer, 14:16], parts_ref[peer + 1, 12:14])
    scal = total[8:12] + jnp.where(row_iota((4, LO)) == 3, between, 0.0)
    ends = jnp.concatenate([scal, parts_ref[0, 12:14], parts_ref[NZ - 1, 14:16]], axis=0)
    for peer in range(NX * NC * NY):
        out_ref[peer, 0:8] = total[0:8]
        out_ref[peer, 8:16] = ends


def whole(a):
    return jnp.sum(jnp.sum(a, axis=0, keepdims=True), axis=1, keepdims=True)


def finish_kernel(
    sums_ref, g0z_ref, dz_ref, g0s_ref, ys_ref, g0f_ref, yf_ref, star_out, zero_out, flat_out
):
    y, zh = lax.axis_index("y"), lax.axis_index("zh")
    scal = jnp.zeros((4, LO), F32)
    for x in range(NX):
        for i in range(NY):
            scal = scal + sums_ref[8 * x + i, 8:12]
    z_rho = jnp.zeros((HI, HALF), F32)
    z_beta, z_eta, z_delta = z_rho, z_rho, z_rho
    z_own = z_rho
    for i in range(4):
        halves = []
        for c in range(NC):
            half = sums_ref[4 * c + i, 0:8]
            for x in range(1, NX):
                half = half + sums_ref[8 * x + 4 * c + i, 0:8]
            halves.append(half)
        part = jnp.concatenate(halves, axis=0)
        cz, qz = part[:, :HALF], part[:, HALF:]
        g0z, dz = g0z_ref[i], dz_ref[i]
        yz = cz / dz
        z_rho += g0z * g0z * dz
        z_beta += g0z * cz
        z_eta += cz * yz
        z_delta += qz * yz
        z_own = jnp.where(i == y, yz, z_own)
    rho0 = whole(z_rho) + whole(scal[0:1])
    beta = whole(z_beta) + whole(scal[1:2])
    eta = whole(z_eta) + whole(scal[2:3])
    between = jnp.zeros((1, LO), F32)
    for x in range(NX - 1):
        between += 4.0 * edge_dot(sums_ref[8 * x, 14:16], sums_ref[8 * x + 8, 12:14])
    delta = 2.0 * whole(z_delta) + whole(scal[3:4] + between)
    curv0 = rho0 + beta
    step0 = rho0 / curv0
    left = beta / curv0
    rho1 = left * left * rho0 - 2.0 * step0 * left * beta + step0 * step0 * eta
    curv_g = (
        left * left * curv0
        - 2.0 * step0 * left * (beta + eta)
        + step0 * step0 * (eta + delta)
    )
    ratio = rho1 / rho0
    mixed = left * curv0 - step0 * (beta + eta)
    curv1 = curv_g + 2.0 * ratio * mixed + ratio * ratio * curv0
    step1 = rho1 / curv1
    along_g = step0 + step1 * (left + ratio)
    along_y = -step1 * step0
    star = along_g * g0s_ref[y // 2] + along_y * ys_ref[y // 2]
    shard = (y % 2) * 2 + zh
    mine = jnp.zeros((4, LO), F32)
    for i in range(4):
        mine = jnp.where(shard == i, star[4 * i : 4 * i + 4], mine)
    star_out[...] = mine
    zero = along_g * g0z_ref[y] + along_y * z_own
    zero_out[...] = jnp.concatenate([zero[0:4], pltpu.roll(zero[0:8], 4, 0)[0:4]], axis=1)
    flat = along_g * g0f_ref[...] + along_y * yf_ref[...]
    flat_out[...] = joined([flat[:8], flat[8:]])


VMEM = pl.BlockSpec(memory_space=pltpu.VMEM)
SMEM = pl.BlockSpec(memory_space=pltpu.SMEM)


HBM = pl.BlockSpec(memory_space=pltpu.HBM)


def call(kernel, shapes, args, specs=None, scratch=(), mib=8, work=20):
    out = [jax.ShapeDtypeStruct(shape, F32) for shape in shapes]
    many = len(out) > 1
    return pl.pallas_call(
        kernel,
        out_shape=tuple(out) if many else out[0],
        in_specs=specs or [VMEM] * len(args),
        out_specs=tuple([VMEM] * len(out)) if many else VMEM,
        scratch_shapes=list(scratch),
        compiler_params=pltpu.CompilerParams(vmem_limit_bytes=mib << 20 if mib else None),
        cost_estimate=pl.CostEstimate(flops=1 << work, bytes_accessed=1 << 20, transcendentals=0),
    )(*args)


def exchange(blocks, axes):
    return lax.all_to_all(blocks, axes, 0, 0, tiled=True)


def hop_pairs():
    def place(tile, y, zh):
        x, rest = divmod(tile, NZ * NC)
        zl, c = divmod(rest, NC)
        return (((x * NZ + zl) * NC + c) * NY + y) * NH + zh

    hop = []
    for tile in range(1, NX * NZ * NC - 1, 2):
        far = (tile + 1) % (NZ * NC) == 0
        for y in range(NY):
            for zh in range(NH):
                here, there = place(tile, y, zh), place(tile + 1, y, 1 - zh if far else zh)
                hop.extend([(here, there), (there, here)])
    return hop


def on_device(star_slot, star_block, exposure, superpixel, magnitude, weight):
    zh = lax.axis_index("zh")
    hop = hop_pairs()
    stars, flats, expos = (2, HI, LO), (HI, LO), (4, HI, HALF)
    obs, expo = call(
        pack_kernel, [(80, LO), (16, 8, LO)],
        (star_block, star_slot[0], exposure[0], superpixel[0], magnitude[0], weight[0]),
        specs=[SMEM] + [HBM] * 5,
        scratch=[pltpu.VMEM((16, LO), t) for t in (I32, I32, I32, F32, F32)]
        + [pltpu.SemaphoreType.DMA((5,))],
        mib=None,
    )
    partner = lax.ppermute(obs, "zh", [(0, 1), (1, 0)])
    expo = exchange(expo, ("zl", "zh"))
    both = jnp.concatenate([obs, partner], axis=0)
    turned = [lax.ppermute(both, "y", [(i, (i + k) % NY) for i in range(NY)]) for k in range(1, NY)]
    tile_obs = jnp.stack([both, *turned])
    expo = expo.reshape(NZ, NH, 8, LO).sum(axis=0)
    expo = jnp.where(zh == 0, expo, expo[::-1]).reshape(HI, LO)
    g0s, ds, g0f, df, hop_row, plane = call(
        sums_kernel, [stars] * 2 + [flats] * 2 + [(2, LO), (32, 24, LO)], (tile_obs, expo), mib=16, work=29
    )
    expo = exchange(plane, PLANE)
    by_hop = lax.ppermute(hop_row, ALL, hop)
    cs, cf, ru = call(
        couple_kernel, [stars, flats, (HI, HALF)], (tile_obs, g0s, g0f),
        scratch=[pltpu.VMEM((4, 8, 4096), F32)], mib=16, work=30,
    )
    fit, cf, yf, g0z, dz = call(
        expo_apply_kernel, [(4, 8, 4096)] + [flats] * 2 + [expos] * 2,
        (tile_obs, expo, g0f, cf, df, by_hop), mib=16, work=30,
    )
    ys, keep, send = call(
        last_kernel, [stars, (16, LO), (16, LO)],
        (tile_obs, fit, g0s, ds, cs, g0f, df, cf, yf, ru),
        scratch=[pltpu.VMEM(stars, F32)], mib=16, work=30,
    )
    got = lax.ppermute(send, "c", [(0, 1), (1, 0)])
    payload = exchange(call(chip_kernel, [(NZ, 16, LO)], (keep, got)), "zl")
    sums = exchange(call(column_kernel, [(32, 16, LO)], (payload,)), PLANE)
    star, zero, flat = call(
        finish_kernel, [(4, LO), (4, LO), (8, 2 * LO)], (sums, g0z, dz, g0s, ys, g0f, yf)
    )
    return star.reshape(-1), zero.reshape(-1), flat


def solution(mesh):
    split = Mesh(mesh.devices.reshape(NX, NZ, NC, NY, NH), ALL)
    tile, loop = ("x", "zl", "c"), ("y", "zh")
    placed = (
        P(tile, loop, None),
        P(tile, loop),
        P(tile, loop, None),
        P(tile, loop, None),
        P(tile, loop, None),
        P(tile, loop, None),
    )
    return jax.shard_map(
        on_device,
        mesh=split,
        in_specs=placed,
        out_specs=(P(ALL), P(loop), P(tile, None)),
        check_vma=False,
    )
```

```python
import jax
import jax.numpy as jnp
from jax import lax
from jax.experimental import pallas as pl
from jax.experimental.pallas import tpu as pltpu
from jax.sharding import Mesh
from jax.sharding import PartitionSpec as P

SMOOTH = 2.0
RIDGE = 0.5
LO, HALF, HI = 128, 64, 16
NX, NZ, NC, NY, NH = 4, 8, 2, 4, 2
ALL = ("x", "zl", "c", "y", "zh")
PLANE = ("x", "c", "y")
COLS = ("x", "c")
F32 = jnp.float32
I32 = jnp.int32
BF16 = jnp.bfloat16
NT = (((1,), (1,)), ((), ()))
NN = (((1,), (0,)), ((), ()))
S, PX, E, W, WM = range(5)
EXACT, FEW = 3, 2
STAR, FLAT = 3, 7


def split(v, count):
    parts = []
    for _ in range(count):
        parts.append(v.astype(BF16))
        v = v - parts[-1].astype(F32)
    return parts


def row_iota(shape):
    return lax.broadcasted_iota(I32, shape, 0)


def row(x, f):
    return x[f : f + 1]


def rows_of(tiles):
    return [row(tile, i) for tile in tiles for i in range(tile.shape[0])]


def small(ids):
    return ids.astype(F32).astype(BF16)


def joined(tiles):
    return jnp.concatenate(tiles, axis=1)


def is_row(ids, count):
    rows = row_iota((count, LO)).astype(F32).astype(ids[0].dtype)
    return [rows == jnp.broadcast_to(one, (count, LO)) for one in ids]


def onehot(lo, size):
    one, zero = jnp.ones((), BF16), jnp.zeros((), BF16)
    return joined([jnp.where(same, one, zero) for same in is_row(lo, size)])


def scatter(values, hi, hot):
    masks = is_row(hi, HI)
    zero = jnp.zeros((), BF16)
    rows = [
        joined([jnp.where(m, jnp.broadcast_to(p, (HI, LO)), zero) for m, p in zip(masks, part)])
        for value in values
        for part in value
    ]
    sums = lax.dot_general(jnp.concatenate(rows, axis=0), hot, NT, preferred_element_type=F32)
    sums = [sums[at : at + HI] for at in range(0, sums.shape[0], HI)]
    count = len(values[0])
    return [sum(sums[i + 1 : i + count], sums[i]) for i in range(0, len(sums), count)]


def picked(table, hi, hot):
    parts = lax.dot_general(
        jnp.concatenate(split(table, FEW), axis=0), hot, NN, preferred_element_type=F32
    )
    found = sum((parts[at : at + HI] for at in range(HI, parts.shape[0], HI)), parts[:HI])
    found = jnp.where(joined(is_row(hi, HI)), found, 0.0)
    return found[:8] + found[8:]


def folded(a, *shifts):
    for shift in shifts:
        a = a + pltpu.roll(a, shift, 0)
    return a


def gather(table, hi, hot):
    return folded(picked(table, hi, hot), 4, 2, 1)


def gather_both(first, second):
    a, b = folded(picked(*first), 4), folded(picked(*second), 4)
    return folded(jnp.where((row_iota(a.shape) & 7) < 4, a, b), 2, 1)


def across(x, f):
    return [x[f : f + 1, i : i + LO] for i in range(0, x.shape[1], LO)]


def split_rows(tiles):
    return [rows_of(part) for part in zip(*(split(tile, EXACT) for tile in tiles))]


class Ids:
    def __init__(self, tiles, size, offsets=None):
        ids = [tile.astype(I32) for tile in tiles]
        if offsets is None:
            high = [i >> 7 for i in ids]
        else:
            high = [((i >> 6) & 1) * 4 + (i >> 7) + at for i, at in zip(ids, offsets)]
        self.size = size
        self.low_rows = rows_of([small(i & (size - 1)) for i in ids])
        self.bf = rows_of([small(h) for h in high])
        self.full = rows_of([h.astype(F32) for h in high])

    def hot(self):
        return onehot(self.low_rows, self.size)


def copies(refs, held, sems):
    return [pltpu.make_async_copy(ref, to, sems.at[i]) for i, (ref, to) in enumerate(zip(refs, held))]


def pack_kernel(
    block_ref, slot_in, expo_in, pix_in, mag_in, w_in, out_ref, expo_ref, slot, expo, pix, mag, w, sems
):
    moves = copies((slot_in, expo_in, pix_in, mag_in, w_in), (slot, expo, pix, mag, w), sems)
    for move in moves:
        move.start()
    for move in moves:
        move.wait()
    rows = row_iota((8, LO))
    weights, weighted = [], []
    for kk in range(2):
        at = pl.ds(8 * kk, 8)
        base = jnp.zeros((8, LO), I32)
        for i in range(8):
            base = jnp.where(rows == i, block_ref[0, 8 * kk + i] * 256 + (i // 2) * 512, base)
        p = pix[at, :]
        weights.append(w[at, :])
        weighted.append(w[at, :] * mag[at, :])
        fields = (
            (slot[at, :] + base).astype(F32),
            ((((p >> 7) & 1) * 8 + (p >> 8)) * LO + (p & 127)).astype(F32),
            expo[at, :].astype(F32),
            weights[kk],
            weighted[kk],
        )
        for f, tile in enumerate(fields):
            out_ref[40 * kk + 8 * f : 40 * kk + 8 * f + 8] = tile
    ids = Ids([expo[0:8], expo[8:16]], HALF, (0, 0))
    total, count = scatter([split_rows(weighted), split_rows(weights)], ids.bf, ids.hot())
    both = joined([total[:8], count[:8]])
    for peer in range(NZ * NH):
        expo_ref[peer] = both


def field(obs_ref, y, rel, kk, f):
    return obs_ref[y, pl.ds(pl.multiple_of(rel * 80 + kk * 40 + f * 8, 8), 8), :]


def chunk(obs_ref, step, f):
    kk, half = step // 2, step % 2
    return [field(obs_ref, 2 * half + yy, rel, kk, f) for yy in range(2) for rel in range(2)]


def own(obs_ref, y, kk, f):
    return [field(obs_ref, y, rel, kk, f) for rel in range(2)]


def edge_rows(flat):
    return jnp.concatenate([flat[0:1], flat[8:9], flat[7:8], flat[15:16]], axis=0)


def sums_kernel(obs_ref, g0s_ref, ds_ref, g0f_ref, df_ref, hop_ref, plane_ref):
    for ref in (g0s_ref, ds_ref, g0f_ref, df_ref):
        ref[...] = jnp.zeros(ref.shape, F32)

    def sums(step, carry):
        values = [split_rows(chunk(obs_ref, step, f)) for f in (WM, W)]
        ids = Ids(chunk(obs_ref, step, S), LO)
        weighted, count = scatter(values, ids.bf, ids.hot())
        g0s_ref[step // 2] += weighted
        ds_ref[step // 2] += count
        ids = Ids(chunk(obs_ref, step, PX), LO)
        weighted, count = scatter(values, ids.bf, ids.hot())
        g0f_ref[...] += weighted
        df_ref[...] += count
        return carry

    lax.fori_loop(0, 4, sums, 0)
    diag = df_ref[...] + (4.0 * SMOOTH + RIDGE)
    g0f = g0f_ref[...] / diag
    df_ref[...] = diag
    g0f_ref[...] = g0f
    diag = ds_ref[...] + RIDGE
    g0s_ref[...] = g0s_ref[...] / diag
    ds_ref[...] = diag
    edges = edge_rows(g0f)
    hop_ref[...] = jnp.where(lax.axis_index("c") == 1, edges[2:4], edges[0:2])
    for peer in range(NX * NC):
        for y in range(NY):
            plane_ref[peer, 16 * y : 16 * y + 16] = obs_ref[y, 160:176]
        plane_ref[peer, 64:68] = edges
        plane_ref[peer, 68:72] = jnp.zeros((4, LO), F32)


def couple_kernel(obs_ref, g0s_ref, g0f_ref, cs_ref, cf_ref, ru_ref, fit_ref):
    cs_ref[...] = jnp.zeros(cs_ref.shape, F32)
    cf_ref[...] = jnp.zeros((HI, LO), F32)

    def couple(step, carry):
        star, flat = Ids(chunk(obs_ref, step, S), LO), Ids(chunk(obs_ref, step, PX), LO)
        hs, hp = star.hot(), flat.hot()
        fit = joined(rows_of(chunk(obs_ref, step, W))) * gather_both(
            (g0s_ref[step // 2], star.full, hs), (g0f_ref[...], flat.full, hp)
        )
        parts = split(fit, FEW)
        (added,) = scatter([[across(part, FLAT) for part in parts]], star.bf, hs)
        cs_ref[step // 2] += added
        (added,) = scatter([[across(part, STAR) for part in parts]], flat.bf, hp)
        cf_ref[...] += added
        fit_ref[step] = fit
        return carry

    lax.fori_loop(0, 4, couple, 0)
    y = lax.axis_index("y")
    total = jnp.zeros((HI, HALF), F32)
    for kk in range(2):
        ids = Ids(own(obs_ref, y, kk, E), HALF, (0, 8))
        at = pl.ds(pl.multiple_of((y % 2) * 2048, 2048), 2048)
        fit = fit_ref[2 * kk + y // 2, :, at]
        parts = split(row(fit, STAR) + row(fit, FLAT), FEW)
        (added,) = scatter([[across(part, 0) for part in parts]], ids.bf, ids.hot())
        total += added
    ru_ref[...] = total


def beside(flat, above, below):
    left, right = flat[:8], flat[8:]
    rows = row_iota((8, LO))
    lanes = lax.broadcasted_iota(I32, (8, LO), 1)
    out = []
    left_up, right_up = pltpu.roll(left, 1, 1), pltpu.roll(right, 1, 1)
    left_down, right_down = pltpu.roll(left, 127, 1), pltpu.roll(right, 127, 1)
    sides = (
        jnp.where(lanes == 0, 0.0, left_up) + jnp.where(lanes == 127, right_down, left_down),
        jnp.where(lanes == 0, left_up, right_up) + jnp.where(lanes == 127, 0.0, right_down),
    )
    for i, half in enumerate((left, right)):
        upper = jnp.where(rows == 0, above[i : i + 1], pltpu.roll(half, 1, 0))
        lower = jnp.where(rows == 7, below[i : i + 1], pltpu.roll(half, 7, 0))
        out.append(sides[i] + upper + lower)
    return jnp.concatenate(out, axis=0)


def fold8(a):
    total = a[0:8]
    for i in range(8, a.shape[0], 8):
        total = total + a[i : i + 8]
    return jnp.sum(total, axis=0, keepdims=True)


def fold_lanes(a):
    total = a[:, 0:LO]
    for i in range(LO, a.shape[1], LO):
        total = total + a[:, i : i + LO]
    return total


def apply_kernel(
    obs_ref, expo_ref, g0s_ref, ds_ref, cs_in, g0f_ref, cf_in, df_ref, ru_ref, hop_ref,
    ys_ref, yf_ref, g0z_ref, dz_ref, out_ref, cs_ref, cf_ref,
):
    part = expo_ref[0, 0:64]
    for xc in range(1, 8):
        part = part + expo_ref[xc, 0:64]
    for y in range(4):
        diag = part[16 * y : 16 * y + 16, HALF:] + RIDGE
        g0z_ref[y] = part[16 * y : 16 * y + 16, :HALF] / diag
        dz_ref[y] = diag
    cs_ref[...] = cs_in[...]
    cf_ref[...] = cf_in[...]

    def apply(step, carry):
        expo = Ids(chunk(obs_ref, step, E), HALF, (0, 8, 0, 8))
        hot = expo.hot()
        found = [
            gather(
                g0z_ref[2 * (step % 2) + yy],
                expo.full[16 * yy : 16 * yy + 16],
                hot[:, 2048 * yy : 2048 * (yy + 1)],
            )
            for yy in range(2)
        ]
        fit = joined(rows_of(chunk(obs_ref, step, W))) * joined(found)
        values = [[across(part, 0) for part in split(fit, FEW)]]
        flat = Ids(chunk(obs_ref, step, PX), LO)
        (added,) = scatter(values, flat.bf, flat.hot())
        cf_ref[...] += added
        star = Ids(chunk(obs_ref, step, S), LO)
        (added,) = scatter(values, star.bf, star.hot())
        cs_ref[step // 2] += added
        return carry

    lax.fori_loop(0, 4, apply, 0)
    x, c, y = lax.axis_index("x"), lax.axis_index("c"), lax.axis_index("y")
    chip = expo_ref[2 * x + 1 - c, 64:68]
    above = jnp.where(c == 1, chip[2:4], hop_ref[...])
    below = jnp.where(c == 1, hop_ref[...], chip[0:2])
    g0f, df = g0f_ref[...], df_ref[...]
    cf = cf_ref[...] - SMOOTH * beside(g0f, above, below)
    yf = cf / df
    yf_ref[...] = yf
    rho, beta, eta = fold8(g0f * g0f * df), fold8(g0f * cf), fold8(cf * yf)
    for kk in range(2):
        g0s, ds, cs = g0s_ref[kk], ds_ref[kk], cs_ref[kk]
        ys = cs / ds
        ys_ref[kk] = ys
        rho += fold8(g0s * g0s * ds)
        beta += fold8(g0s * cs)
        eta += fold8(cs * ys)
    total = jnp.zeros((HI, HALF), F32)
    cross = jnp.zeros((1, LO), F32)
    for kk in range(2):
        star, flat = Ids(own(obs_ref, y, kk, S), LO), Ids(own(obs_ref, y, kk, PX), LO)
        expo = Ids(own(obs_ref, y, kk, E), HALF, (0, 8))
        w = joined(rows_of(own(obs_ref, y, kk, W)))
        both = gather_both((ys_ref[kk], star.full, star.hot()), (yf, flat.full, flat.hot()))
        from_star, from_flat = row(both, STAR), row(both, FLAT)
        parts = split(w * (from_star + from_flat), FEW)
        (added,) = scatter([[across(part, 0) for part in parts]], expo.bf, expo.hot())
        total += added
        cross += fold_lanes(w * from_star * from_flat)
    expos = joined([ru_ref[...], total])
    none = jnp.zeros((2, LO), F32)
    delta = 2.0 * cross - (0.25 * SMOOTH) * fold8(yf * beside(yf, none, none))
    scal = jnp.concatenate(
        [0.25 * rho, 0.25 * beta, 0.25 * eta, delta, edge_rows(yf)], axis=0
    )
    for zl in range(NZ):
        for half in range(NC):
            out_ref[NC * zl + half, 0:8] = expos[8 * half : 8 * half + 8]
            out_ref[NC * zl + half, 8:16] = scal


def edge_dot(last, first):
    both = last * first
    return -(0.5 * SMOOTH) * (both[0:1] + both[1:2])


def column_kernel(parts_ref, out_ref):
    total = parts_ref[0]
    for peer in range(1, NZ * NC):
        total = total + parts_ref[peer]
    between = edge_dot(parts_ref[0, 14:16], parts_ref[1, 12:14])
    for peer in range(1, NZ * NC - 1):
        between += edge_dot(parts_ref[peer, 14:16], parts_ref[peer + 1, 12:14])
    scal = total[8:12] + jnp.where(row_iota((4, LO)) == 3, between, 0.0)
    ends = jnp.concatenate([scal, parts_ref[0, 12:14], parts_ref[NZ * NC - 1, 14:16]], axis=0)
    for peer in range(NX * NC * NY):
        out_ref[peer, 0:8] = total[0:8]
        out_ref[peer, 8:16] = ends


def whole(a):
    return jnp.sum(jnp.sum(a, axis=0, keepdims=True), axis=1, keepdims=True)


def finish_kernel(
    sums_ref, g0z_ref, dz_ref, g0s_ref, ys_ref, g0f_ref, yf_ref, star_out, zero_out, flat_out
):
    y, zh = lax.axis_index("y"), lax.axis_index("zh")
    scal = jnp.zeros((4, LO), F32)
    for x in range(NX):
        for i in range(NY):
            scal = scal + sums_ref[8 * x + i, 8:12]
    z_rho = jnp.zeros((HI, HALF), F32)
    z_beta, z_eta, z_delta = z_rho, z_rho, z_rho
    z_own = z_rho
    for i in range(4):
        halves = []
        for c in range(NC):
            half = sums_ref[4 * c + i, 0:8]
            for x in range(1, NX):
                half = half + sums_ref[8 * x + 4 * c + i, 0:8]
            halves.append(half)
        part = jnp.concatenate(halves, axis=0)
        cz, qz = part[:, :HALF], part[:, HALF:]
        g0z, dz = g0z_ref[i], dz_ref[i]
        yz = cz / dz
        z_rho += g0z * g0z * dz
        z_beta += g0z * cz
        z_eta += cz * yz
        z_delta += qz * yz
        z_own = jnp.where(i == y, yz, z_own)
    rho0 = whole(z_rho) + whole(scal[0:1])
    beta = whole(z_beta) + whole(scal[1:2])
    eta = whole(z_eta) + whole(scal[2:3])
    between = jnp.zeros((1, LO), F32)
    for x in range(NX - 1):
        between += 4.0 * edge_dot(sums_ref[8 * x, 14:16], sums_ref[8 * x + 8, 12:14])
    delta = 2.0 * whole(z_delta) + whole(scal[3:4] + between)
    curv0 = rho0 + beta
    step0 = rho0 / curv0
    left = beta / curv0
    rho1 = left * left * rho0 - 2.0 * step0 * left * beta + step0 * step0 * eta
    curv_g = (
        left * left * curv0
        - 2.0 * step0 * left * (beta + eta)
        + step0 * step0 * (eta + delta)
    )
    ratio = rho1 / rho0
    mixed = left * curv0 - step0 * (beta + eta)
    curv1 = curv_g + 2.0 * ratio * mixed + ratio * ratio * curv0
    step1 = rho1 / curv1
    along_g = step0 + step1 * (left + ratio)
    along_y = -step1 * step0
    star = along_g * g0s_ref[y // 2] + along_y * ys_ref[y // 2]
    shard = (y % 2) * 2 + zh
    mine = jnp.zeros((4, LO), F32)
    for i in range(4):
        mine = jnp.where(shard == i, star[4 * i : 4 * i + 4], mine)
    star_out[...] = mine
    zero = along_g * g0z_ref[y] + along_y * z_own
    zero_out[...] = jnp.concatenate([zero[0:4], pltpu.roll(zero[0:8], 4, 0)[0:4]], axis=1)
    flat = along_g * g0f_ref[...] + along_y * yf_ref[...]
    flat_out[...] = joined([flat[:8], flat[8:]])


VMEM = pl.BlockSpec(memory_space=pltpu.VMEM)
SMEM = pl.BlockSpec(memory_space=pltpu.SMEM)


HBM = pl.BlockSpec(memory_space=pltpu.HBM)


def call(kernel, shapes, args, specs=None, scratch=(), mib=8, work=20):
    out = [jax.ShapeDtypeStruct(shape, F32) for shape in shapes]
    many = len(out) > 1
    return pl.pallas_call(
        kernel,
        out_shape=tuple(out) if many else out[0],
        in_specs=specs or [VMEM] * len(args),
        out_specs=tuple([VMEM] * len(out)) if many else VMEM,
        scratch_shapes=list(scratch),
        compiler_params=pltpu.CompilerParams(vmem_limit_bytes=mib << 20 if mib else None),
        cost_estimate=pl.CostEstimate(flops=1 << work, bytes_accessed=1 << 20, transcendentals=0),
    )(*args)


def exchange(blocks, axes):
    return lax.all_to_all(blocks, axes, 0, 0, tiled=True)


def to_all(block, peers, axes):
    return exchange(jnp.broadcast_to(block[None], (peers, *block.shape)), axes)


def hop_pairs():
    def place(tile, y, zh):
        x, rest = divmod(tile, NZ * NC)
        zl, c = divmod(rest, NC)
        return (((x * NZ + zl) * NC + c) * NY + y) * NH + zh

    hop = []
    for tile in range(1, NX * NZ * NC - 1, 2):
        far = (tile + 1) % (NZ * NC) == 0
        for y in range(NY):
            for zh in range(NH):
                here, there = place(tile, y, zh), place(tile + 1, y, 1 - zh if far else zh)
                hop.extend([(here, there), (there, here)])
    return hop


def on_device(star_slot, star_block, exposure, superpixel, magnitude, weight):
    zh = lax.axis_index("zh")
    hop = hop_pairs()
    stars, flats, expos = (2, HI, LO), (HI, LO), (4, HI, HALF)
    obs, expo = call(
        pack_kernel, [(80, LO), (16, 8, LO)],
        (star_block, star_slot[0], exposure[0], superpixel[0], magnitude[0], weight[0]),
        specs=[SMEM] + [HBM] * 5,
        scratch=[pltpu.VMEM((16, LO), t) for t in (I32, I32, I32, F32, F32)]
        + [pltpu.SemaphoreType.DMA((5,))],
        mib=None,
    )
    partner = lax.ppermute(obs, "zh", [(0, 1), (1, 0)])
    expo = exchange(expo, ("zl", "zh"))
    expo = expo.reshape(NZ, NH, 8, LO).sum(axis=0)
    expo = jnp.where(zh == 0, expo, expo[::-1]).reshape(HI, LO)
    both = lax.optimization_barrier(jnp.concatenate([obs, partner], axis=0))
    tile_obs = jnp.concatenate([both, expo], axis=0)
    tile_obs = to_all(lax.optimization_barrier(tile_obs), NY, "y")
    g0s, ds, g0f, df, hop_row, plane = call(
        sums_kernel, [stars] * 2 + [flats] * 2 + [(2, LO), (8, 72, LO)], (tile_obs,), mib=16, work=29
    )
    expo = exchange(plane, COLS)
    by_hop = lax.ppermute(hop_row, ALL, hop)
    cs, cf, ru = call(
        couple_kernel, [stars, flats, (HI, HALF)], (tile_obs, g0s, g0f),
        scratch=[pltpu.VMEM((4, 8, 4096), F32)], mib=16, work=30,
    )
    ys, yf, g0z, dz, payload = call(
        apply_kernel, [stars, flats] + [expos] * 2 + [(16, 16, LO)],
        (tile_obs, expo, g0s, ds, cs, g0f, cf, df, ru, by_hop),
        scratch=[pltpu.VMEM(stars, F32), pltpu.VMEM(flats, F32)], mib=16, work=30,
    )
    payload = exchange(payload, ("zl", "c"))
    sums = exchange(call(column_kernel, [(32, 16, LO)], (payload,)), PLANE)
    star, zero, flat = call(
        finish_kernel, [(4, LO), (4, LO), (8, 2 * LO)], (sums, g0z, dz, g0s, ys, g0f, yf)
    )
    return star.reshape(-1), zero.reshape(-1), flat


def solution(mesh):
    split = Mesh(mesh.devices.reshape(NX, NZ, NC, NY, NH), ALL)
    tile, loop = ("x", "zl", "c"), ("y", "zh")
    placed = (
        P(tile, loop, None),
        P(tile, loop),
        P(tile, loop, None),
        P(tile, loop, None),
        P(tile, loop, None),
        P(tile, loop, None),
    )
    return jax.shard_map(
        on_device,
        mesh=split,
        in_specs=placed,
        out_specs=(P(ALL), P(loop), P(tile, None)),
        check_vma=False,
    )
```

```python
import jax
import jax.numpy as jnp
from jax import lax
from jax.experimental import pallas as pl
from jax.experimental.pallas import tpu as pltpu
from jax.sharding import Mesh
from jax.sharding import PartitionSpec as P

SMOOTH = 2.0
RIDGE = 0.5
LO, HALF, HI = 128, 64, 16
NX, NZ, NC, NY, NH = 4, 8, 2, 4, 2
ALL = ("x", "zl", "c", "y", "zh")
PLANE = ("x", "c", "y")
COLS = ("x", "c")
F32 = jnp.float32
I32 = jnp.int32
BF16 = jnp.bfloat16
NT = (((1,), (1,)), ((), ()))
NN = (((1,), (0,)), ((), ()))
S, PX, E, W, WM = range(5)
EXACT, FEW = 3, 2
STAR, FLAT = 3, 7


def split(v, count):
    parts = []
    for _ in range(count):
        parts.append(v.astype(BF16))
        v = v - parts[-1].astype(F32)
    return parts


def row_iota(shape):
    return lax.broadcasted_iota(I32, shape, 0)


def row(x, f):
    return x[f : f + 1]


def rows_of(tiles):
    return [row(tile, i) for tile in tiles for i in range(tile.shape[0])]


def small(ids):
    return ids.astype(F32).astype(BF16)


def joined(tiles):
    return jnp.concatenate(tiles, axis=1)


def is_row(ids, count):
    rows = row_iota((count, LO)).astype(F32).astype(ids[0].dtype)
    return [rows == jnp.broadcast_to(one, (count, LO)) for one in ids]


def onehot(lo, size):
    one, zero = jnp.ones((), BF16), jnp.zeros((), BF16)
    return joined([jnp.where(same, one, zero) for same in is_row(lo, size)])


def scatter(values, hi, hot):
    masks = is_row(hi, HI)
    zero = jnp.zeros((), BF16)
    rows = [
        joined([jnp.where(m, jnp.broadcast_to(p, (HI, LO)), zero) for m, p in zip(masks, part)])
        for value in values
        for part in value
    ]
    sums = lax.dot_general(jnp.concatenate(rows, axis=0), hot, NT, preferred_element_type=F32)
    sums = [sums[at : at + HI] for at in range(0, sums.shape[0], HI)]
    count = len(values[0])
    return [sum(sums[i + 1 : i + count], sums[i]) for i in range(0, len(sums), count)]


def picked(table, hi, hot):
    parts = lax.dot_general(
        jnp.concatenate(split(table, FEW), axis=0), hot, NN, preferred_element_type=F32
    )
    found = sum((parts[at : at + HI] for at in range(HI, parts.shape[0], HI)), parts[:HI])
    found = jnp.where(joined(is_row(hi, HI)), found, 0.0)
    return found[:8] + found[8:]


def folded(a, *shifts):
    for shift in shifts:
        a = a + pltpu.roll(a, shift, 0)
    return a


def gather(table, hi, hot):
    return folded(picked(table, hi, hot), 4, 2, 1)


def gather_both(first, second):
    a, b = folded(picked(*first), 4), folded(picked(*second), 4)
    return folded(jnp.where((row_iota(a.shape) & 7) < 4, a, b), 2, 1)


def across(x, f):
    return [x[f : f + 1, i : i + LO] for i in range(0, x.shape[1], LO)]


def split_rows(tiles):
    return [rows_of(part) for part in zip(*(split(tile, EXACT) for tile in tiles))]


class Ids:
    def __init__(self, tiles, size, offsets=None):
        ids = [tile.astype(I32) for tile in tiles]
        if offsets is None:
            high = [i >> 7 for i in ids]
        else:
            high = [((i >> 6) & 1) * 4 + (i >> 7) + at for i, at in zip(ids, offsets)]
        self.size = size
        self.low_rows = rows_of([small(i & (size - 1)) for i in ids])
        self.bf = rows_of([small(h) for h in high])
        self.full = rows_of([h.astype(F32) for h in high])

    def hot(self):
        return onehot(self.low_rows, self.size)


def copies(refs, held, sems):
    return [pltpu.make_async_copy(ref, to, sems.at[i]) for i, (ref, to) in enumerate(zip(refs, held))]


def pack_kernel(
    block_ref, slot_in, expo_in, pix_in, mag_in, w_in, out_ref, expo_ref, slot, expo, pix, mag, w, sems
):
    moves = copies((slot_in, expo_in, pix_in, mag_in, w_in), (slot, expo, pix, mag, w), sems)
    for move in moves:
        move.start()
    for move in moves:
        move.wait()
    rows = row_iota((8, LO))
    weights, weighted = [], []
    for kk in range(2):
        at = pl.ds(8 * kk, 8)
        base = jnp.zeros((8, LO), I32)
        for i in range(8):
            base = jnp.where(rows == i, block_ref[0, 8 * kk + i] * 256 + (i // 2) * 512, base)
        p = pix[at, :]
        weights.append(w[at, :])
        weighted.append(w[at, :] * mag[at, :])
        fields = (
            (slot[at, :] + base).astype(F32),
            ((((p >> 7) & 1) * 8 + (p >> 8)) * LO + (p & 127)).astype(F32),
            expo[at, :].astype(F32),
            weights[kk],
            weighted[kk],
        )
        for f, tile in enumerate(fields):
            out_ref[40 * kk + 8 * f : 40 * kk + 8 * f + 8] = tile
    ids = Ids([expo[0:8], expo[8:16]], HALF, (0, 0))
    total, count = scatter([split_rows(weighted), split_rows(weights)], ids.bf, ids.hot())
    both = joined([total[:8], count[:8]])
    for peer in range(NZ * NH):
        expo_ref[peer] = both


def field(obs_ref, y, rel, kk, f):
    return obs_ref[y, pl.ds(pl.multiple_of(rel * 80 + kk * 40 + f * 8, 8), 8), :]


def chunk(obs_ref, step, f):
    kk, half = step // 2, step % 2
    return [field(obs_ref, 2 * half + yy, rel, kk, f) for yy in range(2) for rel in range(2)]


def own(obs_ref, y, kk, f):
    return [field(obs_ref, y, rel, kk, f) for rel in range(2)]


def edge_rows(flat):
    return jnp.concatenate([flat[0:1], flat[8:9], flat[7:8], flat[15:16]], axis=0)


def add_sums(tiles, kk, star_ref, star_count_ref, flat_ref, flat_count_ref):
    values = [split_rows(tiles(f)) for f in (WM, W)]
    ids = Ids(tiles(S), LO)
    weighted, count = scatter(values, ids.bf, ids.hot())
    star_ref[kk] += weighted
    star_count_ref[kk] += count
    ids = Ids(tiles(PX), LO)
    weighted, count = scatter(values, ids.bf, ids.hot())
    flat_ref[...] += weighted
    flat_count_ref[...] += count


def own_sums_kernel(both_ref, *totals):
    for ref in totals:
        ref[...] = jnp.zeros(ref.shape, F32)
    for kk in range(2):

        def tiles(f):
            return [both_ref[80 * rel + 40 * kk + 8 * f : 80 * rel + 40 * kk + 8 * f + 8] for rel in range(2)]

        add_sums(tiles, kk, *totals)


def sums_kernel(
    obs_ref, star_in, star_count_in, flat_in, flat_count_in, g0s_ref, ds_ref, g0f_ref, df_ref, hop_ref, plane_ref
):
    totals = (g0s_ref, ds_ref, g0f_ref, df_ref)
    for ref, given in zip(totals, (star_in, star_count_in, flat_in, flat_count_in)):
        ref[...] = given[...]
    y = lax.axis_index("y")

    def sums(kk, carry):
        def tiles(f):
            return [tile for d in range(1, NY) for tile in own(obs_ref, (y + d) % NY, kk, f)]

        add_sums(tiles, kk, *totals)
        return carry

    lax.fori_loop(0, 2, sums, 0)
    diag = df_ref[...] + (4.0 * SMOOTH + RIDGE)
    g0f = g0f_ref[...] / diag
    df_ref[...] = diag
    g0f_ref[...] = g0f
    diag = ds_ref[...] + RIDGE
    g0s_ref[...] = g0s_ref[...] / diag
    ds_ref[...] = diag
    edges = edge_rows(g0f)
    hop_ref[...] = jnp.where(lax.axis_index("c") == 1, edges[2:4], edges[0:2])
    for peer in range(NX * NC):
        for y in range(NY):
            plane_ref[peer, 16 * y : 16 * y + 16] = obs_ref[y, 160:176]
        plane_ref[peer, 64:68] = edges
        plane_ref[peer, 68:72] = jnp.zeros((4, LO), F32)


def couple_kernel(obs_ref, g0s_ref, g0f_ref, cs_ref, cf_ref, ru_ref, fit_ref):
    cs_ref[...] = jnp.zeros(cs_ref.shape, F32)
    cf_ref[...] = jnp.zeros((HI, LO), F32)

    def couple(step, carry):
        star, flat = Ids(chunk(obs_ref, step, S), LO), Ids(chunk(obs_ref, step, PX), LO)
        hs, hp = star.hot(), flat.hot()
        fit = joined(rows_of(chunk(obs_ref, step, W))) * gather_both(
            (g0s_ref[step // 2], star.full, hs), (g0f_ref[...], flat.full, hp)
        )
        parts = split(fit, FEW)
        (added,) = scatter([[across(part, FLAT) for part in parts]], star.bf, hs)
        cs_ref[step // 2] += added
        (added,) = scatter([[across(part, STAR) for part in parts]], flat.bf, hp)
        cf_ref[...] += added
        fit_ref[step] = fit
        return carry

    lax.fori_loop(0, 4, couple, 0)
    y = lax.axis_index("y")
    total = jnp.zeros((HI, HALF), F32)
    for kk in range(2):
        ids = Ids(own(obs_ref, y, kk, E), HALF, (0, 8))
        at = pl.ds(pl.multiple_of((y % 2) * 2048, 2048), 2048)
        fit = fit_ref[2 * kk + y // 2, :, at]
        parts = split(row(fit, STAR) + row(fit, FLAT), FEW)
        (added,) = scatter([[across(part, 0) for part in parts]], ids.bf, ids.hot())
        total += added
    ru_ref[...] = total


def beside(flat, above, below):
    left, right = flat[:8], flat[8:]
    rows = row_iota((8, LO))
    lanes = lax.broadcasted_iota(I32, (8, LO), 1)
    out = []
    left_up, right_up = pltpu.roll(left, 1, 1), pltpu.roll(right, 1, 1)
    left_down, right_down = pltpu.roll(left, 127, 1), pltpu.roll(right, 127, 1)
    sides = (
        jnp.where(lanes == 0, 0.0, left_up) + jnp.where(lanes == 127, right_down, left_down),
        jnp.where(lanes == 0, left_up, right_up) + jnp.where(lanes == 127, 0.0, right_down),
    )
    for i, half in enumerate((left, right)):
        upper = jnp.where(rows == 0, above[i : i + 1], pltpu.roll(half, 1, 0))
        lower = jnp.where(rows == 7, below[i : i + 1], pltpu.roll(half, 7, 0))
        out.append(sides[i] + upper + lower)
    return jnp.concatenate(out, axis=0)


def fold8(a):
    total = a[0:8]
    for i in range(8, a.shape[0], 8):
        total = total + a[i : i + 8]
    return jnp.sum(total, axis=0, keepdims=True)


def fold_lanes(a):
    total = a[:, 0:LO]
    for i in range(LO, a.shape[1], LO):
        total = total + a[:, i : i + LO]
    return total


def apply_kernel(
    obs_ref, expo_ref, g0s_ref, ds_ref, cs_in, g0f_ref, cf_in, df_ref, ru_ref, hop_ref,
    ys_ref, yf_ref, g0z_ref, dz_ref, out_ref, cs_ref, cf_ref,
):
    part = expo_ref[0, 0:64]
    for xc in range(1, 8):
        part = part + expo_ref[xc, 0:64]
    for y in range(4):
        diag = part[16 * y : 16 * y + 16, HALF:] + RIDGE
        g0z_ref[y] = part[16 * y : 16 * y + 16, :HALF] / diag
        dz_ref[y] = diag
    cs_ref[...] = cs_in[...]
    cf_ref[...] = cf_in[...]

    def apply(step, carry):
        expo = Ids(chunk(obs_ref, step, E), HALF, (0, 8, 0, 8))
        hot = expo.hot()
        found = [
            gather(
                g0z_ref[2 * (step % 2) + yy],
                expo.full[16 * yy : 16 * yy + 16],
                hot[:, 2048 * yy : 2048 * (yy + 1)],
            )
            for yy in range(2)
        ]
        fit = joined(rows_of(chunk(obs_ref, step, W))) * joined(found)
        values = [[across(part, 0) for part in split(fit, FEW)]]
        flat = Ids(chunk(obs_ref, step, PX), LO)
        (added,) = scatter(values, flat.bf, flat.hot())
        cf_ref[...] += added
        star = Ids(chunk(obs_ref, step, S), LO)
        (added,) = scatter(values, star.bf, star.hot())
        cs_ref[step // 2] += added
        return carry

    lax.fori_loop(0, 4, apply, 0)
    x, c, y = lax.axis_index("x"), lax.axis_index("c"), lax.axis_index("y")
    chip = expo_ref[2 * x + 1 - c, 64:68]
    above = jnp.where(c == 1, chip[2:4], hop_ref[...])
    below = jnp.where(c == 1, hop_ref[...], chip[0:2])
    g0f, df = g0f_ref[...], df_ref[...]
    cf = cf_ref[...] - SMOOTH * beside(g0f, above, below)
    yf = cf / df
    yf_ref[...] = yf
    rho, beta, eta = fold8(g0f * g0f * df), fold8(g0f * cf), fold8(cf * yf)
    for kk in range(2):
        g0s, ds, cs = g0s_ref[kk], ds_ref[kk], cs_ref[kk]
        ys = cs / ds
        ys_ref[kk] = ys
        rho += fold8(g0s * g0s * ds)
        beta += fold8(g0s * cs)
        eta += fold8(cs * ys)
    total = jnp.zeros((HI, HALF), F32)
    cross = jnp.zeros((1, LO), F32)
    for kk in range(2):
        star, flat = Ids(own(obs_ref, y, kk, S), LO), Ids(own(obs_ref, y, kk, PX), LO)
        expo = Ids(own(obs_ref, y, kk, E), HALF, (0, 8))
        w = joined(rows_of(own(obs_ref, y, kk, W)))
        both = gather_both((ys_ref[kk], star.full, star.hot()), (yf, flat.full, flat.hot()))
        from_star, from_flat = row(both, STAR), row(both, FLAT)
        parts = split(w * (from_star + from_flat), FEW)
        (added,) = scatter([[across(part, 0) for part in parts]], expo.bf, expo.hot())
        total += added
        cross += fold_lanes(w * from_star * from_flat)
    expos = joined([ru_ref[...], total])
    none = jnp.zeros((2, LO), F32)
    delta = 2.0 * cross - (0.25 * SMOOTH) * fold8(yf * beside(yf, none, none))
    scal = jnp.concatenate(
        [0.25 * rho, 0.25 * beta, 0.25 * eta, delta, edge_rows(yf)], axis=0
    )
    for zl in range(NZ):
        for half in range(NC):
            out_ref[NC * zl + half, 0:8] = expos[8 * half : 8 * half + 8]
            out_ref[NC * zl + half, 8:16] = scal


def edge_dot(last, first):
    both = last * first
    return -(0.5 * SMOOTH) * (both[0:1] + both[1:2])


def column_kernel(parts_ref, out_ref):
    total = parts_ref[0]
    for peer in range(1, NZ * NC):
        total = total + parts_ref[peer]
    between = edge_dot(parts_ref[0, 14:16], parts_ref[1, 12:14])
    for peer in range(1, NZ * NC - 1):
        between += edge_dot(parts_ref[peer, 14:16], parts_ref[peer + 1, 12:14])
    scal = total[8:12] + jnp.where(row_iota((4, LO)) == 3, between, 0.0)
    ends = jnp.concatenate([scal, parts_ref[0, 12:14], parts_ref[NZ * NC - 1, 14:16]], axis=0)
    for peer in range(NX * NC * NY):
        out_ref[peer, 0:8] = total[0:8]
        out_ref[peer, 8:16] = ends


def whole(a):
    return jnp.sum(jnp.sum(a, axis=0, keepdims=True), axis=1, keepdims=True)


def finish_kernel(
    sums_ref, g0z_ref, dz_ref, g0s_ref, ys_ref, g0f_ref, yf_ref, star_out, zero_out, flat_out
):
    y, zh = lax.axis_index("y"), lax.axis_index("zh")
    scal = jnp.zeros((4, LO), F32)
    for x in range(NX):
        for i in range(NY):
            scal = scal + sums_ref[8 * x + i, 8:12]
    z_rho = jnp.zeros((HI, HALF), F32)
    z_beta, z_eta, z_delta = z_rho, z_rho, z_rho
    z_own = z_rho
    for i in range(4):
        halves = []
        for c in range(NC):
            half = sums_ref[4 * c + i, 0:8]
            for x in range(1, NX):
                half = half + sums_ref[8 * x + 4 * c + i, 0:8]
            halves.append(half)
        part = jnp.concatenate(halves, axis=0)
        cz, qz = part[:, :HALF], part[:, HALF:]
        g0z, dz = g0z_ref[i], dz_ref[i]
        yz = cz / dz
        z_rho += g0z * g0z * dz
        z_beta += g0z * cz
        z_eta += cz * yz
        z_delta += qz * yz
        z_own = jnp.where(i == y, yz, z_own)
    rho0 = whole(z_rho) + whole(scal[0:1])
    beta = whole(z_beta) + whole(scal[1:2])
    eta = whole(z_eta) + whole(scal[2:3])
    between = jnp.zeros((1, LO), F32)
    for x in range(NX - 1):
        between += 4.0 * edge_dot(sums_ref[8 * x, 14:16], sums_ref[8 * x + 8, 12:14])
    delta = 2.0 * whole(z_delta) + whole(scal[3:4] + between)
    curv0 = rho0 + beta
    step0 = rho0 / curv0
    left = beta / curv0
    rho1 = left * left * rho0 - 2.0 * step0 * left * beta + step0 * step0 * eta
    curv_g = (
        left * left * curv0
        - 2.0 * step0 * left * (beta + eta)
        + step0 * step0 * (eta + delta)
    )
    ratio = rho1 / rho0
    mixed = left * curv0 - step0 * (beta + eta)
    curv1 = curv_g + 2.0 * ratio * mixed + ratio * ratio * curv0
    step1 = rho1 / curv1
    along_g = step0 + step1 * (left + ratio)
    along_y = -step1 * step0
    star = along_g * g0s_ref[y // 2] + along_y * ys_ref[y // 2]
    shard = (y % 2) * 2 + zh
    mine = jnp.zeros((4, LO), F32)
    for i in range(4):
        mine = jnp.where(shard == i, star[4 * i : 4 * i + 4], mine)
    star_out[...] = mine
    zero = along_g * g0z_ref[y] + along_y * z_own
    zero_out[...] = jnp.concatenate([zero[0:4], pltpu.roll(zero[0:8], 4, 0)[0:4]], axis=1)
    flat = along_g * g0f_ref[...] + along_y * yf_ref[...]
    flat_out[...] = joined([flat[:8], flat[8:]])


VMEM = pl.BlockSpec(memory_space=pltpu.VMEM)
SMEM = pl.BlockSpec(memory_space=pltpu.SMEM)


HBM = pl.BlockSpec(memory_space=pltpu.HBM)


def call(kernel, shapes, args, specs=None, scratch=(), mib=8, work=20):
    out = [jax.ShapeDtypeStruct(shape, F32) for shape in shapes]
    many = len(out) > 1
    return pl.pallas_call(
        kernel,
        out_shape=tuple(out) if many else out[0],
        in_specs=specs or [VMEM] * len(args),
        out_specs=tuple([VMEM] * len(out)) if many else VMEM,
        scratch_shapes=list(scratch),
        compiler_params=pltpu.CompilerParams(vmem_limit_bytes=mib << 20 if mib else None),
        cost_estimate=pl.CostEstimate(flops=1 << work, bytes_accessed=1 << 20, transcendentals=0),
    )(*args)


def exchange(blocks, axes):
    return lax.all_to_all(blocks, axes, 0, 0, tiled=True)


def to_all(block, peers, axes):
    return exchange(jnp.broadcast_to(block[None], (peers, *block.shape)), axes)


def hop_pairs():
    def place(tile, y, zh):
        x, rest = divmod(tile, NZ * NC)
        zl, c = divmod(rest, NC)
        return (((x * NZ + zl) * NC + c) * NY + y) * NH + zh

    hop = []
    for tile in range(1, NX * NZ * NC - 1, 2):
        far = (tile + 1) % (NZ * NC) == 0
        for y in range(NY):
            for zh in range(NH):
                here, there = place(tile, y, zh), place(tile + 1, y, 1 - zh if far else zh)
                hop.extend([(here, there), (there, here)])
    return hop


def on_device(star_slot, star_block, exposure, superpixel, magnitude, weight):
    zh = lax.axis_index("zh")
    hop = hop_pairs()
    stars, flats, expos = (2, HI, LO), (HI, LO), (4, HI, HALF)
    obs, expo = call(
        pack_kernel, [(80, LO), (16, 8, LO)],
        (star_block, star_slot[0], exposure[0], superpixel[0], magnitude[0], weight[0]),
        specs=[SMEM] + [HBM] * 5,
        scratch=[pltpu.VMEM((16, LO), t) for t in (I32, I32, I32, F32, F32)]
        + [pltpu.SemaphoreType.DMA((5,))],
        mib=None,
    )
    partner = lax.ppermute(obs, "zh", [(0, 1), (1, 0)])
    expo = exchange(expo, ("zl", "zh"))
    expo = expo.reshape(NZ, NH, 8, LO).sum(axis=0)
    expo = jnp.where(zh == 0, expo, expo[::-1]).reshape(HI, LO)
    both = lax.optimization_barrier(jnp.concatenate([obs, partner], axis=0))
    totals = call(own_sums_kernel, [stars] * 2 + [flats] * 2, (both,), work=26)
    both, totals = lax.optimization_barrier((both, totals))
    tile_obs = jnp.concatenate([both, expo], axis=0)
    tile_obs = to_all(lax.optimization_barrier(tile_obs), NY, "y")
    g0s, ds, g0f, df, hop_row, plane = call(
        sums_kernel, [stars] * 2 + [flats] * 2 + [(2, LO), (8, 72, LO)], (tile_obs, *totals), mib=16, work=29
    )
    expo = exchange(plane, COLS)
    by_hop = lax.ppermute(hop_row, ALL, hop)
    cs, cf, ru = call(
        couple_kernel, [stars, flats, (HI, HALF)], (tile_obs, g0s, g0f),
        scratch=[pltpu.VMEM((4, 8, 4096), F32)], mib=16, work=30,
    )
    ys, yf, g0z, dz, payload = call(
        apply_kernel, [stars, flats] + [expos] * 2 + [(16, 16, LO)],
        (tile_obs, expo, g0s, ds, cs, g0f, cf, df, ru, by_hop),
        scratch=[pltpu.VMEM(stars, F32), pltpu.VMEM(flats, F32)], mib=16, work=30,
    )
    payload = exchange(payload, ("zl", "c"))
    sums = exchange(call(column_kernel, [(32, 16, LO)], (payload,)), PLANE)
    star, zero, flat = call(
        finish_kernel, [(4, LO), (4, LO), (8, 2 * LO)], (sums, g0z, dz, g0s, ys, g0f, yf)
    )
    return star.reshape(-1), zero.reshape(-1), flat


def solution(mesh):
    split = Mesh(mesh.devices.reshape(NX, NZ, NC, NY, NH), ALL)
    tile, loop = ("x", "zl", "c"), ("y", "zh")
    placed = (
        P(tile, loop, None),
        P(tile, loop),
        P(tile, loop, None),
        P(tile, loop, None),
        P(tile, loop, None),
        P(tile, loop, None),
    )
    return jax.shard_map(
        on_device,
        mesh=split,
        in_specs=placed,
        out_specs=(P(ALL), P(loop), P(tile, None)),
        check_vma=False,
    )
```

```python
import jax
import jax.numpy as jnp
from jax import lax
from jax.experimental import pallas as pl
from jax.experimental.pallas import tpu as pltpu
from jax.sharding import Mesh
from jax.sharding import PartitionSpec as P

SMOOTH = 2.0
RIDGE = 0.5
LO, HALF, HI = 128, 64, 16
NX, NZ, NC, NY, NH = 4, 8, 2, 4, 2
ALL = ("x", "zl", "c", "y", "zh")
PLANE = ("x", "c", "y")
COLS = ("x", "c")
F32 = jnp.float32
I32 = jnp.int32
BF16 = jnp.bfloat16
NT = (((1,), (1,)), ((), ()))
NN = (((1,), (0,)), ((), ()))
S, PX, E, W, WM = range(5)
EXACT, FEW = 3, 2
STAR, FLAT = 3, 7


def split(v, count):
    parts = []
    for _ in range(count):
        parts.append(v.astype(BF16))
        v = v - parts[-1].astype(F32)
    return parts


def row_iota(shape):
    return lax.broadcasted_iota(I32, shape, 0)


def row(x, f):
    return x[f : f + 1]


def rows_of(tiles):
    return [row(tile, i) for tile in tiles for i in range(tile.shape[0])]


def small(ids):
    return ids.astype(F32).astype(BF16)


def joined(tiles):
    return jnp.concatenate(tiles, axis=1)


def is_row(ids, count):
    rows = row_iota((count, LO)).astype(F32).astype(ids[0].dtype)
    return [rows == jnp.broadcast_to(one, (count, LO)) for one in ids]


def onehot(lo, size):
    one, zero = jnp.ones((), BF16), jnp.zeros((), BF16)
    return joined([jnp.where(same, one, zero) for same in is_row(lo, size)])


def scatter(values, hi, hot):
    masks = is_row(hi, HI)
    zero = jnp.zeros((), BF16)
    rows = [
        joined([jnp.where(m, jnp.broadcast_to(p, (HI, LO)), zero) for m, p in zip(masks, part)])
        for value in values
        for part in value
    ]
    sums = lax.dot_general(jnp.concatenate(rows, axis=0), hot, NT, preferred_element_type=F32)
    sums = [sums[at : at + HI] for at in range(0, sums.shape[0], HI)]
    count = len(values[0])
    return [sum(sums[i + 1 : i + count], sums[i]) for i in range(0, len(sums), count)]


def picked(table, hi, hot):
    parts = lax.dot_general(
        jnp.concatenate(split(table, FEW), axis=0), hot, NN, preferred_element_type=F32
    )
    found = sum((parts[at : at + HI] for at in range(HI, parts.shape[0], HI)), parts[:HI])
    found = jnp.where(joined(is_row(hi, HI)), found, 0.0)
    return found[:8] + found[8:]


def folded(a, *shifts):
    for shift in shifts:
        a = a + pltpu.roll(a, shift, 0)
    return a


def gather(table, hi, hot):
    return folded(picked(table, hi, hot), 4, 2, 1)


def gather_both(first, second):
    a, b = folded(picked(*first), 4), folded(picked(*second), 4)
    return folded(jnp.where((row_iota(a.shape) & 7) < 4, a, b), 2, 1)


def across(x, f):
    return [x[f : f + 1, i : i + LO] for i in range(0, x.shape[1], LO)]


def split_rows(tiles):
    return [rows_of(part) for part in zip(*(split(tile, EXACT) for tile in tiles))]


class Ids:
    def __init__(self, tiles, size, offsets=None):
        ids = [tile.astype(I32) for tile in tiles]
        if offsets is None:
            high = [i >> 7 for i in ids]
        else:
            high = [((i >> 6) & 1) * 4 + (i >> 7) + at for i, at in zip(ids, offsets)]
        self.size = size
        self.low_rows = rows_of([small(i & (size - 1)) for i in ids])
        self.bf = rows_of([small(h) for h in high])
        self.full = rows_of([h.astype(F32) for h in high])

    def hot(self):
        return onehot(self.low_rows, self.size)


def copies(refs, held, sems):
    return [pltpu.make_async_copy(ref, to, sems.at[i]) for i, (ref, to) in enumerate(zip(refs, held))]


def pack_kernel(
    block_ref, slot_in, expo_in, pix_in, mag_in, w_in, out_ref, expo_ref, slot, expo, pix, mag, w, sems
):
    moves = copies((slot_in, expo_in, pix_in, mag_in, w_in), (slot, expo, pix, mag, w), sems)
    for move in moves:
        move.start()
    for move in moves:
        move.wait()
    rows = row_iota((8, LO))
    weights, weighted = [], []
    for kk in range(2):
        at = pl.ds(8 * kk, 8)
        base = jnp.zeros((8, LO), I32)
        for i in range(8):
            base = jnp.where(rows == i, block_ref[0, 8 * kk + i] * 256 + (i // 2) * 512, base)
        p = pix[at, :]
        weights.append(w[at, :])
        weighted.append(w[at, :] * mag[at, :])
        fields = (
            (slot[at, :] + base).astype(F32),
            ((((p >> 7) & 1) * 8 + (p >> 8)) * LO + (p & 127)).astype(F32),
            expo[at, :].astype(F32),
            weights[kk],
            weighted[kk],
        )
        for f, tile in enumerate(fields):
            out_ref[40 * kk + 8 * f : 40 * kk + 8 * f + 8] = tile
    ids = Ids([expo[0:8], expo[8:16]], HALF, (0, 0))
    total, count = scatter([split_rows(weighted), split_rows(weights)], ids.bf, ids.hot())
    both = joined([total[:8], count[:8]])
    for peer in range(NZ * NH):
        expo_ref[peer] = both


def field(obs_ref, y, rel, kk, f):
    return obs_ref[y, pl.ds(pl.multiple_of(rel * 80 + kk * 40 + f * 8, 8), 8), :]


def chunk(obs_ref, step, f):
    kk, half = step // 2, step % 2
    return [field(obs_ref, 2 * half + yy, rel, kk, f) for yy in range(2) for rel in range(2)]


def own(obs_ref, y, kk, f):
    return [field(obs_ref, y, rel, kk, f) for rel in range(2)]


def unrolled(count, step):
    for i in range(count):
        step(i, 0)


def edge_rows(flat):
    return jnp.concatenate([flat[0:1], flat[8:9], flat[7:8], flat[15:16]], axis=0)


def add_sums(tiles, kk, star_ref, star_count_ref, flat_ref, flat_count_ref):
    values = [split_rows(tiles(f)) for f in (WM, W)]
    ids = Ids(tiles(S), LO)
    weighted, count = scatter(values, ids.bf, ids.hot())
    star_ref[kk] += weighted
    star_count_ref[kk] += count
    ids = Ids(tiles(PX), LO)
    weighted, count = scatter(values, ids.bf, ids.hot())
    flat_ref[...] += weighted
    flat_count_ref[...] += count


def own_sums_kernel(both_ref, *totals):
    for ref in totals:
        ref[...] = jnp.zeros(ref.shape, F32)
    for kk in range(2):

        def tiles(f):
            return [both_ref[80 * rel + 40 * kk + 8 * f : 80 * rel + 40 * kk + 8 * f + 8] for rel in range(2)]

        add_sums(tiles, kk, *totals)


def sums_kernel(
    obs_ref, star_in, star_count_in, flat_in, flat_count_in, g0s_ref, ds_ref, g0f_ref, df_ref, hop_ref, plane_ref
):
    totals = (g0s_ref, ds_ref, g0f_ref, df_ref)
    for ref, given in zip(totals, (star_in, star_count_in, flat_in, flat_count_in)):
        ref[...] = given[...]
    y = lax.axis_index("y")

    def sums(kk, carry):
        def tiles(f):
            return [tile for d in range(1, NY) for tile in own(obs_ref, (y + d) % NY, kk, f)]

        add_sums(tiles, kk, *totals)
        return carry

    unrolled(2, sums)
    diag = df_ref[...] + (4.0 * SMOOTH + RIDGE)
    g0f = g0f_ref[...] / diag
    df_ref[...] = diag
    g0f_ref[...] = g0f
    diag = ds_ref[...] + RIDGE
    g0s_ref[...] = g0s_ref[...] / diag
    ds_ref[...] = diag
    edges = edge_rows(g0f)
    hop_ref[...] = jnp.where(lax.axis_index("c") == 1, edges[2:4], edges[0:2])
    for peer in range(NX * NC):
        for y in range(NY):
            plane_ref[peer, 16 * y : 16 * y + 16] = obs_ref[y, 160:176]
        plane_ref[peer, 64:68] = edges
        plane_ref[peer, 68:72] = jnp.zeros((4, LO), F32)


def couple_kernel(obs_ref, g0s_ref, g0f_ref, cs_ref, cf_ref, ru_ref, fit_ref):
    cs_ref[...] = jnp.zeros(cs_ref.shape, F32)
    cf_ref[...] = jnp.zeros((HI, LO), F32)

    def couple(step, carry):
        star, flat = Ids(chunk(obs_ref, step, S), LO), Ids(chunk(obs_ref, step, PX), LO)
        hs, hp = star.hot(), flat.hot()
        fit = joined(rows_of(chunk(obs_ref, step, W))) * gather_both(
            (g0s_ref[step // 2], star.full, hs), (g0f_ref[...], flat.full, hp)
        )
        parts = split(fit, FEW)
        (added,) = scatter([[across(part, FLAT) for part in parts]], star.bf, hs)
        cs_ref[step // 2] += added
        (added,) = scatter([[across(part, STAR) for part in parts]], flat.bf, hp)
        cf_ref[...] += added
        fit_ref[step] = fit
        return carry

    unrolled(4, couple)
    y = lax.axis_index("y")
    total = jnp.zeros((HI, HALF), F32)
    for kk in range(2):
        ids = Ids(own(obs_ref, y, kk, E), HALF, (0, 8))
        at = pl.ds(pl.multiple_of((y % 2) * 2048, 2048), 2048)
        fit = fit_ref[2 * kk + y // 2, :, at]
        parts = split(row(fit, STAR) + row(fit, FLAT), FEW)
        (added,) = scatter([[across(part, 0) for part in parts]], ids.bf, ids.hot())
        total += added
    ru_ref[...] = total


def beside(flat, above, below):
    left, right = flat[:8], flat[8:]
    rows = row_iota((8, LO))
    lanes = lax.broadcasted_iota(I32, (8, LO), 1)
    out = []
    left_up, right_up = pltpu.roll(left, 1, 1), pltpu.roll(right, 1, 1)
    left_down, right_down = pltpu.roll(left, 127, 1), pltpu.roll(right, 127, 1)
    sides = (
        jnp.where(lanes == 0, 0.0, left_up) + jnp.where(lanes == 127, right_down, left_down),
        jnp.where(lanes == 0, left_up, right_up) + jnp.where(lanes == 127, 0.0, right_down),
    )
    for i, half in enumerate((left, right)):
        upper = jnp.where(rows == 0, above[i : i + 1], pltpu.roll(half, 1, 0))
        lower = jnp.where(rows == 7, below[i : i + 1], pltpu.roll(half, 7, 0))
        out.append(sides[i] + upper + lower)
    return jnp.concatenate(out, axis=0)


def fold8(a):
    total = a[0:8]
    for i in range(8, a.shape[0], 8):
        total = total + a[i : i + 8]
    return jnp.sum(total, axis=0, keepdims=True)


def fold_lanes(a):
    total = a[:, 0:LO]
    for i in range(LO, a.shape[1], LO):
        total = total + a[:, i : i + LO]
    return total


def apply_kernel(
    obs_ref, expo_ref, g0s_ref, ds_ref, cs_in, g0f_ref, cf_in, df_ref, ru_ref, hop_ref,
    ys_ref, yf_ref, g0z_ref, dz_ref, out_ref, cs_ref, cf_ref,
):
    part = expo_ref[0, 0:64]
    for xc in range(1, 8):
        part = part + expo_ref[xc, 0:64]
    for y in range(4):
        diag = part[16 * y : 16 * y + 16, HALF:] + RIDGE
        g0z_ref[y] = part[16 * y : 16 * y + 16, :HALF] / diag
        dz_ref[y] = diag
    cs_ref[...] = cs_in[...]
    cf_ref[...] = cf_in[...]

    def apply(step, carry):
        expo = Ids(chunk(obs_ref, step, E), HALF, (0, 8, 0, 8))
        hot = expo.hot()
        found = [
            gather(
                g0z_ref[2 * (step % 2) + yy],
                expo.full[16 * yy : 16 * yy + 16],
                hot[:, 2048 * yy : 2048 * (yy + 1)],
            )
            for yy in range(2)
        ]
        fit = joined(rows_of(chunk(obs_ref, step, W))) * joined(found)
        values = [[across(part, 0) for part in split(fit, FEW)]]
        flat = Ids(chunk(obs_ref, step, PX), LO)
        (added,) = scatter(values, flat.bf, flat.hot())
        cf_ref[...] += added
        star = Ids(chunk(obs_ref, step, S), LO)
        (added,) = scatter(values, star.bf, star.hot())
        cs_ref[step // 2] += added
        return carry

    unrolled(4, apply)
    x, c, y = lax.axis_index("x"), lax.axis_index("c"), lax.axis_index("y")
    chip = expo_ref[2 * x + 1 - c, 64:68]
    above = jnp.where(c == 1, chip[2:4], hop_ref[...])
    below = jnp.where(c == 1, hop_ref[...], chip[0:2])
    g0f, df = g0f_ref[...], df_ref[...]
    cf = cf_ref[...] - SMOOTH * beside(g0f, above, below)
    yf = cf / df
    yf_ref[...] = yf
    rho, beta, eta = fold8(g0f * g0f * df), fold8(g0f * cf), fold8(cf * yf)
    for kk in range(2):
        g0s, ds, cs = g0s_ref[kk], ds_ref[kk], cs_ref[kk]
        ys = cs / ds
        ys_ref[kk] = ys
        rho += fold8(g0s * g0s * ds)
        beta += fold8(g0s * cs)
        eta += fold8(cs * ys)
    total = jnp.zeros((HI, HALF), F32)
    cross = jnp.zeros((1, LO), F32)
    for kk in range(2):
        star, flat = Ids(own(obs_ref, y, kk, S), LO), Ids(own(obs_ref, y, kk, PX), LO)
        expo = Ids(own(obs_ref, y, kk, E), HALF, (0, 8))
        w = joined(rows_of(own(obs_ref, y, kk, W)))
        both = gather_both((ys_ref[kk], star.full, star.hot()), (yf, flat.full, flat.hot()))
        from_star, from_flat = row(both, STAR), row(both, FLAT)
        parts = split(w * (from_star + from_flat), FEW)
        (added,) = scatter([[across(part, 0) for part in parts]], expo.bf, expo.hot())
        total += added
        cross += fold_lanes(w * from_star * from_flat)
    expos = joined([ru_ref[...], total])
    none = jnp.zeros((2, LO), F32)
    delta = 2.0 * cross - (0.25 * SMOOTH) * fold8(yf * beside(yf, none, none))
    scal = jnp.concatenate(
        [0.25 * rho, 0.25 * beta, 0.25 * eta, delta, edge_rows(yf)], axis=0
    )
    for zl in range(NZ):
        for half in range(NC):
            out_ref[NC * zl + half, 0:8] = expos[8 * half : 8 * half + 8]
            out_ref[NC * zl + half, 8:16] = scal


def edge_dot(last, first):
    both = last * first
    return -(0.5 * SMOOTH) * (both[0:1] + both[1:2])


def column_kernel(parts_ref, out_ref):
    total = parts_ref[0]
    for peer in range(1, NZ * NC):
        total = total + parts_ref[peer]
    between = edge_dot(parts_ref[0, 14:16], parts_ref[1, 12:14])
    for peer in range(1, NZ * NC - 1):
        between += edge_dot(parts_ref[peer, 14:16], parts_ref[peer + 1, 12:14])
    scal = total[8:12] + jnp.where(row_iota((4, LO)) == 3, between, 0.0)
    ends = jnp.concatenate([scal, parts_ref[0, 12:14], parts_ref[NZ * NC - 1, 14:16]], axis=0)
    for peer in range(NX * NC * NY):
        out_ref[peer, 0:8] = total[0:8]
        out_ref[peer, 8:16] = ends


def whole(a):
    return jnp.sum(jnp.sum(a, axis=0, keepdims=True), axis=1, keepdims=True)


def finish_kernel(
    sums_ref, g0z_ref, dz_ref, g0s_ref, ys_ref, g0f_ref, yf_ref, star_out, zero_out, flat_out
):
    y, zh = lax.axis_index("y"), lax.axis_index("zh")
    scal = jnp.zeros((4, LO), F32)
    for x in range(NX):
        for i in range(NY):
            scal = scal + sums_ref[8 * x + i, 8:12]
    z_rho = jnp.zeros((HI, HALF), F32)
    z_beta, z_eta, z_delta = z_rho, z_rho, z_rho
    z_own = z_rho
    for i in range(4):
        halves = []
        for c in range(NC):
            half = sums_ref[4 * c + i, 0:8]
            for x in range(1, NX):
                half = half + sums_ref[8 * x + 4 * c + i, 0:8]
            halves.append(half)
        part = jnp.concatenate(halves, axis=0)
        cz, qz = part[:, :HALF], part[:, HALF:]
        g0z, dz = g0z_ref[i], dz_ref[i]
        yz = cz / dz
        z_rho += g0z * g0z * dz
        z_beta += g0z * cz
        z_eta += cz * yz
        z_delta += qz * yz
        z_own = jnp.where(i == y, yz, z_own)
    rho0 = whole(z_rho) + whole(scal[0:1])
    beta = whole(z_beta) + whole(scal[1:2])
    eta = whole(z_eta) + whole(scal[2:3])
    between = jnp.zeros((1, LO), F32)
    for x in range(NX - 1):
        between += 4.0 * edge_dot(sums_ref[8 * x, 14:16], sums_ref[8 * x + 8, 12:14])
    delta = 2.0 * whole(z_delta) + whole(scal[3:4] + between)
    curv0 = rho0 + beta
    step0 = rho0 / curv0
    left = beta / curv0
    rho1 = left * left * rho0 - 2.0 * step0 * left * beta + step0 * step0 * eta
    curv_g = (
        left * left * curv0
        - 2.0 * step0 * left * (beta + eta)
        + step0 * step0 * (eta + delta)
    )
    ratio = rho1 / rho0
    mixed = left * curv0 - step0 * (beta + eta)
    curv1 = curv_g + 2.0 * ratio * mixed + ratio * ratio * curv0
    step1 = rho1 / curv1
    along_g = step0 + step1 * (left + ratio)
    along_y = -step1 * step0
    star = along_g * g0s_ref[y // 2] + along_y * ys_ref[y // 2]
    shard = (y % 2) * 2 + zh
    mine = jnp.zeros((4, LO), F32)
    for i in range(4):
        mine = jnp.where(shard == i, star[4 * i : 4 * i + 4], mine)
    star_out[...] = mine
    zero = along_g * g0z_ref[y] + along_y * z_own
    zero_out[...] = jnp.concatenate([zero[0:4], pltpu.roll(zero[0:8], 4, 0)[0:4]], axis=1)
    flat = along_g * g0f_ref[...] + along_y * yf_ref[...]
    flat_out[...] = joined([flat[:8], flat[8:]])


VMEM = pl.BlockSpec(memory_space=pltpu.VMEM)
SMEM = pl.BlockSpec(memory_space=pltpu.SMEM)


HBM = pl.BlockSpec(memory_space=pltpu.HBM)


def call(kernel, shapes, args, specs=None, scratch=(), mib=8, work=20):
    out = [jax.ShapeDtypeStruct(shape, F32) for shape in shapes]
    many = len(out) > 1
    return pl.pallas_call(
        kernel,
        out_shape=tuple(out) if many else out[0],
        in_specs=specs or [VMEM] * len(args),
        out_specs=tuple([VMEM] * len(out)) if many else VMEM,
        scratch_shapes=list(scratch),
        compiler_params=pltpu.CompilerParams(vmem_limit_bytes=mib << 20 if mib else None),
        cost_estimate=pl.CostEstimate(flops=1 << work, bytes_accessed=1 << 20, transcendentals=0),
    )(*args)


def exchange(blocks, axes):
    return lax.all_to_all(blocks, axes, 0, 0, tiled=True)


def to_all(block, peers, axes):
    return exchange(jnp.broadcast_to(block[None], (peers, *block.shape)), axes)


def hop_pairs():
    def place(tile, y, zh):
        x, rest = divmod(tile, NZ * NC)
        zl, c = divmod(rest, NC)
        return (((x * NZ + zl) * NC + c) * NY + y) * NH + zh

    hop = []
    for tile in range(1, NX * NZ * NC - 1, 2):
        far = (tile + 1) % (NZ * NC) == 0
        for y in range(NY):
            for zh in range(NH):
                here, there = place(tile, y, zh), place(tile + 1, y, 1 - zh if far else zh)
                hop.extend([(here, there), (there, here)])
    return hop


def on_device(star_slot, star_block, exposure, superpixel, magnitude, weight):
    zh = lax.axis_index("zh")
    hop = hop_pairs()
    stars, flats, expos = (2, HI, LO), (HI, LO), (4, HI, HALF)
    obs, expo = call(
        pack_kernel, [(80, LO), (16, 8, LO)],
        (star_block, star_slot[0], exposure[0], superpixel[0], magnitude[0], weight[0]),
        specs=[SMEM] + [HBM] * 5,
        scratch=[pltpu.VMEM((16, LO), t) for t in (I32, I32, I32, F32, F32)]
        + [pltpu.SemaphoreType.DMA((5,))],
        mib=None,
    )
    partner = lax.ppermute(obs, "zh", [(0, 1), (1, 0)])
    expo = exchange(expo, ("zl", "zh"))
    expo = expo.reshape(NZ, NH, 8, LO).sum(axis=0)
    expo = jnp.where(zh == 0, expo, expo[::-1]).reshape(HI, LO)
    both = lax.optimization_barrier(jnp.concatenate([obs, partner], axis=0))
    totals = call(own_sums_kernel, [stars] * 2 + [flats] * 2, (both,), work=26)
    both, totals = lax.optimization_barrier((both, totals))
    tile_obs = jnp.concatenate([both, expo], axis=0)
    tile_obs = to_all(lax.optimization_barrier(tile_obs), NY, "y")
    g0s, ds, g0f, df, hop_row, plane = call(
        sums_kernel, [stars] * 2 + [flats] * 2 + [(2, LO), (8, 72, LO)], (tile_obs, *totals), mib=16, work=29
    )
    expo = exchange(plane, COLS)
    by_hop = lax.ppermute(hop_row, ALL, hop)
    cs, cf, ru = call(
        couple_kernel, [stars, flats, (HI, HALF)], (tile_obs, g0s, g0f),
        scratch=[pltpu.VMEM((4, 8, 4096), F32)], mib=16, work=30,
    )
    ys, yf, g0z, dz, payload = call(
        apply_kernel, [stars, flats] + [expos] * 2 + [(16, 16, LO)],
        (tile_obs, expo, g0s, ds, cs, g0f, cf, df, ru, by_hop),
        scratch=[pltpu.VMEM(stars, F32), pltpu.VMEM(flats, F32)], mib=16, work=30,
    )
    payload = exchange(payload, ("zl", "c"))
    sums = exchange(call(column_kernel, [(32, 16, LO)], (payload,)), PLANE)
    star, zero, flat = call(
        finish_kernel, [(4, LO), (4, LO), (8, 2 * LO)], (sums, g0z, dz, g0s, ys, g0f, yf)
    )
    return star.reshape(-1), zero.reshape(-1), flat


def solution(mesh):
    split = Mesh(mesh.devices.reshape(NX, NZ, NC, NY, NH), ALL)
    tile, loop = ("x", "zl", "c"), ("y", "zh")
    placed = (
        P(tile, loop, None),
        P(tile, loop),
        P(tile, loop, None),
        P(tile, loop, None),
        P(tile, loop, None),
        P(tile, loop, None),
    )
    return jax.shard_map(
        on_device,
        mesh=split,
        in_specs=placed,
        out_specs=(P(ALL), P(loop), P(tile, None)),
        check_vma=False,
    )
```

```python
import jax
import jax.numpy as jnp
from jax import lax
from jax.experimental import pallas as pl
from jax.experimental.pallas import tpu as pltpu
from jax.sharding import Mesh
from jax.sharding import PartitionSpec as P

SMOOTH = 2.0
RIDGE = 0.5
LO, HALF, HI = 128, 64, 16
NX, NZ, NC, NY, NH = 4, 8, 2, 4, 2
ALL = ("x", "zl", "c", "y", "zh")
PLANE = ("x", "c", "y")
COLS = ("x", "c")
F32 = jnp.float32
I32 = jnp.int32
BF16 = jnp.bfloat16
NT = (((1,), (1,)), ((), ()))
NN = (((1,), (0,)), ((), ()))
S, PX, E, W, WM = range(5)
EXACT, FEW = 3, 2
STAR, FLAT = 3, 7


def split(v, count):
    parts = []
    for _ in range(count):
        parts.append(v.astype(BF16))
        v = v - parts[-1].astype(F32)
    return parts


def row_iota(shape):
    return lax.broadcasted_iota(I32, shape, 0)


def row(x, f):
    return x[f : f + 1]


def rows_of(tiles):
    return [row(tile, i) for tile in tiles for i in range(tile.shape[0])]


def small(ids):
    return ids.astype(F32).astype(BF16)


def joined(tiles):
    return jnp.concatenate(tiles, axis=1)


def is_row(ids, count):
    rows = row_iota((count, LO)).astype(F32).astype(ids[0].dtype)
    return [rows == jnp.broadcast_to(one, (count, LO)) for one in ids]


def onehot(lo, size):
    one, zero = jnp.ones((), BF16), jnp.zeros((), BF16)
    return joined([jnp.where(same, one, zero) for same in is_row(lo, size)])


def scatter(values, hi, hot):
    masks = is_row(hi, HI)
    zero = jnp.zeros((), BF16)
    rows = [
        joined([jnp.where(m, jnp.broadcast_to(p, (HI, LO)), zero) for m, p in zip(masks, part)])
        for value in values
        for part in value
    ]
    sums = lax.dot_general(jnp.concatenate(rows, axis=0), hot, NT, preferred_element_type=F32)
    sums = [sums[at : at + HI] for at in range(0, sums.shape[0], HI)]
    count = len(values[0])
    return [sum(sums[i + 1 : i + count], sums[i]) for i in range(0, len(sums), count)]


def picked(table, hi, hot):
    parts = lax.dot_general(
        jnp.concatenate(split(table, FEW), axis=0), hot, NN, preferred_element_type=F32
    )
    found = sum((parts[at : at + HI] for at in range(HI, parts.shape[0], HI)), parts[:HI])
    found = jnp.where(joined(is_row(hi, HI)), found, 0.0)
    return found[:8] + found[8:]


def folded(a, *shifts):
    for shift in shifts:
        a = a + pltpu.roll(a, shift, 0)
    return a


def gather(table, hi, hot):
    return folded(picked(table, hi, hot), 4, 2, 1)


def gather_both(first, second):
    a, b = folded(picked(*first), 4), folded(picked(*second), 4)
    return folded(jnp.where((row_iota(a.shape) & 7) < 4, a, b), 2, 1)


def across(x, f):
    return [x[f : f + 1, i : i + LO] for i in range(0, x.shape[1], LO)]


def split_rows(tiles):
    return [rows_of(part) for part in zip(*(split(tile, EXACT) for tile in tiles))]


class Ids:
    def __init__(self, tiles, size, offsets=None):
        ids = [tile.astype(I32) for tile in tiles]
        if offsets is None:
            high = [i >> 7 for i in ids]
        else:
            high = [((i >> 6) & 1) * 4 + (i >> 7) + at for i, at in zip(ids, offsets)]
        self.size = size
        self.low_rows = rows_of([small(i & (size - 1)) for i in ids])
        self.bf = rows_of([small(h) for h in high])
        self.full = rows_of([h.astype(F32) for h in high])

    def hot(self):
        return onehot(self.low_rows, self.size)


def copies(refs, held, sems):
    return [pltpu.make_async_copy(ref, to, sems.at[i]) for i, (ref, to) in enumerate(zip(refs, held))]


def pack_kernel(
    block_ref, slot_in, expo_in, pix_in, mag_in, w_in, out_ref, expo_ref, slot, expo, pix, mag, w, sems
):
    moves = copies((slot_in, expo_in, pix_in, mag_in, w_in), (slot, expo, pix, mag, w), sems)
    for move in moves:
        move.start()
    for move in moves:
        move.wait()
    rows = row_iota((8, LO))
    weights, weighted = [], []
    for kk in range(2):
        at = pl.ds(8 * kk, 8)
        base = jnp.zeros((8, LO), I32)
        for i in range(8):
            base = jnp.where(rows == i, block_ref[0, 8 * kk + i] * 256 + (i // 2) * 512, base)
        p = pix[at, :]
        weights.append(w[at, :])
        weighted.append(w[at, :] * mag[at, :])
        fields = (
            (slot[at, :] + base).astype(F32),
            ((((p >> 7) & 1) * 8 + (p >> 8)) * LO + (p & 127)).astype(F32),
            expo[at, :].astype(F32),
            weights[kk],
            weighted[kk],
        )
        for f, tile in enumerate(fields):
            out_ref[40 * kk + 8 * f : 40 * kk + 8 * f + 8] = tile
    ids = Ids([expo[0:8], expo[8:16]], HALF, (0, 0))
    total, count = scatter([split_rows(weighted), split_rows(weights)], ids.bf, ids.hot())
    both = joined([total[:8], count[:8]])
    for peer in range(NZ * NH):
        expo_ref[peer] = both


def field(obs_ref, y, rel, kk, f):
    return obs_ref[y, pl.ds(pl.multiple_of(rel * 64 + kk * 32 + f * 8, 8), 8), :]


def chunk(obs_ref, step, f):
    kk, half = step // 2, step % 2
    return [field(obs_ref, 2 * half + yy, rel, kk, f) for yy in range(2) for rel in range(2)]


def own(obs_ref, y, kk, f):
    return [field(obs_ref, y, rel, kk, f) for rel in range(2)]


def unrolled(count, step):
    for i in range(count):
        step(i, 0)


def edge_rows(flat):
    return jnp.concatenate([flat[0:1], flat[8:9], flat[7:8], flat[15:16]], axis=0)


def add_sums(tiles, kk, star_ref, star_count_ref, flat_ref, flat_count_ref):
    values = [split_rows(tiles(f)) for f in (WM, W)]
    ids = Ids(tiles(S), LO)
    weighted, count = scatter(values, ids.bf, ids.hot())
    star_ref[kk] += weighted
    star_count_ref[kk] += count
    ids = Ids(tiles(PX), LO)
    weighted, count = scatter(values, ids.bf, ids.hot())
    flat_ref[...] += weighted
    flat_count_ref[...] += count


def own_sums_kernel(both_ref, out_ref, *totals):
    for ref in totals:
        ref[...] = jnp.zeros(ref.shape, F32)
    for kk in range(2):

        def tiles(f):
            return [both_ref[80 * rel + 40 * kk + 8 * f : 80 * rel + 40 * kk + 8 * f + 8] for rel in range(2)]

        add_sums(tiles, kk, *totals)
    star, star_count, flat, flat_count = totals
    for kk in range(2):
        out_ref[16 * kk : 16 * kk + 16] = star[kk]
        out_ref[32 + 16 * kk : 48 + 16 * kk] = star_count[kk]
    out_ref[64:80] = flat[...]
    out_ref[80:96] = flat_count[...]


def sums_kernel(obs_ref, g0s_ref, ds_ref, g0f_ref, df_ref, hop_ref, plane_ref):
    total = obs_ref[0, 144:240]
    for y in range(1, NY):
        total = total + obs_ref[y, 144:240]
    for kk in range(2):
        g0s_ref[kk] = total[16 * kk : 16 * kk + 16]
        ds_ref[kk] = total[32 + 16 * kk : 48 + 16 * kk]
    g0f_ref[...] = total[64:80]
    df_ref[...] = total[80:96]
    diag = df_ref[...] + (4.0 * SMOOTH + RIDGE)
    g0f = g0f_ref[...] / diag
    df_ref[...] = diag
    g0f_ref[...] = g0f
    diag = ds_ref[...] + RIDGE
    g0s_ref[...] = g0s_ref[...] / diag
    ds_ref[...] = diag
    edges = edge_rows(g0f)
    hop_ref[...] = jnp.where(lax.axis_index("c") == 1, edges[2:4], edges[0:2])
    for peer in range(NX * NC):
        for y in range(NY):
            plane_ref[peer, 16 * y : 16 * y + 16] = obs_ref[y, 128:144]
        plane_ref[peer, 64:68] = edges
        plane_ref[peer, 68:72] = jnp.zeros((4, LO), F32)


def couple_kernel(obs_ref, g0s_ref, g0f_ref, cs_ref, cf_ref, ru_ref, fit_ref):
    cs_ref[...] = jnp.zeros(cs_ref.shape, F32)
    cf_ref[...] = jnp.zeros((HI, LO), F32)

    def couple(step, carry):
        star, flat = Ids(chunk(obs_ref, step, S), LO), Ids(chunk(obs_ref, step, PX), LO)
        hs, hp = star.hot(), flat.hot()
        fit = joined(rows_of(chunk(obs_ref, step, W))) * gather_both(
            (g0s_ref[step // 2], star.full, hs), (g0f_ref[...], flat.full, hp)
        )
        parts = split(fit, FEW)
        (added,) = scatter([[across(part, FLAT) for part in parts]], star.bf, hs)
        cs_ref[step // 2] += added
        (added,) = scatter([[across(part, STAR) for part in parts]], flat.bf, hp)
        cf_ref[...] += added
        fit_ref[step] = fit
        return carry

    unrolled(4, couple)
    y = lax.axis_index("y")
    total = jnp.zeros((HI, HALF), F32)
    for kk in range(2):
        ids = Ids(own(obs_ref, y, kk, E), HALF, (0, 8))
        at = pl.ds(pl.multiple_of((y % 2) * 2048, 2048), 2048)
        fit = fit_ref[2 * kk + y // 2, :, at]
        parts = split(row(fit, STAR) + row(fit, FLAT), FEW)
        (added,) = scatter([[across(part, 0) for part in parts]], ids.bf, ids.hot())
        total += added
    ru_ref[...] = total


def beside(flat, above, below):
    left, right = flat[:8], flat[8:]
    rows = row_iota((8, LO))
    lanes = lax.broadcasted_iota(I32, (8, LO), 1)
    out = []
    left_up, right_up = pltpu.roll(left, 1, 1), pltpu.roll(right, 1, 1)
    left_down, right_down = pltpu.roll(left, 127, 1), pltpu.roll(right, 127, 1)
    sides = (
        jnp.where(lanes == 0, 0.0, left_up) + jnp.where(lanes == 127, right_down, left_down),
        jnp.where(lanes == 0, left_up, right_up) + jnp.where(lanes == 127, 0.0, right_down),
    )
    for i, half in enumerate((left, right)):
        upper = jnp.where(rows == 0, above[i : i + 1], pltpu.roll(half, 1, 0))
        lower = jnp.where(rows == 7, below[i : i + 1], pltpu.roll(half, 7, 0))
        out.append(sides[i] + upper + lower)
    return jnp.concatenate(out, axis=0)


def fold8(a):
    total = a[0:8]
    for i in range(8, a.shape[0], 8):
        total = total + a[i : i + 8]
    return jnp.sum(total, axis=0, keepdims=True)


def fold_lanes(a):
    total = a[:, 0:LO]
    for i in range(LO, a.shape[1], LO):
        total = total + a[:, i : i + LO]
    return total


def apply_kernel(
    obs_ref, expo_ref, g0s_ref, ds_ref, cs_in, g0f_ref, cf_in, df_ref, ru_ref, hop_ref,
    ys_ref, yf_ref, g0z_ref, dz_ref, out_ref, cs_ref, cf_ref,
):
    part = expo_ref[0, 0:64]
    for xc in range(1, 8):
        part = part + expo_ref[xc, 0:64]
    for y in range(4):
        diag = part[16 * y : 16 * y + 16, HALF:] + RIDGE
        g0z_ref[y] = part[16 * y : 16 * y + 16, :HALF] / diag
        dz_ref[y] = diag
    cs_ref[...] = cs_in[...]
    cf_ref[...] = cf_in[...]

    def apply(step, carry):
        expo = Ids(chunk(obs_ref, step, E), HALF, (0, 8, 0, 8))
        hot = expo.hot()
        found = [
            gather(
                g0z_ref[2 * (step % 2) + yy],
                expo.full[16 * yy : 16 * yy + 16],
                hot[:, 2048 * yy : 2048 * (yy + 1)],
            )
            for yy in range(2)
        ]
        fit = joined(rows_of(chunk(obs_ref, step, W))) * joined(found)
        values = [[across(part, 0) for part in split(fit, FEW)]]
        flat = Ids(chunk(obs_ref, step, PX), LO)
        (added,) = scatter(values, flat.bf, flat.hot())
        cf_ref[...] += added
        star = Ids(chunk(obs_ref, step, S), LO)
        (added,) = scatter(values, star.bf, star.hot())
        cs_ref[step // 2] += added
        return carry

    unrolled(4, apply)
    x, c, y = lax.axis_index("x"), lax.axis_index("c"), lax.axis_index("y")
    chip = expo_ref[2 * x + 1 - c, 64:68]
    above = jnp.where(c == 1, chip[2:4], hop_ref[...])
    below = jnp.where(c == 1, hop_ref[...], chip[0:2])
    g0f, df = g0f_ref[...], df_ref[...]
    cf = cf_ref[...] - SMOOTH * beside(g0f, above, below)
    yf = cf / df
    yf_ref[...] = yf
    rho, beta, eta = fold8(g0f * g0f * df), fold8(g0f * cf), fold8(cf * yf)
    for kk in range(2):
        g0s, ds, cs = g0s_ref[kk], ds_ref[kk], cs_ref[kk]
        ys = cs / ds
        ys_ref[kk] = ys
        rho += fold8(g0s * g0s * ds)
        beta += fold8(g0s * cs)
        eta += fold8(cs * ys)
    total = jnp.zeros((HI, HALF), F32)
    cross = jnp.zeros((1, LO), F32)
    for kk in range(2):
        star, flat = Ids(own(obs_ref, y, kk, S), LO), Ids(own(obs_ref, y, kk, PX), LO)
        expo = Ids(own(obs_ref, y, kk, E), HALF, (0, 8))
        w = joined(rows_of(own(obs_ref, y, kk, W)))
        both = gather_both((ys_ref[kk], star.full, star.hot()), (yf, flat.full, flat.hot()))
        from_star, from_flat = row(both, STAR), row(both, FLAT)
        parts = split(w * (from_star + from_flat), FEW)
        (added,) = scatter([[across(part, 0) for part in parts]], expo.bf, expo.hot())
        total += added
        cross += fold_lanes(w * from_star * from_flat)
    expos = joined([ru_ref[...], total])
    none = jnp.zeros((2, LO), F32)
    delta = 2.0 * cross - (0.25 * SMOOTH) * fold8(yf * beside(yf, none, none))
    scal = jnp.concatenate(
        [0.25 * rho, 0.25 * beta, 0.25 * eta, delta, edge_rows(yf)], axis=0
    )
    for zl in range(NZ):
        for half in range(NC):
            out_ref[NC * zl + half, 0:8] = expos[8 * half : 8 * half + 8]
            out_ref[NC * zl + half, 8:16] = scal


def edge_dot(last, first):
    both = last * first
    return -(0.5 * SMOOTH) * (both[0:1] + both[1:2])


def column_kernel(parts_ref, out_ref):
    total = parts_ref[0]
    for peer in range(1, NZ * NC):
        total = total + parts_ref[peer]
    between = edge_dot(parts_ref[0, 14:16], parts_ref[1, 12:14])
    for peer in range(1, NZ * NC - 1):
        between += edge_dot(parts_ref[peer, 14:16], parts_ref[peer + 1, 12:14])
    scal = total[8:12] + jnp.where(row_iota((4, LO)) == 3, between, 0.0)
    ends = jnp.concatenate([scal, parts_ref[0, 12:14], parts_ref[NZ * NC - 1, 14:16]], axis=0)
    for peer in range(NX * NC * NY):
        out_ref[peer, 0:8] = total[0:8]
        out_ref[peer, 8:16] = ends


def whole(a):
    return jnp.sum(jnp.sum(a, axis=0, keepdims=True), axis=1, keepdims=True)


def finish_kernel(
    sums_ref, g0z_ref, dz_ref, g0s_ref, ys_ref, g0f_ref, yf_ref, star_out, zero_out, flat_out
):
    y, zh = lax.axis_index("y"), lax.axis_index("zh")
    scal = jnp.zeros((4, LO), F32)
    for x in range(NX):
        for i in range(NY):
            scal = scal + sums_ref[8 * x + i, 8:12]
    z_rho = jnp.zeros((HI, HALF), F32)
    z_beta, z_eta, z_delta = z_rho, z_rho, z_rho
    z_own = z_rho
    for i in range(4):
        halves = []
        for c in range(NC):
            half = sums_ref[4 * c + i, 0:8]
            for x in range(1, NX):
                half = half + sums_ref[8 * x + 4 * c + i, 0:8]
            halves.append(half)
        part = jnp.concatenate(halves, axis=0)
        cz, qz = part[:, :HALF], part[:, HALF:]
        g0z, dz = g0z_ref[i], dz_ref[i]
        yz = cz / dz
        z_rho += g0z * g0z * dz
        z_beta += g0z * cz
        z_eta += cz * yz
        z_delta += qz * yz
        z_own = jnp.where(i == y, yz, z_own)
    rho0 = whole(z_rho) + whole(scal[0:1])
    beta = whole(z_beta) + whole(scal[1:2])
    eta = whole(z_eta) + whole(scal[2:3])
    between = jnp.zeros((1, LO), F32)
    for x in range(NX - 1):
        between += 4.0 * edge_dot(sums_ref[8 * x, 14:16], sums_ref[8 * x + 8, 12:14])
    delta = 2.0 * whole(z_delta) + whole(scal[3:4] + between)
    curv0 = rho0 + beta
    step0 = rho0 / curv0
    left = beta / curv0
    rho1 = left * left * rho0 - 2.0 * step0 * left * beta + step0 * step0 * eta
    curv_g = (
        left * left * curv0
        - 2.0 * step0 * left * (beta + eta)
        + step0 * step0 * (eta + delta)
    )
    ratio = rho1 / rho0
    mixed = left * curv0 - step0 * (beta + eta)
    curv1 = curv_g + 2.0 * ratio * mixed + ratio * ratio * curv0
    step1 = rho1 / curv1
    along_g = step0 + step1 * (left + ratio)
    along_y = -step1 * step0
    star = along_g * g0s_ref[y // 2] + along_y * ys_ref[y // 2]
    shard = (y % 2) * 2 + zh
    mine = jnp.zeros((4, LO), F32)
    for i in range(4):
        mine = jnp.where(shard == i, star[4 * i : 4 * i + 4], mine)
    star_out[...] = mine
    zero = along_g * g0z_ref[y] + along_y * z_own
    zero_out[...] = jnp.concatenate([zero[0:4], pltpu.roll(zero[0:8], 4, 0)[0:4]], axis=1)
    flat = along_g * g0f_ref[...] + along_y * yf_ref[...]
    flat_out[...] = joined([flat[:8], flat[8:]])


VMEM = pl.BlockSpec(memory_space=pltpu.VMEM)
SMEM = pl.BlockSpec(memory_space=pltpu.SMEM)


HBM = pl.BlockSpec(memory_space=pltpu.HBM)


def call(kernel, shapes, args, specs=None, scratch=(), mib=8, work=20):
    out = [jax.ShapeDtypeStruct(shape, F32) for shape in shapes]
    many = len(out) > 1
    return pl.pallas_call(
        kernel,
        out_shape=tuple(out) if many else out[0],
        in_specs=specs or [VMEM] * len(args),
        out_specs=tuple([VMEM] * len(out)) if many else VMEM,
        scratch_shapes=list(scratch),
        compiler_params=pltpu.CompilerParams(vmem_limit_bytes=mib << 20 if mib else None),
        cost_estimate=pl.CostEstimate(flops=1 << work, bytes_accessed=1 << 20, transcendentals=0),
    )(*args)


def exchange(blocks, axes):
    return lax.all_to_all(blocks, axes, 0, 0, tiled=True)


def to_all(block, peers, axes):
    return exchange(jnp.broadcast_to(block[None], (peers, *block.shape)), axes)


def hop_pairs():
    def place(tile, y, zh):
        x, rest = divmod(tile, NZ * NC)
        zl, c = divmod(rest, NC)
        return (((x * NZ + zl) * NC + c) * NY + y) * NH + zh

    hop = []
    for tile in range(1, NX * NZ * NC - 1, 2):
        far = (tile + 1) % (NZ * NC) == 0
        for y in range(NY):
            for zh in range(NH):
                here, there = place(tile, y, zh), place(tile + 1, y, 1 - zh if far else zh)
                hop.extend([(here, there), (there, here)])
    return hop


def on_device(star_slot, star_block, exposure, superpixel, magnitude, weight):
    zh = lax.axis_index("zh")
    hop = hop_pairs()
    stars, flats, expos = (2, HI, LO), (HI, LO), (4, HI, HALF)
    obs, expo = call(
        pack_kernel, [(80, LO), (16, 8, LO)],
        (star_block, star_slot[0], exposure[0], superpixel[0], magnitude[0], weight[0]),
        specs=[SMEM] + [HBM] * 5,
        scratch=[pltpu.VMEM((16, LO), t) for t in (I32, I32, I32, F32, F32)]
        + [pltpu.SemaphoreType.DMA((5,))],
        mib=None,
    )
    partner = lax.ppermute(obs, "zh", [(0, 1), (1, 0)])
    expo = exchange(expo, ("zl", "zh"))
    expo = expo.reshape(NZ, NH, 8, LO).sum(axis=0)
    expo = jnp.where(zh == 0, expo, expo[::-1]).reshape(HI, LO)
    both = lax.optimization_barrier(jnp.concatenate([obs, partner], axis=0))
    totals = call(
        own_sums_kernel, [(96, LO)], (both,),
        scratch=[pltpu.VMEM(stars, F32)] * 2 + [pltpu.VMEM(flats, F32)] * 2, work=26,
    )
    sent = both.reshape(4, 40, LO)[:, :32].reshape(128, LO)
    sent, totals = lax.optimization_barrier((sent, totals))
    tile_obs = jnp.concatenate([sent, expo, totals], axis=0)
    tile_obs = to_all(lax.optimization_barrier(tile_obs), NY, "y")
    g0s, ds, g0f, df, hop_row, plane = call(
        sums_kernel, [stars] * 2 + [flats] * 2 + [(2, LO), (8, 72, LO)], (tile_obs,), mib=16, work=29
    )
    expo = exchange(plane, COLS)
    by_hop = lax.ppermute(hop_row, ALL, hop)
    cs, cf, ru = call(
        couple_kernel, [stars, flats, (HI, HALF)], (tile_obs, g0s, g0f),
        scratch=[pltpu.VMEM((4, 8, 4096), F32)], mib=16, work=30,
    )
    ys, yf, g0z, dz, payload = call(
        apply_kernel, [stars, flats] + [expos] * 2 + [(16, 16, LO)],
        (tile_obs, expo, g0s, ds, cs, g0f, cf, df, ru, by_hop),
        scratch=[pltpu.VMEM(stars, F32), pltpu.VMEM(flats, F32)], mib=16, work=30,
    )
    payload = exchange(payload, ("zl", "c"))
    sums = exchange(call(column_kernel, [(32, 16, LO)], (payload,)), PLANE)
    star, zero, flat = call(
        finish_kernel, [(4, LO), (4, LO), (8, 2 * LO)], (sums, g0z, dz, g0s, ys, g0f, yf)
    )
    return star.reshape(-1), zero.reshape(-1), flat


def solution(mesh):
    split = Mesh(mesh.devices.reshape(NX, NZ, NC, NY, NH), ALL)
    tile, loop = ("x", "zl", "c"), ("y", "zh")
    placed = (
        P(tile, loop, None),
        P(tile, loop),
        P(tile, loop, None),
        P(tile, loop, None),
        P(tile, loop, None),
        P(tile, loop, None),
    )
    return jax.shard_map(
        on_device,
        mesh=split,
        in_specs=placed,
        out_specs=(P(ALL), P(loop), P(tile, None)),
        check_vma=False,
    )
```
